32 devices in a mesh: seq: 8 (over y, x, core), head: 4 (over z).
Axes of the slice: x: 2, y: 2, z: 4, core: 2. Of those that a mesh axis runs over, the one named last changes fastest.
Arguments:
- hidden: bfloat16 [8192, 1536], P('seq'), may hold values from -6 to 6
- in_gain: bfloat16 [1536], replicated, may hold values from 0.5 to 1.5
- proj_gate: bfloat16 [1536, 3072], P(None, 'head'), may hold values from -0.15625 to 0.15625
- proj_input: bfloat16 [1536, 3072], P(None, 'head'), may hold values from -0.15625 to 0.15625
- proj_states: bfloat16 [1536, 256], P('head'), may hold values from -0.15625 to 0.15625
- proj_step: bfloat16 [1536, 48], P(None, 'head'), may hold values from -0.15625 to 0.15625
- conv_input: bfloat16 [4, 3072], P(None, 'head'), may hold values from -3 to 3
- conv_input_bias: bfloat16 [3072], P('head'), may hold values from -3 to 3
- conv_states: bfloat16 [4, 256], replicated, may hold values from -3 to 3
- conv_states_bias: bfloat16 [256], replicated, may hold values from -3 to 3
- step_bias: float32 [48], P('head'), may hold values from -4.5 to -3.5
- decay_log: float32 [48], P('head'), may hold values from -6.3 to 1.4, as said below
- skip_gain: float32 [48], P('head'), may hold values from 0.5 to 1.5
- gate_gain: bfloat16 [3072], P('head'), may hold values from 0.5 to 1.5
- proj_output: bfloat16 [3072, 1536], P('head'), may hold values from -0.109375 to 0.109375
- cotangent: bfloat16 [8192, 1536], P('seq'), may hold values from -6 to 6
Outputs:
- result: float32 [8192, 1536], P('seq')
- grad_hidden: float32 [8192, 1536], P('seq')
- grad_in_gain: float32 [1536], replicated
- grad_proj_gate: float32 [1536, 3072], P('seq', 'head')
- grad_proj_input: float32 [1536, 3072], P('seq', 'head')
- grad_proj_states: float32 [1536, 256], P('head', 'seq')
- grad_proj_step: float32 [1536, 48], P('seq', 'head')
- grad_conv_input: float32 [4, 3072], P(None, 'head')
- grad_conv_input_bias: float32 [3072], P('head')
- grad_conv_states: float32 [4, 256], replicated
- grad_conv_states_bias: float32 [256], replicated
- grad_step_bias: float32 [48], P('head')
- grad_decay_log: float32 [48], P('head')
- grad_skip_gain: float32 [48], P('head')
- grad_gate_gain: float32 [3072], P('head')
- grad_proj_output: float32 [3072, 1536], P('head', 'seq')
The draws below stay inside these ranges and needn't reach their ends.
Inputs may be any that keep to these rules, and one draw needn't show every extreme that they name: `decay_log`: one value a head.
All inputs are finite; a program needn't handle non-finite values.
Results may differ from the reference program's by a relative error of at most 0.00185.
The reference program's roundings to bfloat16 on the way count: a program that leaves them out, or rounds other values in their place, can miss the bound.
Values may be sent and summed in bfloat16 or wider, within the bound.
A program may use at most 128 MiB of HBM per device.

```python
import math
import jax
import jax.numpy as jnp
from jax import lax

D = 1536
DI = 3072
P_SIZE = 64
N = 128
K = 4
BLOCK = 256
SEQS = 1
H = 48
LENGTH = 8192
TOKENS = 8192


def draw_decay_log(key, part):
    return jax.random.uniform(key, (H,), jnp.float32, math.log(0.004), math.log(4.0))


def shard_levels(key, dims, cuts, smallest, top_value):
    factor_of = 1.0
    for dim, blocks in cuts:
        heights = jax.random.uniform(jax.random.fold_in(jax.random.fold_in(key, 6), dim), (blocks,), jnp.float32, smallest / len(cuts), top_value / len(cuts))
        factor_of = factor_of * jnp.repeat(jnp.exp(heights), dims[dim] // blocks).reshape((-1,) + (1,) * (len(dims) - 1 - dim))
    return factor_of


def centred(rng, shape, spread, bound, split=(), held_as=jnp.bfloat16):
    loudness = shard_levels(rng, shape, split, -0.22, 0.18) if split else 1.0
    result = jax.random.normal(rng, shape, jnp.float32) * spread * loudness
    return jnp.minimum(jnp.maximum(result, -bound), bound).astype(held_as)


def setup_inputs(seed: int = 0) -> dict:
    key_list = jax.random.split(jax.random.key(seed), 17)
    hidden = centred(key_list[0], (TOKENS, D), 1.0, 6.0, ((0, 8),))
    in_gain = jnp.clip(1.0 + 0.1 * jax.random.normal(key_list[1], (D,), jnp.float32), 0.5, 1.5).astype(jnp.bfloat16)
    proj_gate = centred(key_list[2], (D, DI), D ** -0.5, 0.15625, ((1, 4),))
    proj_input = centred(key_list[3], (D, DI), D ** -0.5, 0.15625, ((1, 4),))
    proj_states = centred(key_list[4], (D, 2 * N), D ** -0.5, 0.15625, ((0, 4),))
    proj_step = centred(key_list[5], (D, H), D ** -0.5, 0.15625, ((1, 4),))
    conv_input = centred(key_list[6], (K, DI), K ** -0.5, 3.0, ((1, 4),))
    conv_input_bias = centred(key_list[7], (DI,), 0.5, 3.0, ((0, 4),))
    conv_states = centred(key_list[8], (K, 2 * N), K ** -0.5, 3.0)
    conv_states_bias = centred(key_list[9], (2 * N,), 0.5, 3.0)
    step_bias = jnp.clip(-4.5 + 1.0 * jax.random.uniform(key_list[10], (H,), jnp.float32) ** shard_levels(key_list[10], (H,), ((0, 4),), -0.2, 0.2), -4.5, -3.5)
    decay_log = draw_decay_log(jax.random.fold_in(key_list[16], 71), 0)
    skip_gain = jnp.clip(0.5 + 1.0 * jax.random.uniform(key_list[12], (H,), jnp.float32) ** shard_levels(key_list[12], (H,), ((0, 4),), -0.2, 0.2), 0.5, 1.5)
    gate_gain = jnp.clip(1.0 + 0.1 * jax.random.normal(key_list[13], (DI,), jnp.float32), 0.5, 1.5).astype(jnp.bfloat16)
    proj_output = centred(key_list[14], (DI, D), DI ** -0.5, 0.109375, ((0, 4),))
    cotangent = centred(key_list[15], (TOKENS, D), 1.0, 6.0, ((0, 8),))
    return {"hidden": hidden, "in_gain": in_gain, "proj_gate": proj_gate, "proj_input": proj_input, "proj_states": proj_states, "proj_step": proj_step, "conv_input": conv_input, "conv_input_bias": conv_input_bias, "conv_states": conv_states, "conv_states_bias": conv_states_bias, "step_bias": step_bias, "decay_log": decay_log, "skip_gain": skip_gain, "gate_gain": gate_gain, "proj_output": proj_output, "cotangent": cotangent}


EPS = 1e-05
HIGH = lax.Precision.HIGHEST

@jax.custom_vjp
def low(v):
    return lax.optimization_barrier(v.astype(jnp.bfloat16)).astype(jnp.float32)

@jax.custom_vjp
def low_back(v):
    return v

def low_keep(v):
    return (low(v), None)

def low_pass(kept, grad):
    return (grad,)

def back_keep(v):
    return (v, None)

def back_low(kept, grad):
    return (low(grad),)
low.defvjp(low_keep, low_pass)
low_back.defvjp(back_keep, back_low)

def matmul_high(left, right):
    return jnp.dot(left, right, precision=HIGH, preferred_element_type=jnp.float32)

def causal_conv(inputs, kernel, bias):
    width = kernel.shape[0]
    length = inputs.shape[0]
    padded = jnp.concatenate([jnp.zeros((width - 1, inputs.shape[1]), jnp.float32), inputs], axis=0)
    summed = bias[None, :] + jnp.zeros((length, inputs.shape[1]), jnp.float32)
    for offset in range(width):
        summed = summed + kernel[offset][None, :] * padded[offset:offset + length]
    return jax.nn.silu(summed)

def ssd_block(carry_state, block_x, block_step, block_b, block_c, decay_rate):
    length = block_x.shape[0]
    log_sums = jnp.cumsum(block_step * decay_rate[None, :], axis=0)
    row_ids = lax.broadcasted_iota(jnp.int32, (length, length), 0)
    col_ids = lax.broadcasted_iota(jnp.int32, (length, length), 1)
    causal = (row_ids >= col_ids)[None, :, :]
    log_gaps = log_sums.T[:, :, None] - log_sums.T[:, None, :]
    weights = jnp.where(causal, jnp.exp(jnp.where(causal, log_gaps, 0.0)), 0.0)
    scores = jnp.einsum('tn,sn->ts', block_c, block_b, precision=HIGH)
    mixing = scores[None, :, :] * weights * block_step.T[:, None, :]
    intra_out = jnp.einsum('hts,shp->thp', mixing, block_x, precision=HIGH)
    carried = jnp.exp(log_sums)[:, :, None] * jnp.einsum('tn,hpn->thp', block_c, carry_state, precision=HIGH)
    to_end = jnp.exp(log_sums[-1][None, :] - log_sums) * block_step
    new_state = jnp.exp(log_sums[-1])[:, None, None] * carry_state + jnp.einsum('sh,shp,sn->hpn', to_end, block_x, block_b, precision=HIGH)
    return (new_state, intra_out + carried, log_sums)

def ssd_sequence(input_heads, step_size, bmat, cmat, decay_rate):
    block_count = input_heads.shape[0] // BLOCK

    def advance(carry_state, pieces):
        new_state, block_out, log_sums = ssd_block(carry_state, pieces[0], pieces[1], pieces[2], pieces[3], decay_rate)
        return (new_state, block_out)
    start_state = jnp.zeros((H, P_SIZE, N), jnp.float32)
    pieces = (input_heads.reshape(block_count, BLOCK, H, P_SIZE), step_size.reshape(block_count, BLOCK, H), bmat.reshape(block_count, BLOCK, N), cmat.reshape(block_count, BLOCK, N))
    final_state, block_out = lax.scan(jax.checkpoint(advance), start_state, pieces)
    return block_out.reshape(-1, H, P_SIZE)

def layer(params, hidden):
    in_gain, proj_gate, proj_input, proj_states, proj_step, conv_input, conv_input_bias, conv_states, conv_states_bias, step_bias, decay_log, skip_gain, gate_gain, proj_output = params
    inv_rms = lax.rsqrt(lax.optimization_barrier(jnp.mean(hidden * hidden, axis=-1, keepdims=True)) + EPS)
    normed = low(hidden * inv_rms * in_gain[None, :])
    gate_pre = low_back(matmul_high(normed, proj_gate))
    input_pre = low_back(matmul_high(normed, proj_input))
    states_pre = low_back(matmul_high(normed, proj_states))
    step_pre = low_back(matmul_high(normed, proj_step))
    input_conv = causal_conv(input_pre, conv_input, conv_input_bias)
    states_conv = causal_conv(states_pre, conv_states, conv_states_bias)
    step_size = jax.nn.softplus(step_pre + step_bias[None, :])
    decay_rate = -jnp.exp(decay_log)
    input_heads = input_conv.reshape(-1, H, P_SIZE)
    ssd_out = ssd_sequence(input_heads, step_size, states_conv[:, :N], states_conv[:, N:], decay_rate)
    ssd_out = (ssd_out + skip_gain[None, :, None] * input_heads).reshape(-1, DI)
    gated = ssd_out * jax.nn.silu(gate_pre)
    gate_inv = lax.rsqrt(lax.optimization_barrier(jnp.mean(gated * gated, axis=-1, keepdims=True)) + EPS)
    ynorm = low(gated * gate_inv * gate_gain[None, :])
    return hidden + matmul_high(ynorm, proj_output)

def reference(hidden, in_gain, proj_gate, proj_input, proj_states, proj_step, conv_input, conv_input_bias, conv_states, conv_states_bias, step_bias, decay_log, skip_gain, gate_gain, proj_output, cotangent):
    params = tuple((item.astype(jnp.float32) for item in (in_gain, proj_gate, proj_input, proj_states, proj_step, conv_input, conv_input_bias, conv_states, conv_states_bias, step_bias, decay_log, skip_gain, gate_gain, proj_output)))
    seq_hidden = hidden.astype(jnp.float32).reshape(SEQS, LENGTH, D)
    seq_cotan = cotangent.astype(jnp.float32).reshape(SEQS, LENGTH, D)

    def one_sequence(gradients, pair_in):
        output, pullback = jax.vjp(layer, params, pair_in[0])
        grad_params, grad_input = pullback(pair_in[1])
        return (jax.tree.map(jnp.add, gradients, grad_params), (output, grad_input))
    zero_grads = jax.tree.map(jnp.zeros_like, params)
    gradients, (outputs, grad_inputs) = lax.scan(one_sequence, zero_grads, (seq_hidden, seq_cotan))
    return (outputs.reshape(TOKENS, D), grad_inputs.reshape(TOKENS, D), gradients[0], gradients[1], gradients[2], gradients[3], gradients[4], gradients[5], gradients[6], gradients[7], gradients[8], gradients[9], gradients[10], gradients[11], gradients[12], gradients[13])
```

```python
import functools

import jax
import jax.numpy as jnp
import numpy as np
from jax import lax
from jax.experimental import pallas as pl
from jax.experimental.pallas import tpu as pltpu
from jax.sharding import PartitionSpec as P


DI = 3072
EPS = 1e-05
Q = 128
LANES = 128
HALO = 8
TAPS = 4

F32 = jnp.float32
BF16 = jnp.bfloat16
NN = (((1,), (0,)), ((), ()))
NT = (((1,), (1,)), ((), ()))
TN = (((0,), (0,)), ((), ()))
VMEM_LIMIT = 60 * 1024 * 1024
MESH_ID = pl.DeviceIdType.MESH


def dg(left, right, dims):
    return lax.dot_general(left, right, dims, preferred_element_type=F32)


def split(value):
    high = value.astype(BF16)
    return high, (value - high.astype(F32)).astype(BF16)


def dot3(left, right, dims):
    (lh, ll), (rh, rl) = split(left), split(right)
    return dg(lh, rh, dims) + (dg(lh, rl, dims) + dg(ll, rh, dims))


def spread(heads, onehot):
    high, low = split(heads)
    return dg(high, onehot, NN) + dg(low, onehot, NN)


def gather(wide, onehot):
    high, low = split(wide)
    return dg(high, onehot, NT) + dg(low, onehot, NT)


def sigmoid(value):
    return 1.0 / (1.0 + jnp.exp(-value))


def silu(value):
    return value * sigmoid(value)


def shifted(block, axis, distance):
    devices = range(lax.axis_size(axis))
    route = [(i - distance, i) for i in devices if i - distance in devices]
    return lax.ppermute(block, axis, route)


def call(kernel, grid, ins, outs, scratch=(), flops=0, collective=None):
    in_specs = [spec for _, spec in ins]
    size = sum(a.size * a.dtype.itemsize for a, _ in ins) + sum(
        s.size * s.dtype.itemsize for s, _ in outs
    )
    return pl.pallas_call(
        kernel,
        grid=grid,
        in_specs=in_specs,
        out_specs=[spec for _, spec in outs],
        out_shape=[shape for shape, _ in outs],
        scratch_shapes=list(scratch),
        cost_estimate=pl.CostEstimate(flops=flops, bytes_accessed=size, transcendentals=0),
        compiler_params=pltpu.CompilerParams(vmem_limit_bytes=VMEM_LIMIT)
        if collective is None
        else pltpu.CompilerParams(
            vmem_limit_bytes=VMEM_LIMIT, collective_id=collective, has_side_effects=True
        ),
    )(*[a for a, _ in ins])


def sds(shape, dtype=F32):
    return jax.ShapeDtypeStruct(shape, dtype)


def rows(width, reverse=None):
    if reverse is None:
        return pl.BlockSpec((Q, width), lambda c: (c, 0))
    return pl.BlockSpec((Q, width), lambda c: (reverse - 1 - c, 0))


def whole(shape):
    return pl.BlockSpec(shape, lambda c: (0,) * len(shape))


def before(width):
    return pl.BlockSpec((HALO, width), lambda c: (jnp.maximum(c * (Q // HALO) - 1, 0), 0))


def triangle(lower):
    a = lax.broadcasted_iota(jnp.int32, (Q, Q), 0)
    b = lax.broadcasted_iota(jnp.int32, (Q, Q), 1)
    return a >= b if lower else a <= b


def tri_sum(lower, value):
    mask = triangle(lower).astype(BF16)
    high = value.astype(BF16)
    rest = value - high.astype(F32)
    mid = rest.astype(BF16)
    low = (rest - mid.astype(F32)).astype(BF16)
    return dg(mask, high, NN) + (dg(mask, mid, NN) + dg(mask, low, NN))


def conv_act(pre_ref, prev_ref, halo_ref, params, at, ext_ref):
    first = pl.program_id(0) == 0
    size = ext_ref.shape[1]
    ext_ref[:HALO, :] = jnp.where(first, halo_ref[...], prev_ref[...])
    ext_ref[HALO:, :] = pre_ref[...]
    taps = TAPS
    total = params[at + taps : at + taps + 1, :size] + params[at + taps - 1 : at + taps, :size] * pre_ref[...]
    for k in range(taps - 1):
        start = HALO - taps + 1 + k
        total = total + params[at + k : at + k + 1, :size] * ext_ref[start : start + Q, :]
    return total


def states_kernel(
    n, pre, pre_prev, pre_halo, normed, normed_halo, step_w, vec, taps_in, taps_st, onehot, *refs
):
    pieces, refs = refs[:n], refs[n:]
    act_o, sact_o, spre_o, shalo_o, spre_step_o, step_o, cum_o, cumt_o, sin_o, dev_o, total_o = refs[:11]
    before_o, params = refs[11:13]
    ext, sext, state, total, full = refs[13:]
    c = pl.program_id(0)
    me = lax.axis_index("head")
    state_size = bmat_width(sact_o)
    inner = pre.shape[1]
    two = 2 * state_size
    hot = onehot[...]

    def line(first, size):
        return jnp.concatenate([vec[r : r + 1, :] for r in range(first, first + size // LANES)], axis=1)

    @pl.when(c == 0)
    def _():
        state[...] = jnp.zeros_like(state)
        total[...] = jnp.zeros_like(total)
        height = pieces[0].shape[0]
        for k in range(n):
            full[pl.ds(pl.multiple_of(((me + n - k) % n) * height, height), height), :] = pieces[k][...]
        params[...] = jnp.zeros_like(params)
        per = inner // LANES
        params[0:TAPS, :] = taps_in[...].astype(F32)
        params[4:5, :] = line(3, inner)
        params[5:6, :] = line(3 + per, inner)
        params[6:7, :] = spread(jnp.broadcast_to(vec[2:3, :], (HALO, LANES)), hot)[:1]
        params[7:8, :LANES] = -jnp.exp(vec[0:1, :])
        params[7:8, LANES : 2 * LANES] = vec[1:2, :]
        params[8 : 8 + TAPS, :two] = taps_st[...].astype(F32)
        params[12:13, :two] = line(3 + 2 * per, two)
        first = dg(normed_halo[...], full[...], NN)
        shalo_o[...] = jnp.where(lax.axis_index("seq") == 0, 0.0, first)
        sext[Q:, :] = shalo_o[...]

    sext[:HALO, :] = sext[Q:, :]
    spre = dg(normed[...], full[...], NN)
    spre_o[...] = spre
    sext[HALO:, :] = spre
    step_pre = dg(normed[...], step_w[...], NN)
    spre_step_o[...] = step_pre
    act = conv_act(pre, pre_prev, pre_halo, params, 0, ext)
    sact = params[12:13, :two] + params[8 + TAPS - 1 : 8 + TAPS, :two] * spre
    for k in range(TAPS - 1):
        start = HALO - TAPS + 1 + k
        sact = sact + params[8 + k : 9 + k, :two] * sext[start : start + Q, :]
    act_o[...] = act
    sact_o[...] = sact
    bmat = silu(sact[:, :state_size])
    step = jax.nn.softplus(step_pre + params[7:8, LANES : 2 * LANES])
    cum = tri_sum(True, step * params[7:8, :LANES])
    step_o[...] = step
    cum_o[...] = cum
    cumt_o[...] = cum.T
    last = cum[Q - 1 :, :]
    weight = spread(step * jnp.exp(last - cum), hot)
    xw = silu(act) * weight
    sin_o[...] = state[...]
    before_o[...] = total[...]
    decay = spread(jnp.broadcast_to(jnp.exp(last), (HALO, LANES)), hot)[:1]
    state[...] = state[...] * decay + dot3(bmat, xw, TN)
    total[...] = total[...] + last
    dev_o[:state_size, :] = state[...]
    dev_o[state_size:, :] = spread(jnp.broadcast_to(jnp.exp(total[...]), (HALO, LANES)), hot)
    total_o[...] = total[...]


def bmat_width(ref):
    return ref.shape[1] // 2


def pair_stack(value):
    high, low = split(value)
    return jnp.concatenate(
        [
            jnp.concatenate([high, low], axis=1),
            jnp.concatenate([high, jnp.zeros_like(high)], axis=1),
        ],
        axis=0,
    )


def intra_kernel(
    ns, act, sact, step, cum, cumt, params, onehot, packed, out, incoming,
    xs_ref, entered, got_s, got_d, prefix, sems,
):
    c = pl.program_id(0)
    count = pl.num_programs(0)
    seq = lax.axis_index("seq")
    begin, turn, end = swap_states(ns, packed, entered, got_s, got_d, prefix, sems, False)
    barrier = pltpu.get_barrier_semaphore()

    @pl.when(c == 0)
    def _():
        for k in range(1, ns):
            pl.semaphore_signal(
                barrier, inc=1, device_id={"seq": (seq + k) % ns}, device_id_type=MESH_ID
            )
        pl.semaphore_wait(barrier, ns - 1)
        begin()

    state_size = bmat_width(sact)
    sconv = silu(sact[...])
    bmat, cmat = sconv[:, :state_size], sconv[:, state_size:]
    scores = dot3(cmat, bmat, NT)
    x = silu(act[...])
    xs_ref[...] = x * spread(step[...], onehot[...])
    out[...] = x * params[6:7, :]
    causal = triangle(True)
    lane = lax.broadcasted_iota(jnp.int32, (Q, LANES), 1)
    for p in range(act.shape[1] // LANES):
        cols = slice(p * LANES, (p + 1) * LANES)
        right = pair_stack(xs_ref[:, cols])
        got = []
        for j in range(2):
            h = p * 2 + j
            gap = cum[:, h : h + 1] - cumt[h : h + 1, :]
            mixing = scores * jnp.exp(jnp.where(causal, gap, -1e30))
            wide = dg(jnp.concatenate(split(mixing), axis=1), right, NN)
            got.append(wide[:, :LANES] + wide[:, LANES:])
        out[:, cols] = out[:, cols] + jnp.where(lane < LANES // 2, got[0], got[1])

    @pl.when(c == count // 2)
    def _():
        turn()

    @pl.when(c == count - 1)
    def _():
        end()
        incoming[...] = entered[...]


STREAMS = 4
GAP = 2
SPAN = 83.0


def encode(value):
    top = jnp.max(jnp.abs(value), axis=1, keepdims=True)
    scale = (top * 1.004 + 1e-30).astype(BF16)
    code = jnp.exp(value * (SPAN / scale.astype(F32))).astype(BF16)
    return code, jnp.broadcast_to(scale, (value.shape[0], LANES))


def decode(block, width):
    scale = block[:, width : width + 1].astype(F32) * (1.0 / SPAN)
    return jnp.log(block[:, :width].astype(F32)) * scale


def swap_states(ns, packed, out, got_s, got_d, prefix, sems, reverse):
    seq = lax.axis_index("seq")
    own = out.shape[0] // ns
    total = out.shape[0]

    def rows_of(j):
        return pl.ds(pl.multiple_of(j * own, own), own)

    def remote(src, dst, send, recv, to):
        return pltpu.make_async_remote_copy(
            src_ref=src,
            dst_ref=dst,
            send_sem=send,
            recv_sem=recv,
            device_id={"seq": to},
            device_id_type=MESH_ID,
        )

    def copies(k, arriving):
        other = (seq + k) % ns
        slot = other if arriving else seq
        part = packed.at[rows_of(other)]
        decay = packed.at[pl.ds(total, HALO)]
        return (
            remote(part, got_s.at[slot], sems.at[0, k], sems.at[1, slot], other),
            remote(decay, got_d.at[slot], sems.at[2, k], sems.at[3, slot], other),
        )

    def answer(k, arriving):
        other = (seq + k) % ns
        slot = other if arriving else seq
        return remote(
            prefix.at[other], out.at[rows_of(slot)], sems.at[4, k], sems.at[5, slot], other
        )

    def begin():
        for k in range(1, ns):
            for copy in copies(k, False):
                copy.start()

    def turn():
        got_s[seq] = packed[rows_of(seq), :]
        got_d[seq] = packed[total:, :]
        for k in range(1, ns):
            for copy in copies(k, True):
                copy.wait_recv()
        carry = jnp.zeros((own, out.shape[1]), F32)
        for i in reversed(range(ns)) if reverse else range(ns):
            prefix[i] = carry
            carry = carry * got_d[i, 0:1, :] + got_s[i]
        for k in range(1, ns):
            answer(k, False).start()
        out[rows_of(seq), :] = prefix[seq]

    def end():
        for k in range(1, ns):
            answer(k, True).wait_recv()
        for k in range(1, ns):
            answer(k, False).wait_send()
            for copy in copies(k, False):
                copy.wait_send()

    return begin, turn, end


def swap_scratch(ns, shape):
    own = shape[0] // ns
    return [
        pltpu.VMEM((ns, own, shape[1]), F32),
        pltpu.VMEM((ns, HALO, shape[1]), F32),
        pltpu.VMEM((ns, own, shape[1]), F32),
        pltpu.SemaphoreType.DMA((6, ns)),
    ]


def reduce_kernel(n, ns, dims, cols, with_sums, *refs):
    terms = len(dims)
    lefts, rights = refs[:terms], refs[terms : 2 * terms]
    refs = refs[2 * terms :]
    if with_sums:
        hidden_ref, inv_ref, small_a, small_b, states_ref, out_ref, sum_a, sum_b, sum_s = refs[:9]
        refs = refs[9:]
    else:
        packed, out_ref, later = refs[:3]
        refs = refs[3:]
    part, code_r, code_l, got_r, got_l, sr_sem, sl_sem, rr_sem, rl_sem, ar_sem, al_sem, ag_sem = refs[:12]
    me = lax.axis_index("head")
    tokens = part.shape[0]
    width = part.shape[1]
    span = tokens // STREAMS
    rows_own = span // n
    has_right, has_left = me < n - 1, me > 0

    barrier = pltpu.get_barrier_semaphore()
    for k in range(1, n):
        pl.semaphore_signal(
            barrier, inc=1, device_id={"head": (me + k) % n}, device_id_type=MESH_ID
        )
    seq = lax.axis_index("seq")
    for k in range(1, ns):
        pl.semaphore_signal(
            barrier, inc=1, device_id={"seq": (seq + k) % ns}, device_id_type=MESH_ID
        )
    expected = n + ns - 2
    if with_sums:
        got_a, got_b, got_s, got_c, mine_b = refs[12:17]
        sa_sem, ra_sem, sb_sem, rb_sem, ss_sem, rs_sem, sc_sem, rc_sem = refs[17:]
    else:
        begin, turn, end = swap_states(ns, packed, later, *refs[12:], True)

    def to_seq(src, dst, ssem, rsem, k):
        return pltpu.make_async_remote_copy(
            src_ref=src,
            dst_ref=dst.at[seq],
            send_sem=ssem.at[k],
            recv_sem=rsem.at[seq],
            device_id={"seq": (seq + k) % ns},
            device_id_type=MESH_ID,
        )

    def from_seq(src, dst, ssem, rsem, k):
        other = (seq + k) % ns
        return pltpu.make_async_remote_copy(
            src_ref=src,
            dst_ref=dst.at[other],
            send_sem=ssem.at[k],
            recv_sem=rsem.at[other],
            device_id={"seq": other},
            device_id_type=MESH_ID,
        )

    def states_at(j):
        own = sum_s.shape[0]
        return states_ref.at[pl.ds(pl.multiple_of(j * own, own), own)]

    def at(d, h):
        return pl.ds(pl.multiple_of(h * span + d * rows_own, rows_own), rows_own)

    def step(d, h, right):
        code, got, ssem, rsem = (
            (code_r, got_r, sr_sem, rr_sem) if right else (code_l, got_l, sl_sem, rl_sem)
        )
        return pltpu.make_async_remote_copy(
            src_ref=code.at[at(d, h)],
            dst_ref=got.at[at(d, h)],
            send_sem=ssem.at[h, d],
            recv_sem=rsem.at[h, d],
            device_id={"head": me + 1 if right else me - 1},
            device_id_type=MESH_ID,
        )

    def hand_on(b, h, right):
        return pltpu.make_async_remote_copy(
            src_ref=out_ref.at[at(b, h)],
            dst_ref=out_ref.at[at(b, h)],
            send_sem=(ar_sem if right else al_sem).at[h, b],
            recv_sem=ag_sem.at[h, b],
            device_id={"head": me + 1 if right else me - 1},
            device_id_type=MESH_ID,
        )

    def put(ref, where, value):
        code, scale = encode(value)
        ref[where, :width] = code
        ref[where, width:] = scale

    def compute(h):
        where = pl.ds(h * span, span)
        total = None
        for left, right, dim, col in zip(lefts, rights, dims, cols):
            value = left[where, :] if col is None else left[where, col[0] : col[1]]
            term = dg(value, right[...], dim)
            total = term if total is None else total + term
        part[where, :] = total
        if with_sums:
            seen = total * (hidden_ref[where, :].astype(F32) * inv_ref[where, :])
            row = jnp.sum(seen, axis=0, keepdims=True)
            mine_b[0:1, :] = row if h == 0 else mine_b[0:1, :] + row

    def chain(h, u):
        for right in (True, False):
            d = me + (n - 1 - u) if right else me - (n - 1 - u)
            code, got = (code_r, got_r) if right else (code_l, got_l)
            inside = d <= n - 1 if right else d >= 0
            fed = has_left if right else has_right

            @pl.when(inside & fed)
            def _():
                step(d, h, right).wait_recv()
                put(code, at(d, h), part[at(d, h), :] + decode(got[at(d, h), :], width))
                step(d, h, right).start()

            @pl.when(inside & jnp.logical_not(fed))
            def _():
                put(code, at(d, h), part[at(d, h), :])
                step(d, h, right).start()

    def finish(h):
        own = at(me, h)

        @pl.when(has_left)
        def _():
            step(me, h, True).wait_recv()
            part[own, :] = part[own, :] + decode(got_r[own, :], width)

        @pl.when(has_right)
        def _():
            step(me, h, False).wait_recv()
            part[own, :] = part[own, :] + decode(got_l[own, :], width)

        if not with_sums:
            put(out_ref, pl.ds(h * rows_own, rows_own), part[own, :])
            return

        put(out_ref, own, part[own, :])

        @pl.when(has_right)
        def _():
            hand_on(me, h, True).start()

        @pl.when(has_left)
        def _():
            hand_on(me, h, False).start()

    def relay(h, s):
        @pl.when(me - s >= 0)
        def _():
            hand_on(me - s, h, True).wait_recv()

            @pl.when(has_right)
            def _():
                hand_on(me - s, h, True).start()

        @pl.when(me + s < n)
        def _():
            hand_on(me + s, h, False).wait_recv()

            @pl.when(has_left)
            def _():
                hand_on(me + s, h, False).start()

    for t in range(GAP * (STREAMS - 1) + 2 * n - 1):
        for h in range(STREAMS):
            u = t - GAP * h
            if u == 0:
                compute(h)
                if h == 0:
                    pl.semaphore_wait(barrier, expected)
                    if with_sums:
                        for k in range(1, ns):
                            to_seq(small_a, got_a, sa_sem, ra_sem, k).start()
                            to_seq(states_at((seq + k) % ns), got_s, ss_sem, rs_sem, k).start()
                    else:
                        begin()
                if h == STREAMS - 1 and with_sums:
                    mine_b[8:16, :] = jnp.zeros((8, width), F32)
                    mine_b[8:16, : small_b.shape[1]] = small_b[...]
                    for k in range(1, ns):
                        to_seq(mine_b, got_b, sb_sem, rb_sem, k).start()
            if 0 <= u < n - 1:
                chain(h, u)
            if u == n - 1:
                finish(h)
            if with_sums and n - 1 < u < 2 * n - 1:
                relay(h, u - n + 1)
        if not with_sums and t == n - 1:
            turn()
    if not with_sums:
        end()
    if with_sums:
        total = small_a[...]
        for k in range(1, ns):
            from_seq(small_a, got_a, sa_sem, ra_sem, k).wait_recv()
            total = total + got_a[(seq + k) % ns]
        sum_a[...] = total
        total = states_at(seq)[...]
        for k in range(1, ns):
            from_seq(states_at(seq), got_s, ss_sem, rs_sem, k).wait_recv()
            total = total + got_s[(seq + k) % ns]
        sum_s[...] = total
        total = mine_b[...]
        for k in range(1, ns):
            from_seq(mine_b, got_b, sb_sem, rb_sem, k).wait_recv()
            total = total + got_b[(seq + k) % ns]
        sum_b[...] = total

        def to_head(k):
            return pltpu.make_async_remote_copy(
                src_ref=sum_b,
                dst_ref=got_c.at[me],
                send_sem=sc_sem.at[k],
                recv_sem=rc_sem.at[me],
                device_id={"head": (me + k) % n},
                device_id_type=MESH_ID,
            )

        def from_head(k):
            other = (me + k) % n
            return pltpu.make_async_remote_copy(
                src_ref=sum_b,
                dst_ref=got_c.at[other],
                send_sem=sc_sem.at[k],
                recv_sem=rc_sem.at[other],
                device_id={"head": other},
                device_id_type=MESH_ID,
            )

        for k in range(1, n):
            to_head(k).start()
        total = sum_b[...]
        for k in range(1, n):
            from_head(k).wait_recv()
        for k in range(1, n):
            to_head(k).wait_send()
            total = total + got_c[(me + k) % n]
        sum_b[...] = total
        for k in range(1, ns):
            to_seq(small_a, got_a, sa_sem, ra_sem, k).wait_send()
            to_seq(states_at((seq + k) % ns), got_s, ss_sem, rs_sem, k).wait_send()
            to_seq(mine_b, got_b, sb_sem, rb_sem, k).wait_send()
    for h in range(STREAMS):
        for i in range(n):

            @pl.when(i > me)
            def _():
                step(i, h, True).wait_send()

            @pl.when(i < me)
            def _():
                step(i, h, False).wait_send()

            if with_sums:

                @pl.when(has_right & (i <= me))
                def _():
                    hand_on(i, h, True).wait_send()

                @pl.when(has_left & (i >= me))
                def _():
                    hand_on(i, h, False).wait_send()


def reduce_over_heads(products, dims, collective, sums=None, packed=None, cols=None):
    n, ns = lax.axis_size("head"), lax.axis_size("seq")
    tokens, width = products[0][0].shape[0], products[0][1].shape[dims[0][0][1][0] ^ 1]
    lefts, rights = [a for a, _ in products], [b for _, b in products]
    dma = pltpu.SemaphoreType.DMA
    coded = pltpu.VMEM((tokens, width + LANES), BF16)
    scratch = [pltpu.VMEM((tokens, width), F32), coded, coded, coded, coded]
    scratch += [dma((STREAMS, n))] * 7
    if sums is not None:
        extra = list(sums)
        small_a = sums[2].shape
        states = (sums[4].shape[0] // ns, sums[4].shape[1])
        out_shape = [sds((tokens, width + LANES), BF16), sds(small_a), sds((16, width)), sds(states)]
        scratch += [
            pltpu.VMEM((ns, *small_a), F32),
            pltpu.VMEM((ns, 16, width), F32),
            pltpu.VMEM((ns, *states), F32),
            pltpu.VMEM((n, 16, width), F32),
            pltpu.VMEM((16, width), F32),
        ]
        scratch += [dma((ns,))] * 6 + [dma((n,))] * 2
    else:
        extra = [packed]
        states = (packed.shape[0] - HALO, packed.shape[1])
        out_shape = [sds((tokens // n, width + LANES), BF16), sds(states)]
        scratch += swap_scratch(ns, states)
    vmem = pl.BlockSpec(memory_space=pltpu.VMEM)
    return pl.pallas_call(
        functools.partial(reduce_kernel, n, ns, dims, cols or [None] * len(dims), sums is not None),
        in_specs=[vmem] * (len(lefts) + len(rights) + len(extra)),
        out_specs=[vmem] * len(out_shape),
        out_shape=out_shape,
        scratch_shapes=scratch,
        compiler_params=pltpu.CompilerParams(
            collective_id=collective, has_side_effects=True, vmem_limit_bytes=VMEM_LIMIT
        ),
        cost_estimate=pl.CostEstimate(
            flops=2 * tokens * width * sum(a.shape[1] for a in lefts),
            bytes_accessed=100 * tokens * width,
            transcendentals=0,
        ),
        name="reduce_heads" if sums is not None else "scatter_heads",
    )(*lefts, *rights, *extra)


def result_kernel(n, *refs):
    pieces, hidden, out = refs[:n], refs[n], refs[n + 1]
    me = lax.axis_index("head")
    width = out.shape[1]
    size = out.shape[0] // n
    for k in range(n):
        where = pl.ds(pl.multiple_of(((me + n - k) % n) * size, size), size)
        out[where, :] = hidden[where, :].astype(F32) + decode(pieces[k][...], width)


def turn_kernel(value, out):
    high = value.shape[0]
    more = jnp.zeros((-high % LANES, value.shape[1]), F32)
    out[...] = jnp.concatenate([value[...], more], axis=0).T[:, :high]


def hidden_kernel(code, hidden, cotangent, inv, gain, out):
    width = out.shape[1]
    grad = decode(code[...], width) * gain[...]
    resid = hidden[...].astype(F32)
    scale = inv[...]
    dots = jnp.sum(grad * resid, axis=1, keepdims=True) * (1.0 / width)
    out[...] = (
        cotangent[...].astype(F32) + scale * grad - resid * (scale * scale * scale * dots)
    )


def rows_of_sums(square, cross):
    ones = jnp.ones((HALO, square.shape[1]), BF16)
    (sh, sl), (ch, cl) = split(square), split(cross)
    first = dg(ones, sh, NT) + dg(ones, sl, NT)
    second = dg(ones, ch, NT) + dg(ones, cl, NT)
    row = lax.broadcasted_iota(jnp.int32, first.shape, 0)
    return jnp.where(row == 0, first, second)


def middle_kernel(
    n, yloc, act, sact, cum, sin, before_log, total_log, incoming, gate, gyn, params, onehot,
    y_o, ynorm_o, gpre_o, gssd_o, dout_o, dev_o, rows_o,
    keep, mine, got, adj, ssem, rsem,
):
    i = pl.program_id(0)
    count = pl.num_programs(0) // 2
    c = jnp.where(i < count, i, 2 * count - 1 - i)
    me = lax.axis_index("head")
    state_size = bmat_width(sact)
    hot = onehot[...]
    gain = params[5:6, :]
    where = pl.ds(pl.multiple_of(c * Q, Q), Q)
    barrier = pltpu.get_barrier_semaphore()

    def copy(k, arriving):
        other = (me + k) % n
        return pltpu.make_async_remote_copy(
            src_ref=mine,
            dst_ref=got.at[other if arriving else me],
            send_sem=ssem.at[k],
            recv_sem=rsem.at[other if arriving else me],
            device_id={"head": other},
            device_id_type=MESH_ID,
        )

    @pl.when(i == 0)
    def _():
        for k in range(1, n):
            pl.semaphore_signal(
                barrier, inc=1, device_id={"head": (me + k) % n}, device_id_type=MESH_ID
            )

    cmat = silu(sact[:, state_size:])
    gv = gate[...]
    sg = sigmoid(gv)
    gsilu = gv * sg
    growth = spread(jnp.exp(cum[...]), hot)

    @pl.when(i < count)
    def _():
        carry = spread(jnp.broadcast_to(jnp.exp(before_log[...]), (HALO, LANES)), hot)[:1]
        state = sin[...] + carry * incoming[...]
        y = yloc[...] + growth * dot3(cmat, state, NN)
        y_o[...] = y
        keep[where, :] = y
        gated = y * gsilu
        mine[:, where] = rows_of_sums(gated * gated, gyn[...] * gain * gated)

    @pl.when(i == count - 1)
    def _():
        pl.semaphore_wait(barrier, n - 1)
        for k in range(1, n):
            copy(k, False).start()

    @pl.when(i == count)
    def _():
        adj[...] = jnp.zeros_like(adj)
        rows_o[...] = jnp.zeros_like(rows_o)
        total = mine[...]
        for k in range(1, n):
            copy(k, True).wait_recv()
        for k in range(1, n):
            copy(k, False).wait_send()
            total = total + got[(me + k) % n]
        mine[...] = total

    @pl.when(i >= count)
    def _():
        total = mine[:, where]
        columns = jnp.concatenate([total, jnp.zeros((Q - HALO, Q), F32)], axis=0).T
        inv = lax.rsqrt(columns[:, 0:1] / DI + EPS)
        cross = columns[:, 1:2] / DI
        yv = keep[where, :]
        gated = yv * gsilu
        normed = gated * inv
        ynorm_o[...] = (normed * gain).astype(BF16)
        rows_o[0:1, :] = rows_o[0:1, :] + jnp.sum(gyn[...] * normed, axis=0, keepdims=True)
        ggated = inv * (gyn[...] * gain) - normed * (inv * inv * cross)
        gpre_o[...] = (ggated * yv * sg * (1.0 + gv * (1.0 - sg))).astype(BF16)
        gssd = ggated * gsilu
        gssd_o[...] = gssd
        rows_o[1:2, :] = rows_o[1:2, :] + jnp.sum(gssd * silu(act[...]), axis=0, keepdims=True)
        dout_o[...] = adj[...]
        decay = spread(jnp.broadcast_to(jnp.exp(cum[Q - 1 :, :]), (HALO, LANES)), hot)[:1]
        adj[...] = adj[...] * decay + dot3(cmat, gssd * growth, TN)

    @pl.when(i == 2 * count - 1)
    def _():
        dev_o[:state_size, :] = adj[...]
        whole_log = jnp.broadcast_to(jnp.exp(total_log[...]), (HALO, LANES))
        dev_o[state_size:, :] = spread(whole_log, hot)


def back_kernel(
    n, ns, act, sact, y, gssd, step, step_pre, cum, cumt, sin, dout, before_log, total_log, incoming,
    later, params, onehot, rows_in, pre, pre_prev, pre_halo, spre, spre_prev, spre_halo,
    gin_o, gsb_out, small_a, small_b,
    gsb_o, gstep, xs_ref, u_ref, st_ref, gext, sext, pext, spext, halo_send, halo_got, shalo_send, shalo_got,
    psend, pgot, h_sem, p_send, p_recv, g_send, g_recv,
):
    c = pl.program_id(0)
    count = pl.num_programs(0) - 1
    total_chunks = psend.shape[0] // Q
    groups = total_chunks // n
    taps = TAPS
    me, seq = lax.axis_index("head"), lax.axis_index("seq")
    state_size = bmat_width(sact)
    two = 2 * state_size
    barrier = pltpu.get_barrier_semaphore()

    def halo(src, dst, k):
        return pltpu.make_async_remote_copy(
            src_ref=src,
            dst_ref=dst,
            send_sem=h_sem.at[k],
            recv_sem=h_sem.at[k + 1],
            device_id={"seq": (seq + ns - 1) % ns},
            device_id_type=MESH_ID,
        )

    def chunk_rows(k):
        return pl.ds(pl.multiple_of(k * Q, Q), Q)

    def to_owner(k):
        return pltpu.make_async_remote_copy(
            src_ref=psend.at[chunk_rows(k)],
            dst_ref=pgot.at[me, chunk_rows(k // n)],
            send_sem=p_send.at[k],
            recv_sem=p_recv.at[me, k // n],
            device_id={"head": k % n},
            device_id_type=MESH_ID,
        )

    def from_other(j, g):
        return pltpu.make_async_remote_copy(
            src_ref=psend.at[chunk_rows(g)],
            dst_ref=pgot.at[j, chunk_rows(g)],
            send_sem=p_send.at[g],
            recv_sem=p_recv.at[j, g],
            device_id={"head": j},
            device_id_type=MESH_ID,
        )

    def give(k, g, arriving):
        other = (me + k) % n
        owner = other if arriving else me
        where = chunk_rows(g * n + owner)
        return pltpu.make_async_remote_copy(
            src_ref=gsb_o.at[where],
            dst_ref=gsb_o.at[where],
            send_sem=g_send.at[k, g],
            recv_sem=g_recv.at[owner, g],
            device_id={"head": other},
            device_id_type=MESH_ID,
        )

    @pl.when(c == 0)
    def _():
        for k in range(1, n):
            pl.semaphore_signal(
                barrier, inc=1, device_id={"head": (me + k) % n}, device_id_type=MESH_ID
            )

        @pl.when(seq < ns - 1)
        def _():
            pl.semaphore_signal(
                barrier, inc=1, device_id={"seq": (seq + 1) % ns}, device_id_type=MESH_ID
            )

        small_a[...] = jnp.zeros_like(small_a)
        small_b[...] = jnp.zeros_like(small_b)
        small_a[5:7, :] = rows_in[0:2, :]

    @pl.when(c < count)
    def _():
        hot = onehot[...]
        skip = params[6:7, :]
        rate = params[7:8, :LANES]
        sactv = sact[...]
        ssg = sigmoid(sactv)
        sconv = sactv * ssg
        bmat, cmat = sconv[:, :state_size], sconv[:, state_size:]
        actv = act[...]
        sg = sigmoid(actv)
        x = actv * sg
        cumv, stepv = cum[...], step[...]
        last = cumv[Q - 1 :, :]
        step_wide = spread(stepv, hot)
        xs = x * step_wide
        xs_ref[...] = xs
        g = gssd[...]

        def row(value):
            return spread(jnp.broadcast_to(jnp.exp(value), (HALO, LANES)), hot)[:1]

        state = sin[...] + row(before_log[...]) * incoming[...]
        adj = dout[...] + row(total_log[...] - before_log[...] - last) * later[...]
        to_end = spread(jnp.exp(last - cumv), hot)
        u_state = to_end * dot3(bmat, adj, NN)
        ends = row(last) * jnp.sum(adj * state, axis=0, keepdims=True) + jnp.sum(
            xs * u_state, axis=0, keepdims=True
        )
        scores_t = dot3(bmat, cmat, NT)
        later_mask = triangle(False)
        lane = lax.broadcasted_iota(jnp.int32, (Q, LANES), 1)
        st_ref[...] = jnp.zeros_like(st_ref)
        for p in range(act.shape[1] // LANES):
            cols = slice(p * LANES, (p + 1) * LANES)
            right = pair_stack(gssd[:, cols])
            g_high, g_low = right[:Q, :LANES], right[:Q, LANES:]
            twice = jnp.concatenate([g_high, g_high], axis=1)
            pair = xs_ref[:, cols]
            got = []
            for j in range(2):
                h = p * 2 + j
                gap = cumt[h : h + 1, :] - cum[:, h : h + 1]
                decay = jnp.exp(jnp.where(later_mask, gap, -1e30))
                wide = dg(jnp.concatenate(split(scores_t * decay), axis=1), right, NN)
                got.append(wide[:, :LANES] + wide[:, LANES:])
                mine = (lane < LANES // 2) if j == 0 else (lane >= LANES // 2)
                xh, xl = split(jnp.where(mine, pair, 0.0))
                inner = dg(jnp.concatenate([xh, xl], axis=1), twice, NT) + dg(xh, g_low, NT)
                st_ref[...] = st_ref[...] + decay * inner
            u_ref[:, cols] = jnp.where(lane < LANES // 2, got[0], got[1])
        u = u_ref[...] + u_state
        sc = st_ref[...]
        g_scaled = g * spread(jnp.exp(cumv), hot)
        gstates = jnp.concatenate(
            [
                dot3(sc, cmat, NN) + dot3(xs * to_end, adj, NT),
                dot3(sc.T, bmat, NN) + dot3(g_scaled, state, NT),
            ],
            axis=1,
        )
        gsact = gstates * (ssg * (1.0 + sactv * (1.0 - ssg)))
        gact = (step_wide * u + skip * g) * (sg * (1.0 + actv * (1.0 - sg)))
        u_ref[...] = gact
        sext[Q + HALO :, :] = gsact
        small_a[4:5, :] = small_a[4:5, :] + jnp.sum(gact, axis=0, keepdims=True)
        small_b[4:5, :] = small_b[4:5, :] + jnp.sum(gsact, axis=0, keepdims=True)
        direct = gather(x * u, hot)
        flow = gather(g * (y[...] - skip * x), hot) - stepv * direct
        ends_heads = gather(jnp.broadcast_to(ends, (HALO, ends.shape[1])), hot)[:1]
        da = tri_sum(False, flow) + ends_heads
        slope = (direct + rate * da) * sigmoid(step_pre[...] + params[7:8, LANES : 2 * LANES])
        gstep[Q:, :] = slope.astype(BF16)
        small_a[7:8, :LANES] = small_a[7:8, :LANES] + jnp.sum(
            stepv * rate * da, axis=0, keepdims=True
        )
        small_a[7:8, LANES : 2 * LANES] = small_a[7:8, LANES : 2 * LANES] + jnp.sum(
            slope, axis=0, keepdims=True
        )

    @pl.when(c == 0)
    def _():
        halo_send[...] = u_ref[:HALO, :]
        shalo_send[...] = sext[Q + HALO : Q + 2 * HALO, :]
        pl.semaphore_wait(barrier, n - 1 + jnp.where(seq > 0, 1, 0))

        @pl.when(seq > 0)
        def _():
            halo(halo_send, halo_got, 0).start()
            halo(shalo_send, shalo_got, 2).start()

    @pl.when(c == count)
    def _():
        @pl.when(seq < ns - 1)
        def _():
            halo(halo_send, halo_got, 0).wait_recv()
            halo(shalo_send, shalo_got, 2).wait_recv()
            u_ref[:HALO, :] = halo_got[...]
            sext[Q + HALO : Q + 2 * HALO, :] = shalo_got[...]

        @pl.when(seq == ns - 1)
        def _():
            u_ref[:HALO, :] = jnp.zeros((HALO, u_ref.shape[1]), F32)
            sext[Q + HALO : Q + 2 * HALO, :] = jnp.zeros((HALO, two), F32)

        @pl.when(seq > 0)
        def _():
            halo(halo_send, halo_got, 0).wait_send()
            halo(shalo_send, shalo_got, 2).wait_send()

    @pl.when(c >= 1)
    def _():
        gext[Q:, :] = u_ref[:HALO, :]
        sext[Q : Q + HALO, :] = sext[Q + HALO : Q + 2 * HALO, :]
        pext[:HALO, :] = jnp.where(c == 1, pre_halo[...], pre_prev[...])
        pext[HALO:, :] = pre[...]
        spext[:HALO, :] = jnp.where(c == 1, spre_halo[...], spre_prev[...])
        spext[HALO:, :] = spre[...]

        def conv_back(ext, ext_pre, taps_at, size, sums):
            g = ext[:Q, :]
            total = params[taps_at + taps - 1 : taps_at + taps, :size] * g
            for k in range(taps - 1):
                start = taps - 1 - k
                total = total + params[taps_at + k : taps_at + k + 1, :size] * ext[start : start + Q, :]
            for k in range(taps):
                start = HALO - taps + 1 + k
                sums[k : k + 1, :] = sums[k : k + 1, :] + jnp.sum(
                    g * ext_pre[start : start + Q, :], axis=0, keepdims=True
                )
            return total

        inner = gext.shape[1]
        gin_o[:, :inner] = conv_back(gext, pext, 0, inner, small_a).astype(BF16)
        gin_o[:, inner:] = gstep[:Q, :]
        psend[chunk_rows(c - 1), :] = conv_back(sext, spext, 8, two, small_b)

        @pl.when((c - 1) % n != me)
        def _():
            to_owner(c - 1).start()

    @pl.when(c < count)
    def _():
        gext[:Q, :] = u_ref[...]
        gstep[:Q, :] = gstep[Q:, :]
        sext[:Q, :] = sext[Q + HALO :, :]

    for g in range(groups):

        @pl.when(c == min((g + 1) * n + 2, total_chunks))
        def _():
            own = chunk_rows(g * n + me)
            total = psend[own, :]
            for k in range(1, n):
                j = (me + k) % n
                from_other(j, g).wait_recv()
                total = total + pgot[j, g * Q : (g + 1) * Q, :]
            gsb_o[own, :] = total.astype(BF16)
            for k in range(1, n):
                give(k, g, False).start()

    @pl.when(c == count)
    def _():
        for g in range(groups):
            for k in range(1, n):
                give(k, g, True).wait_recv()
        gsb_out[...] = gsb_o[...]
        for g in range(groups):
            for k in range(1, n):
                give(k, g, False).wait_send()
        for k in range(total_chunks):

            @pl.when(k % n != me)
            def _():
                to_owner(k).wait_send()


def matmul_low(left, right):
    return jnp.dot(left, right, preferred_element_type=F32)


def times_transposed(left, right):
    return dg(left, right, NT)


def transposed_times(left, right):
    return dg(left, right, TN)


def on_device(
    hidden,
    in_gain,
    proj_gate,
    proj_input,
    proj_states,
    proj_step,
    conv_input,
    conv_input_bias,
    conv_states,
    conv_states_bias,
    step_bias,
    decay_log,
    skip_gain,
    gate_gain,
    proj_output,
    cotangent,
):
    seg_count = lax.axis_size("seq")
    seg_index = lax.axis_index("seq")
    head_index = lax.axis_index("head")
    is_first = seg_index == 0
    tokens, width = hidden.shape
    heads = proj_step.shape[1]
    inner = proj_gate.shape[1]
    state_size = conv_states.shape[1] // 2
    head_dim = inner // heads
    row_width = proj_states.shape[0]
    count = tokens // Q
    gain_full = in_gain.astype(F32)

    def pad_heads(value):
        return jnp.pad(value, [(0, 0)] * (value.ndim - 1) + [(0, LANES - heads)])

    n, ns = lax.axis_size("head"), seg_count

    def turned(value, k):
        return lax.ppermute(value, "head", [(i, (i + k) % n) for i in range(n)])

    pieces = [proj_states] + [turned(proj_states, k) for k in range(1, n)]
    hidden_halo = shifted(hidden[tokens - HALO :], "seq", 1)

    def norm(rows_):
        value = rows_.astype(F32)
        inv = lax.rsqrt(jnp.mean(value * value, axis=-1, keepdims=True) + EPS)
        return inv, (value * inv * gain_full[None, :]).astype(BF16)

    inv_rms, normed = norm(hidden)
    normed_halo = norm(hidden_halo)[1]
    keep = jnp.where(is_first, 0.0, 1.0)
    proj_step_wide = pad_heads(proj_step)
    input_pre = matmul_low(normed, proj_input)
    input_halo = matmul_low(normed_halo, proj_input) * keep
    gate_pre = matmul_low(normed, proj_gate)
    grad_ynorm = times_transposed(cotangent, proj_output)
    two = 2 * state_size
    flat = jnp.concatenate(
        [
            pad_heads(decay_log),
            pad_heads(step_bias),
            pad_heads(skip_gain),
            conv_input_bias.astype(F32),
            gate_gain.astype(F32),
            conv_states_bias.astype(F32),
        ]
    )
    flat = jnp.pad(flat, (0, -flat.shape[0] % 1024))
    vec = flat.reshape(-1, LANES)
    onehot = jnp.asarray(
        np.arange(LANES)[:, None] == np.arange(inner)[None, :] // head_dim, dtype=BF16
    )
    hot = (onehot, whole((LANES, inner)))
    state_rows = pl.BlockSpec((state_size, inner), lambda c: (c, 0))
    packed_shape = (state_size + HALO, inner)
    (
        act, sact, states_pre, states_halo, step_pre, step, cum, cumt, sin, packed, total_log,
        before_log, params,
    ) = call(
        functools.partial(states_kernel, n),
        (count,),
        [
            (input_pre, rows(inner)),
            (input_pre, before(inner)),
            (input_halo, whole((HALO, inner))),
            (normed, rows(width)),
            (normed_halo, whole((HALO, width))),
            (proj_step_wide, whole((width, LANES))),
            (vec, whole(vec.shape)),
            (conv_input, whole(conv_input.shape)),
            (conv_states, whole(conv_states.shape)),
            hot,
        ]
        + [(piece, whole(piece.shape)) for piece in pieces],
        [
            (sds((tokens, inner)), rows(inner)),
            (sds((tokens, two)), rows(two)),
            (sds((tokens, two)), rows(two)),
            (sds((HALO, two)), whole((HALO, two))),
            (sds((tokens, LANES)), rows(LANES)),
            (sds((tokens, LANES)), rows(LANES)),
            (sds((tokens, LANES)), rows(LANES)),
            (sds((tokens, LANES)), rows(LANES)),
            (sds((count * state_size, inner)), state_rows),
            (sds(packed_shape), whole(packed_shape)),
            (sds((1, LANES)), whole((1, LANES))),
            (sds((count, 1, LANES)), pl.BlockSpec((None, 1, LANES), lambda c: (c, 0, 0))),
            (sds((16, inner)), whole((16, inner))),
        ],
        scratch=[
            pltpu.VMEM((Q + HALO, inner), F32),
            pltpu.VMEM((Q + HALO, two), F32),
            pltpu.VMEM((state_size, inner), F32),
            pltpu.VMEM((1, LANES), F32),
            pltpu.VMEM((width, two), BF16),
        ],
        flops=10 * tokens * inner * state_size,
    )
    par = (params, whole((16, inner)))
    packed, gate_pre, grad_ynorm = lax.optimization_barrier((packed, gate_pre, grad_ynorm))
    yloc, incoming = call(
        functools.partial(intra_kernel, ns),
        (count,),
        [
            (act, rows(inner)),
            (sact, rows(two)),
            (step, rows(LANES)),
            (cum, rows(LANES)),
            (cumt, rows(LANES)),
            par,
            hot,
            (packed, whole(packed_shape)),
        ],
        [
            (sds((tokens, inner)), rows(inner)),
            (sds((state_size, inner)), whole((state_size, inner))),
        ],
        scratch=[pltpu.VMEM((Q, inner), F32), pltpu.VMEM((state_size, inner), F32)]
        + swap_scratch(ns, (state_size, inner)),
        flops=12 * tokens * inner * Q,
        collective=5,
    )

    def both(i):
        return jnp.where(i < count, i, 2 * count - 1 - i)

    def fore(i):
        return jnp.minimum(i, count - 1)

    def aft(i):
        return jnp.minimum(2 * count - 1 - i, count - 1)

    def at(size, which, height=Q):
        return pl.BlockSpec((height, size), lambda i: (which(i), 0))

    y, ynorm, grad_gate_pre, grad_ssd, dout, packed_back, grad_rows = call(
        functools.partial(middle_kernel, n),
        (2 * count,),
        [
            (yloc, at(inner, fore)),
            (act, at(inner, aft)),
            (sact, at(two, both)),
            (cum, at(LANES, both)),
            (sin, at(inner, fore, state_size)),
            (before_log, pl.BlockSpec((None, 1, LANES), lambda i: (fore(i), 0, 0))),
            (total_log, whole((1, LANES))),
            (incoming, whole((state_size, inner))),
            (gate_pre, at(inner, both)),
            (grad_ynorm, at(inner, both)),
            par,
            hot,
        ],
        [
            (sds((tokens, inner)), at(inner, fore)),
            (sds((tokens, inner), BF16), at(inner, aft)),
            (sds((tokens, inner), BF16), at(inner, aft)),
            (sds((tokens, inner)), at(inner, aft)),
            (sds((count * state_size, inner)), at(inner, aft, state_size)),
            (sds(packed_shape), whole(packed_shape)),
            (sds((HALO, inner)), whole((HALO, inner))),
        ],
        scratch=[
            pltpu.VMEM((tokens, inner), F32),
            pltpu.VMEM((HALO, tokens), F32),
            pltpu.VMEM((n, HALO, tokens), F32),
            pltpu.VMEM((state_size, inner), F32),
            pltpu.SemaphoreType.DMA((n,)),
            pltpu.SemaphoreType.DMA((n,)),
        ],
        flops=12 * tokens * inner * state_size,
        collective=3,
    )
    local_proj_output = transposed_times(cotangent, ynorm)
    local_proj_gate = transposed_times(normed, grad_gate_pre)
    own_code, later = reduce_over_heads(
        [(ynorm, proj_output)], [NN], 1, packed=packed_back
    )
    codes = [own_code]
    for k in range(1, n):
        codes.append(turned(own_code, k))
    summed_out = lax.psum_scatter(
        local_proj_output, "seq", scatter_dimension=0, tiled=True
    )
    grad_proj_output = pl.pallas_call(
        turn_kernel, out_shape=sds(summed_out.shape[::-1]), name="turn"
    )(summed_out)
    grad_proj_gate = lax.psum_scatter(
        local_proj_gate, "seq", scatter_dimension=0, tiled=True
    )

    def held(size, height=Q):
        return pl.BlockSpec((height, size), lambda c: (jnp.minimum(c, count - 1), 0))

    def prior(size):
        return pl.BlockSpec((Q, size), lambda c: (jnp.maximum(c - 1, 0), 0))

    def prior_edge(size):
        return pl.BlockSpec(
            (HALO, size), lambda c: (jnp.maximum((c - 1) * (Q // HALO) - 1, 0), 0)
        )

    dma = pltpu.SemaphoreType.DMA
    groups = count // n
    grad_in_b, grad_states_b, small_a, small_b = call(
        functools.partial(back_kernel, n, ns),
        (count + 1,),
        [
            (act, held(inner)),
            (sact, held(two)),
            (y, held(inner)),
            (grad_ssd, held(inner)),
            (step, held(LANES)),
            (step_pre, held(LANES)),
            (cum, held(LANES)),
            (cumt, held(LANES)),
            (sin, held(inner, state_size)),
            (dout, held(inner, state_size)),
            (
                before_log,
                pl.BlockSpec((None, 1, LANES), lambda c: (jnp.minimum(c, count - 1), 0, 0)),
            ),
            (total_log, whole((1, LANES))),
            (incoming, whole((state_size, inner))),
            (later, whole((state_size, inner))),
            par,
            hot,
            (grad_rows, whole((HALO, inner))),
            (input_pre, prior(inner)),
            (input_pre, prior_edge(inner)),
            (input_halo, whole((HALO, inner))),
            (states_pre, prior(two)),
            (states_pre, prior_edge(two)),
            (states_halo, whole((HALO, two))),
        ],
        [
            (sds((tokens, inner + LANES), BF16), prior(inner + LANES)),
            (sds((tokens, two), BF16), whole((tokens, two))),
            (sds((16, inner)), whole((16, inner))),
            (sds((HALO, two)), whole((HALO, two))),
        ],
        scratch=[
            pltpu.VMEM((tokens, two), BF16),
            pltpu.VMEM((2 * Q, LANES), BF16),
            pltpu.VMEM((Q, inner), F32),
            pltpu.VMEM((Q, inner), F32),
            pltpu.VMEM((Q, Q), F32),
            pltpu.VMEM((Q + HALO, inner), F32),
            pltpu.VMEM((2 * Q + HALO, two), F32),
            pltpu.VMEM((Q + HALO, inner), F32),
            pltpu.VMEM((Q + HALO, two), F32),
            pltpu.VMEM((HALO, inner), F32),
            pltpu.VMEM((HALO, inner), F32),
            pltpu.VMEM((HALO, two), F32),
            pltpu.VMEM((HALO, two), F32),
            pltpu.VMEM((tokens, two), F32),
            pltpu.VMEM((n, groups * Q, two), F32),
            dma((4,)),
            dma((count,)),
            dma((n, groups)),
            dma((n, groups)),
            dma((n, groups)),
        ],
        flops=40 * tokens * inner * Q,
        collective=4,
    )
    stream = tokens // STREAMS
    result = call(
        functools.partial(result_kernel, n),
        (STREAMS,),
        [
            (code, pl.BlockSpec((stream // n, width + LANES), lambda c: (c, 0)))
            for code in codes
        ]
        + [(hidden, pl.BlockSpec((stream, width), lambda c: (c, 0)))],
        [(sds((tokens, width)), pl.BlockSpec((stream, width), lambda c: (c, 0)))],
        flops=20 * tokens * width,
    )[0]
    row_start = head_index * row_width
    own_states = lax.dynamic_update_slice_in_dim(
        jnp.zeros((width, two), BF16), proj_states, row_start, 0
    )
    normed_rows = lax.dynamic_slice_in_dim(normed, row_start, row_width, 1)
    local_proj_in = transposed_times(normed, grad_in_b)
    local_proj_states = transposed_times(grad_states_b, normed_rows)
    summed_in = lax.psum_scatter(local_proj_in, "seq", scatter_dimension=0, tiled=True)
    grad_code, sum_a, sum_b, grad_proj_states = reduce_over_heads(
        [
            (grad_gate_pre, proj_gate),
            (grad_in_b, proj_input),
            (grad_in_b, proj_step_wide),
            (grad_states_b, own_states),
        ],
        [NT] * 4,
        2,
        (hidden, inv_rms, small_a, small_b, local_proj_states),
        cols=(None, (0, inner), (inner, inner + LANES), None),
    )
    grad_hidden = call(
        hidden_kernel,
        (count,),
        [
            (grad_code, rows(width + LANES)),
            (hidden, rows(width)),
            (cotangent, rows(width)),
            (inv_rms, rows(1)),
            (gain_full[None, :], whole((1, width))),
        ],
        [(sds((tokens, width)), rows(width))],
        flops=20 * tokens * width,
    )[0]
    return (
        result,
        grad_hidden,
        sum_b[0],
        grad_proj_gate,
        summed_in[:, :inner],
        grad_proj_states.T,
        summed_in[:, inner : inner + heads],
        sum_a[:TAPS],
        sum_a[4],
        sum_b[8 : 8 + TAPS, :two],
        sum_b[12, :two],
        sum_a[7, LANES : LANES + heads],
        sum_a[7, :heads],
        jnp.sum(sum_a[6].reshape(heads, head_dim), axis=1),
        sum_a[5],
        grad_proj_output,
    )


def solution(mesh):
    in_specs = (
        P("seq", None),
        P(),
        P(None, "head"),
        P(None, "head"),
        P("head", None),
        P(None, "head"),
        P(None, "head"),
        P("head"),
        P(),
        P(),
        P("head"),
        P("head"),
        P("head"),
        P("head"),
        P("head", None),
        P("seq", None),
    )
    out_specs = (
        P("seq", None),
        P("seq", None),
        P(),
        P("seq", "head"),
        P("seq", "head"),
        P("head", "seq"),
        P("seq", "head"),
        P(None, "head"),
        P("head"),
        P(),
        P(),
        P("head"),
        P("head"),
        P("head"),
        P("head"),
        P("head", "seq"),
    )

    return jax.shard_map(
        on_device, mesh=mesh, in_specs=in_specs, out_specs=out_specs, check_vma=False
    )
```

```python
import functools

import jax
import jax.numpy as jnp
import numpy as np
from jax import lax
from jax.experimental import pallas as pl
from jax.experimental.pallas import tpu as pltpu
from jax.sharding import PartitionSpec as P


DI = 3072
EPS = 1e-05
Q = 128
LANES = 128
HALO = 8
TAPS = 4

F32 = jnp.float32
BF16 = jnp.bfloat16
NN = (((1,), (0,)), ((), ()))
NT = (((1,), (1,)), ((), ()))
TN = (((0,), (0,)), ((), ()))
VMEM_LIMIT = 60 * 1024 * 1024
MESH_ID = pl.DeviceIdType.MESH


def dg(left, right, dims):
    return lax.dot_general(left, right, dims, preferred_element_type=F32)


def split(value):
    high = value.astype(BF16)
    return high, (value - high.astype(F32)).astype(BF16)


def dot3(left, right, dims):
    (lh, ll), (rh, rl) = split(left), split(right)
    return dg(lh, rh, dims) + (dg(lh, rl, dims) + dg(ll, rh, dims))


def spread(heads, onehot):
    high, low = split(heads)
    return dg(high, onehot, NN) + dg(low, onehot, NN)


def gather(wide, onehot):
    high, low = split(wide)
    return dg(high, onehot, NT) + dg(low, onehot, NT)


def sigmoid(value):
    return 1.0 / (1.0 + jnp.exp(-value))


def silu(value):
    return value * sigmoid(value)


def shifted(block, axis, distance):
    devices = range(lax.axis_size(axis))
    route = [(i - distance, i) for i in devices if i - distance in devices]
    return lax.ppermute(block, axis, route)


def call(kernel, grid, ins, outs, scratch=(), flops=0, collective=None):
    in_specs = [spec for _, spec in ins]
    size = sum(a.size * a.dtype.itemsize for a, _ in ins) + sum(
        s.size * s.dtype.itemsize for s, _ in outs
    )
    return pl.pallas_call(
        kernel,
        grid=grid,
        in_specs=in_specs,
        out_specs=[spec for _, spec in outs],
        out_shape=[shape for shape, _ in outs],
        scratch_shapes=list(scratch),
        cost_estimate=pl.CostEstimate(flops=flops, bytes_accessed=size, transcendentals=0),
        compiler_params=pltpu.CompilerParams(vmem_limit_bytes=VMEM_LIMIT)
        if collective is None
        else pltpu.CompilerParams(
            vmem_limit_bytes=VMEM_LIMIT, collective_id=collective, has_side_effects=True
        ),
    )(*[a for a, _ in ins])


def sds(shape, dtype=F32):
    return jax.ShapeDtypeStruct(shape, dtype)


def rows(width, reverse=None):
    if reverse is None:
        return pl.BlockSpec((Q, width), lambda c: (c, 0))
    return pl.BlockSpec((Q, width), lambda c: (reverse - 1 - c, 0))


def whole(shape):
    return pl.BlockSpec(shape, lambda c: (0,) * len(shape))


def before(width):
    return pl.BlockSpec((HALO, width), lambda c: (jnp.maximum(c * (Q // HALO) - 1, 0), 0))


def triangle(lower):
    a = lax.broadcasted_iota(jnp.int32, (Q, Q), 0)
    b = lax.broadcasted_iota(jnp.int32, (Q, Q), 1)
    return a >= b if lower else a <= b


def tri_sum(lower, value):
    mask = triangle(lower).astype(BF16)
    high = value.astype(BF16)
    rest = value - high.astype(F32)
    mid = rest.astype(BF16)
    low = (rest - mid.astype(F32)).astype(BF16)
    return dg(mask, high, NN) + (dg(mask, mid, NN) + dg(mask, low, NN))


def conv_act(pre_ref, prev_ref, halo_ref, params, at, ext_ref):
    first = pl.program_id(0) == 0
    size = ext_ref.shape[1]
    ext_ref[:HALO, :] = jnp.where(first, halo_ref[...], prev_ref[...])
    ext_ref[HALO:, :] = pre_ref[...]
    taps = TAPS
    total = params[at + taps : at + taps + 1, :size] + params[at + taps - 1 : at + taps, :size] * pre_ref[...]
    for k in range(taps - 1):
        start = HALO - taps + 1 + k
        total = total + params[at + k : at + k + 1, :size] * ext_ref[start : start + Q, :]
    return total


def states_kernel(
    n, pre, pre_prev, pre_halo, normed, normed_halo, step_w, vec, taps_in, taps_st, onehot, *refs
):
    pieces, refs = refs[:n], refs[n:]
    act_o, sact_o, spre_o, shalo_o, spre_step_o, step_o, cum_o, cumt_o, sin_o, dev_o, total_o = refs[:11]
    before_o, params = refs[11:13]
    ext, sext, state, total, full = refs[13:]
    c = pl.program_id(0)
    me = lax.axis_index("head")
    state_size = bmat_width(sact_o)
    inner = pre.shape[1]
    two = 2 * state_size
    hot = onehot[...]

    def line(first, size):
        return jnp.concatenate([vec[r : r + 1, :] for r in range(first, first + size // LANES)], axis=1)

    @pl.when(c == 0)
    def _():
        state[...] = jnp.zeros_like(state)
        total[...] = jnp.zeros_like(total)
        height = pieces[0].shape[0]
        for k in range(n):
            full[pl.ds(pl.multiple_of(((me + n - k) % n) * height, height), height), :] = pieces[k][...]
        params[...] = jnp.zeros_like(params)
        per = inner // LANES
        params[0:TAPS, :] = taps_in[...].astype(F32)
        params[4:5, :] = line(3, inner)
        params[5:6, :] = line(3 + per, inner)
        params[6:7, :] = spread(jnp.broadcast_to(vec[2:3, :], (HALO, LANES)), hot)[:1]
        params[7:8, :LANES] = -jnp.exp(vec[0:1, :])
        params[7:8, LANES : 2 * LANES] = vec[1:2, :]
        params[8 : 8 + TAPS, :two] = taps_st[...].astype(F32)
        params[12:13, :two] = line(3 + 2 * per, two)
        first = dg(normed_halo[...], full[...], NN)
        shalo_o[...] = jnp.where(lax.axis_index("seq") == 0, 0.0, first)
        sext[Q:, :] = shalo_o[...]

    sext[:HALO, :] = sext[Q:, :]
    spre = dg(normed[...], full[...], NN)
    spre_o[...] = spre
    sext[HALO:, :] = spre
    step_pre = dg(normed[...], step_w[...], NN)
    spre_step_o[...] = step_pre
    act = conv_act(pre, pre_prev, pre_halo, params, 0, ext)
    sact = params[12:13, :two] + params[8 + TAPS - 1 : 8 + TAPS, :two] * spre
    for k in range(TAPS - 1):
        start = HALO - TAPS + 1 + k
        sact = sact + params[8 + k : 9 + k, :two] * sext[start : start + Q, :]
    act_o[...] = act
    sact_o[...] = sact
    bmat = silu(sact[:, :state_size])
    step = jax.nn.softplus(step_pre + params[7:8, LANES : 2 * LANES])
    cum = tri_sum(True, step * params[7:8, :LANES])
    step_o[...] = step
    cum_o[...] = cum
    cumt_o[...] = cum.T
    last = cum[Q - 1 :, :]
    weight = spread(step * jnp.exp(last - cum), hot)
    xw = silu(act) * weight
    sin_o[...] = state[...]
    before_o[...] = total[...]
    decay = spread(jnp.broadcast_to(jnp.exp(last), (HALO, LANES)), hot)[:1]
    state[...] = state[...] * decay + dot3(bmat, xw, TN)
    total[...] = total[...] + last
    dev_o[:state_size, :] = state[...]
    dev_o[state_size:, :] = spread(jnp.broadcast_to(jnp.exp(total[...]), (HALO, LANES)), hot)
    total_o[...] = total[...]


def bmat_width(ref):
    return ref.shape[1] // 2


def pair_stack(value):
    high, low = split(value)
    return jnp.concatenate(
        [
            jnp.concatenate([high, low], axis=1),
            jnp.concatenate([high, jnp.zeros_like(high)], axis=1),
        ],
        axis=0,
    )


def intra_kernel(
    ns, act, sact, step, cum, cumt, params, onehot, packed, out, incoming,
    xs_ref, entered, got_s, got_d, prefix, sems,
):
    c = pl.program_id(0)
    count = pl.num_programs(0)
    seq = lax.axis_index("seq")
    begin, turn, end = swap_states(ns, packed, entered, got_s, got_d, prefix, sems, False)
    barrier = pltpu.get_barrier_semaphore()

    @pl.when(c == 0)
    def _():
        for k in range(1, ns):
            pl.semaphore_signal(
                barrier, inc=1, device_id={"seq": (seq + k) % ns}, device_id_type=MESH_ID
            )
        pl.semaphore_wait(barrier, ns - 1)
        begin()

    state_size = bmat_width(sact)
    sconv = silu(sact[...])
    bmat, cmat = sconv[:, :state_size], sconv[:, state_size:]
    scores = dot3(cmat, bmat, NT)
    x = silu(act[...])
    xs_ref[...] = x * spread(step[...], onehot[...])
    out[...] = x * params[6:7, :]
    causal = triangle(True)
    lane = lax.broadcasted_iota(jnp.int32, (Q, LANES), 1)
    for p in range(act.shape[1] // LANES):
        cols = slice(p * LANES, (p + 1) * LANES)
        right = pair_stack(xs_ref[:, cols])
        got = []
        for j in range(2):
            h = p * 2 + j
            gap = cum[:, h : h + 1] - cumt[h : h + 1, :]
            mixing = scores * jnp.exp(jnp.where(causal, gap, -1e30))
            wide = dg(jnp.concatenate(split(mixing), axis=1), right, NN)
            got.append(wide[:, :LANES] + wide[:, LANES:])
        out[:, cols] = out[:, cols] + jnp.where(lane < LANES // 2, got[0], got[1])

    @pl.when(c == count // 2)
    def _():
        turn()

    @pl.when(c == count - 1)
    def _():
        end()
        incoming[...] = entered[...]


STREAMS = 4
GAP = 2
SPAN = 83.0


def encode(value):
    top = jnp.max(jnp.abs(value), axis=1, keepdims=True)
    scale = (top * 1.004 + 1e-30).astype(BF16)
    code = jnp.exp(value * (SPAN / scale.astype(F32))).astype(BF16)
    return code, jnp.broadcast_to(scale, (value.shape[0], LANES))


def decode(block, width):
    scale = block[:, width : width + 1].astype(F32) * (1.0 / SPAN)
    return jnp.log(block[:, :width].astype(F32)) * scale


def swap_states(ns, packed, out, got_s, got_d, prefix, sems, reverse):
    seq = lax.axis_index("seq")
    own = out.shape[0] // ns
    total = out.shape[0]

    def rows_of(j):
        return pl.ds(pl.multiple_of(j * own, own), own)

    def remote(src, dst, send, recv, to):
        return pltpu.make_async_remote_copy(
            src_ref=src,
            dst_ref=dst,
            send_sem=send,
            recv_sem=recv,
            device_id={"seq": to},
            device_id_type=MESH_ID,
        )

    def copies(k, arriving):
        other = (seq + k) % ns
        slot = other if arriving else seq
        part = packed.at[rows_of(other)]
        decay = packed.at[pl.ds(total, HALO)]
        return (
            remote(part, got_s.at[slot], sems.at[0, k], sems.at[1, slot], other),
            remote(decay, got_d.at[slot], sems.at[2, k], sems.at[3, slot], other),
        )

    def answer(k, arriving):
        other = (seq + k) % ns
        slot = other if arriving else seq
        return remote(
            prefix.at[other], out.at[rows_of(slot)], sems.at[4, k], sems.at[5, slot], other
        )

    def begin():
        for k in range(1, ns):
            for copy in copies(k, False):
                copy.start()

    def turn():
        got_s[seq] = packed[rows_of(seq), :]
        got_d[seq] = packed[total:, :]
        for k in range(1, ns):
            for copy in copies(k, True):
                copy.wait_recv()
        carry = jnp.zeros((own, out.shape[1]), F32)
        for i in reversed(range(ns)) if reverse else range(ns):
            prefix[i] = carry
            carry = carry * got_d[i, 0:1, :] + got_s[i]
        for k in range(1, ns):
            answer(k, False).start()
        out[rows_of(seq), :] = prefix[seq]

    def end():
        for k in range(1, ns):
            answer(k, True).wait_recv()
        for k in range(1, ns):
            answer(k, False).wait_send()
            for copy in copies(k, False):
                copy.wait_send()

    return begin, turn, end


def swap_scratch(ns, shape):
    own = shape[0] // ns
    return [
        pltpu.VMEM((ns, own, shape[1]), F32),
        pltpu.VMEM((ns, HALO, shape[1]), F32),
        pltpu.VMEM((ns, own, shape[1]), F32),
        pltpu.SemaphoreType.DMA((6, ns)),
    ]


def put(ref, where, value):
    code, scale = encode(value)
    width = value.shape[1]
    ref[where, :width] = code
    ref[where, width:] = scale


def chain_scratch(tokens, width, n):
    coded = pltpu.VMEM((tokens, width + LANES), BF16)
    return [pltpu.VMEM((tokens, width), F32), coded, coded, coded] + [
        pltpu.SemaphoreType.DMA((STREAMS, n))
    ] * 6


def chains(n, all_ref, part, code, got_r, got_l, s_sem, rr_sem, rl_sem, ar_sem, al_sem, ag_sem):
    me = lax.axis_index("head")
    tokens, width = part.shape
    span = tokens // STREAMS
    rows_own = span // n
    has_right, has_left = me < n - 1, me > 0

    def at(d, h):
        return pl.ds(pl.multiple_of(h * span + d * rows_own, rows_own), rows_own)

    def step(d, h, right):
        return pltpu.make_async_remote_copy(
            src_ref=code.at[at(d, h)],
            dst_ref=(got_r if right else got_l).at[at(d, h)],
            send_sem=s_sem.at[h, d],
            recv_sem=(rr_sem if right else rl_sem).at[h, d],
            device_id={"head": me + 1 if right else me - 1},
            device_id_type=MESH_ID,
        )

    def hand_on(b, h, right):
        return pltpu.make_async_remote_copy(
            src_ref=all_ref.at[at(b, h)],
            dst_ref=all_ref.at[at(b, h)],
            send_sem=(ar_sem if right else al_sem).at[h, b],
            recv_sem=ag_sem.at[h, b],
            device_id={"head": me + 1 if right else me - 1},
            device_id_type=MESH_ID,
        )

    def chain(h, u):
        for right in (True, False):
            d = me + (n - 1 - u) if right else me - (n - 1 - u)
            got = got_r if right else got_l
            inside = d <= n - 1 if right else d >= 0
            fed = has_left if right else has_right

            @pl.when(inside & fed)
            def _():
                step(d, h, right).wait_recv()
                put(code, at(d, h), part[at(d, h), :] + decode(got[at(d, h), :], width))
                step(d, h, right).start()

            @pl.when(inside & jnp.logical_not(fed))
            def _():
                put(code, at(d, h), part[at(d, h), :])
                step(d, h, right).start()

    def finish(h):
        own = at(me, h)

        @pl.when(has_left)
        def _():
            step(me, h, True).wait_recv()
            part[own, :] = part[own, :] + decode(got_r[own, :], width)

        @pl.when(has_right)
        def _():
            step(me, h, False).wait_recv()
            part[own, :] = part[own, :] + decode(got_l[own, :], width)

        put(all_ref, own, part[own, :])

        @pl.when(has_right)
        def _():
            hand_on(me, h, True).start()

        @pl.when(has_left)
        def _():
            hand_on(me, h, False).start()

    def relay(h, s):
        @pl.when(me - s >= 0)
        def _():
            hand_on(me - s, h, True).wait_recv()

            @pl.when(has_right)
            def _():
                hand_on(me - s, h, True).start()

        @pl.when(me + s < n)
        def _():
            hand_on(me + s, h, False).wait_recv()

            @pl.when(has_left)
            def _():
                hand_on(me + s, h, False).start()

    def slot(t):
        for h in range(STREAMS):
            u = t - GAP * h
            if 0 <= u < n - 1:
                chain(h, u)
            if u == n - 1:
                finish(h)
            if n - 1 < u < 2 * n - 1:
                relay(h, u - n + 1)

    def drain():
        for h in range(STREAMS):
            for i in range(n):

                @pl.when(i > me)
                def _():
                    step(i, h, True).wait_send()

                @pl.when(i < me)
                def _():
                    step(i, h, False).wait_send()

                @pl.when(has_right & (i <= me))
                def _():
                    hand_on(i, h, True).wait_send()

                @pl.when(has_left & (i >= me))
                def _():
                    hand_on(i, h, False).wait_send()

    return slot, drain


def slots_of(n):
    return GAP * (STREAMS - 1) + 2 * n - 1


def greet(n, ns):
    barrier = pltpu.get_barrier_semaphore()
    me, seq = lax.axis_index("head"), lax.axis_index("seq")
    for k in range(1, n):
        pl.semaphore_signal(
            barrier, inc=1, device_id={"head": (me + k) % n}, device_id_type=MESH_ID
        )
    for k in range(1, ns):
        pl.semaphore_signal(
            barrier, inc=1, device_id={"seq": (seq + k) % ns}, device_id_type=MESH_ID
        )
    return barrier


def reduce_kernel(n, ns, dims, cols, *refs):
    terms = len(dims)
    lefts, rights = refs[:terms], refs[terms : 2 * terms]
    refs = refs[2 * terms :]
    hidden_ref, inv_ref, small_a, small_b, states_ref, out_ref, sum_a, sum_b, sum_s = refs[:9]
    slot, drain = chains(n, out_ref, *refs[9:19])
    part = refs[9]
    got_a, got_b, got_s, got_c, mine_b = refs[19:24]
    sa_sem, ra_sem, sb_sem, rb_sem, ss_sem, rs_sem, sc_sem, rc_sem = refs[24:]
    me, seq = lax.axis_index("head"), lax.axis_index("seq")
    tokens, width = part.shape
    span = tokens // STREAMS
    barrier = greet(n, ns)

    def to_seq(src, dst, ssem, rsem, k):
        return pltpu.make_async_remote_copy(
            src_ref=src,
            dst_ref=dst.at[seq],
            send_sem=ssem.at[k],
            recv_sem=rsem.at[seq],
            device_id={"seq": (seq + k) % ns},
            device_id_type=MESH_ID,
        )

    def from_seq(src, dst, ssem, rsem, k):
        other = (seq + k) % ns
        return pltpu.make_async_remote_copy(
            src_ref=src,
            dst_ref=dst.at[other],
            send_sem=ssem.at[k],
            recv_sem=rsem.at[other],
            device_id={"seq": other},
            device_id_type=MESH_ID,
        )

    def states_at(j):
        own = sum_s.shape[0]
        return states_ref.at[pl.ds(pl.multiple_of(j * own, own), own)]

    def compute(h):
        where = pl.ds(h * span, span)
        total = None
        for left, right, dim, col in zip(lefts, rights, dims, cols):
            value = left[where, :] if col is None else left[where, col[0] : col[1]]
            term = dg(value, right[...], dim)
            total = term if total is None else total + term
        part[where, :] = total
        seen = total * (hidden_ref[where, :].astype(F32) * inv_ref[where, :])
        row = jnp.sum(seen, axis=0, keepdims=True)
        mine_b[0:1, :] = row if h == 0 else mine_b[0:1, :] + row

    for t in range(slots_of(n)):
        for h in range(STREAMS):
            if t == GAP * h:
                compute(h)
        if t == 0:
            pl.semaphore_wait(barrier, n + ns - 2)
        slot(t)
        if t == 1:
            for k in range(1, ns):
                to_seq(small_a, got_a, sa_sem, ra_sem, k).start()
                to_seq(states_at((seq + k) % ns), got_s, ss_sem, rs_sem, k).start()
        if t == GAP * (STREAMS - 1):
            mine_b[8:16, :] = jnp.zeros((8, width), F32)
            mine_b[8:16, : small_b.shape[1]] = small_b[...]
            for k in range(1, ns):
                to_seq(mine_b, got_b, sb_sem, rb_sem, k).start()
        if t == slots_of(n) - 2:
            total = small_a[...]
            for k in range(1, ns):
                from_seq(small_a, got_a, sa_sem, ra_sem, k).wait_recv()
                total = total + got_a[(seq + k) % ns]
            sum_a[...] = total
            total = states_at(seq)[...]
            for k in range(1, ns):
                from_seq(states_at(seq), got_s, ss_sem, rs_sem, k).wait_recv()
                total = total + got_s[(seq + k) % ns]
            sum_s[...] = total
            total = mine_b[...]
            for k in range(1, ns):
                from_seq(mine_b, got_b, sb_sem, rb_sem, k).wait_recv()
                total = total + got_b[(seq + k) % ns]
            sum_b[...] = total

            def to_head(k):
                return pltpu.make_async_remote_copy(
                    src_ref=sum_b,
                    dst_ref=got_c.at[me],
                    send_sem=sc_sem.at[k],
                    recv_sem=rc_sem.at[me],
                    device_id={"head": (me + k) % n},
                    device_id_type=MESH_ID,
                )

            def from_head(k):
                other = (me + k) % n
                return pltpu.make_async_remote_copy(
                    src_ref=sum_b,
                    dst_ref=got_c.at[other],
                    send_sem=sc_sem.at[k],
                    recv_sem=rc_sem.at[other],
                    device_id={"head": other},
                    device_id_type=MESH_ID,
                )

            for k in range(1, n):
                to_head(k).start()
    total = sum_b[...]
    for k in range(1, n):
        from_head(k).wait_recv()
    for k in range(1, n):
        to_head(k).wait_send()
        total = total + got_c[(me + k) % n]
    sum_b[...] = total
    for k in range(1, ns):
        to_seq(small_a, got_a, sa_sem, ra_sem, k).wait_send()
        to_seq(states_at((seq + k) % ns), got_s, ss_sem, rs_sem, k).wait_send()
        to_seq(mine_b, got_b, sb_sem, rb_sem, k).wait_send()
    drain()


def reduce_over_heads(products, dims, cols, collective, sums):
    n, ns = lax.axis_size("head"), lax.axis_size("seq")
    tokens, width = sums[0].shape
    lefts, rights = [a for a, _ in products], [b for _, b in products]
    dma = pltpu.SemaphoreType.DMA
    small_a = sums[2].shape
    states = (sums[4].shape[0] // ns, sums[4].shape[1])
    out_shape = [sds((tokens, width + LANES), BF16), sds(small_a), sds((16, width)), sds(states)]
    scratch = chain_scratch(tokens, width, n) + [
        pltpu.VMEM((ns, *small_a), F32),
        pltpu.VMEM((ns, 16, width), F32),
        pltpu.VMEM((ns, *states), F32),
        pltpu.VMEM((n, 16, width), F32),
        pltpu.VMEM((16, width), F32),
    ]
    scratch += [dma((ns,))] * 6 + [dma((n,))] * 2
    vmem = pl.BlockSpec(memory_space=pltpu.VMEM)
    return pl.pallas_call(
        functools.partial(reduce_kernel, n, ns, dims, cols),
        in_specs=[vmem] * (len(lefts) + len(rights) + len(sums)),
        out_specs=[vmem] * len(out_shape),
        out_shape=out_shape,
        scratch_shapes=scratch,
        compiler_params=pltpu.CompilerParams(
            collective_id=collective, has_side_effects=True, vmem_limit_bytes=VMEM_LIMIT
        ),
        cost_estimate=pl.CostEstimate(
            flops=2 * tokens * width * sum(a.shape[1] for a in lefts),
            bytes_accessed=100 * tokens * width,
            transcendentals=0,
        ),
        name="reduce_heads",
    )(*lefts, *rights, *sums)


def result_kernel(code, hidden, out):
    out[...] = hidden[...].astype(F32) + decode(code[...], out.shape[1])


def turn_kernel(value, out):
    high = value.shape[0]
    more = jnp.zeros((-high % LANES, value.shape[1]), F32)
    out[...] = jnp.concatenate([value[...], more], axis=0).T[:, :high]


def hidden_kernel(code, hidden, cotangent, inv, gain, out):
    width = out.shape[1]
    grad = decode(code[...], width) * gain[...]
    resid = hidden[...].astype(F32)
    scale = inv[...]
    dots = jnp.sum(grad * resid, axis=1, keepdims=True) * (1.0 / width)
    out[...] = (
        cotangent[...].astype(F32) + scale * grad - resid * (scale * scale * scale * dots)
    )


def rows_of_sums(square, cross):
    ones = jnp.ones((HALO, square.shape[1]), BF16)
    (sh, sl), (ch, cl) = split(square), split(cross)
    first = dg(ones, sh, NT) + dg(ones, sl, NT)
    second = dg(ones, ch, NT) + dg(ones, cl, NT)
    row = lax.broadcasted_iota(jnp.int32, first.shape, 0)
    return jnp.where(row == 0, first, second)


def middle_kernel(
    n, yloc, act, sact, cum, sin, before_log, total_log, incoming, gate, gyn, params, onehot,
    y_o, ynorm_o, gpre_o, gssd_o, dout_o, dev_o, rows_o,
    keep, mine, got, adj, ssem, rsem,
):
    i = pl.program_id(0)
    count = pl.num_programs(0) // 2
    c = jnp.where(i < count, i, 2 * count - 1 - i)
    me = lax.axis_index("head")
    state_size = bmat_width(sact)
    hot = onehot[...]
    gain = params[5:6, :]
    where = pl.ds(pl.multiple_of(c * Q, Q), Q)
    barrier = pltpu.get_barrier_semaphore()

    def copy(k, arriving):
        other = (me + k) % n
        return pltpu.make_async_remote_copy(
            src_ref=mine,
            dst_ref=got.at[other if arriving else me],
            send_sem=ssem.at[k],
            recv_sem=rsem.at[other if arriving else me],
            device_id={"head": other},
            device_id_type=MESH_ID,
        )

    @pl.when(i == 0)
    def _():
        for k in range(1, n):
            pl.semaphore_signal(
                barrier, inc=1, device_id={"head": (me + k) % n}, device_id_type=MESH_ID
            )

    cmat = silu(sact[:, state_size:])
    gv = gate[...]
    sg = sigmoid(gv)
    gsilu = gv * sg
    growth = spread(jnp.exp(cum[...]), hot)

    @pl.when(i < count)
    def _():
        carry = spread(jnp.broadcast_to(jnp.exp(before_log[...]), (HALO, LANES)), hot)[:1]
        state = sin[...] + carry * incoming[...]
        y = yloc[...] + growth * dot3(cmat, state, NN)
        y_o[...] = y
        keep[where, :] = y
        gated = y * gsilu
        mine[:, where] = rows_of_sums(gated * gated, gyn[...] * gain * gated)

    @pl.when(i == count - 1)
    def _():
        pl.semaphore_wait(barrier, n - 1)
        for k in range(1, n):
            copy(k, False).start()

    @pl.when(i == count)
    def _():
        adj[...] = jnp.zeros_like(adj)
        rows_o[...] = jnp.zeros_like(rows_o)
        total = mine[...]
        for k in range(1, n):
            copy(k, True).wait_recv()
        for k in range(1, n):
            copy(k, False).wait_send()
            total = total + got[(me + k) % n]
        mine[...] = total

    @pl.when(i >= count)
    def _():
        total = mine[:, where]
        columns = jnp.concatenate([total, jnp.zeros((Q - HALO, Q), F32)], axis=0).T
        inv = lax.rsqrt(columns[:, 0:1] / DI + EPS)
        cross = columns[:, 1:2] / DI
        yv = keep[where, :]
        gated = yv * gsilu
        normed = gated * inv
        ynorm_o[...] = (normed * gain).astype(BF16)
        rows_o[0:1, :] = rows_o[0:1, :] + jnp.sum(gyn[...] * normed, axis=0, keepdims=True)
        ggated = inv * (gyn[...] * gain) - normed * (inv * inv * cross)
        gpre_o[...] = (ggated * yv * sg * (1.0 + gv * (1.0 - sg))).astype(BF16)
        gssd = ggated * gsilu
        gssd_o[...] = gssd
        rows_o[1:2, :] = rows_o[1:2, :] + jnp.sum(gssd * silu(act[...]), axis=0, keepdims=True)
        dout_o[...] = adj[...]
        decay = spread(jnp.broadcast_to(jnp.exp(cum[Q - 1 :, :]), (HALO, LANES)), hot)[:1]
        adj[...] = adj[...] * decay + dot3(cmat, gssd * growth, TN)

    @pl.when(i == 2 * count - 1)
    def _():
        dev_o[:state_size, :] = adj[...]
        whole_log = jnp.broadcast_to(jnp.exp(total_log[...]), (HALO, LANES))
        dev_o[state_size:, :] = spread(whole_log, hot)


def back_kernel(
    n, ns, act, sact, y, gssd, step, step_pre, cum, cumt, sin, dout, before_log, total_log, incoming,
    ynorm, proj_output, packed,
    params, onehot, rows_in, pre, pre_prev, pre_halo, spre, spre_prev, spre_halo,
    gin_o, gsb_out, small_a, small_b, code_out,
    gsb_o, gstep, xs_ref, u_ref, st_ref, gext, sext, pext, spext, halo_send, halo_got, shalo_send, shalo_got,
    psum, pgot, h_sem, p_send, p_recv, g_send, g_recv,
    later, got_states, got_decays, prefix, swap_sems, all_ref, part, *chain_refs,
):
    i = pl.program_id(0)
    c = i - 1
    count = pl.num_programs(0) - 2
    total_chunks = psum.shape[0] // Q
    begin, turn, end = swap_states(
        ns, packed, later, got_states, got_decays, prefix, swap_sems, True
    )
    slot, drain = chains(n, all_ref, part, *chain_refs)
    span = part.shape[0] // STREAMS
    groups = total_chunks // n
    taps = TAPS
    me, seq = lax.axis_index("head"), lax.axis_index("seq")
    state_size = bmat_width(sact)
    two = 2 * state_size

    def halo(src, dst, k):
        return pltpu.make_async_remote_copy(
            src_ref=src,
            dst_ref=dst,
            send_sem=h_sem.at[k],
            recv_sem=h_sem.at[k + 1],
            device_id={"seq": (seq + ns - 1) % ns},
            device_id_type=MESH_ID,
        )

    def chunk_rows(k):
        return pl.ds(pl.multiple_of(k * Q, Q), Q)

    def to_owner(k):
        return pltpu.make_async_remote_copy(
            src_ref=psum.at[chunk_rows(k)],
            dst_ref=pgot.at[me, chunk_rows(k // n)],
            send_sem=p_send.at[k],
            recv_sem=p_recv.at[me, k // n],
            device_id={"head": k % n},
            device_id_type=MESH_ID,
        )

    def from_other(j, g):
        return pltpu.make_async_remote_copy(
            src_ref=psum.at[chunk_rows(g)],
            dst_ref=pgot.at[j, chunk_rows(g)],
            send_sem=p_send.at[g],
            recv_sem=p_recv.at[j, g],
            device_id={"head": j},
            device_id_type=MESH_ID,
        )

    def give(k, g, arriving):
        other = (me + k) % n
        owner = other if arriving else me
        where = chunk_rows(g * n + owner)
        return pltpu.make_async_remote_copy(
            src_ref=gsb_o.at[where],
            dst_ref=gsb_o.at[where],
            send_sem=g_send.at[k, g],
            recv_sem=g_recv.at[owner, g],
            device_id={"head": other},
            device_id_type=MESH_ID,
        )

    @pl.when(i == 0)
    def _():
        barrier = greet(n, ns)
        small_a[...] = jnp.zeros_like(small_a)
        small_b[...] = jnp.zeros_like(small_b)
        small_a[5:7, :] = rows_in[0:2, :]

        def compute(h):
            where = pl.ds(h * span, span)
            part[where, :] = dg(ynorm[where, :], proj_output[...], NN)

        compute(0)
        pl.semaphore_wait(barrier, n + ns - 2)
        begin()
        slot(0)
        compute(1)
        slot(1)
        for h in range(2, STREAMS):
            compute(h)
        turn()
        slot(2)
        end()

    @pl.when((c >= 0) & (c < count))
    def _():
        hot = onehot[...]
        skip = params[6:7, :]
        rate = params[7:8, :LANES]
        sactv = sact[...]
        ssg = sigmoid(sactv)
        sconv = sactv * ssg
        bmat, cmat = sconv[:, :state_size], sconv[:, state_size:]
        actv = act[...]
        sg = sigmoid(actv)
        x = actv * sg
        cumv, stepv = cum[...], step[...]
        last = cumv[Q - 1 :, :]
        step_wide = spread(stepv, hot)
        xs = x * step_wide
        xs_ref[...] = xs
        g = gssd[...]

        def row(value):
            return spread(jnp.broadcast_to(jnp.exp(value), (HALO, LANES)), hot)[:1]

        state = sin[...] + row(before_log[...]) * incoming[...]
        adj = dout[...] + row(total_log[...] - before_log[...] - last) * later[...]
        to_end = spread(jnp.exp(last - cumv), hot)
        u_state = to_end * dot3(bmat, adj, NN)
        ends = row(last) * jnp.sum(adj * state, axis=0, keepdims=True) + jnp.sum(
            xs * u_state, axis=0, keepdims=True
        )
        scores_t = dot3(bmat, cmat, NT)
        later_mask = triangle(False)
        lane = lax.broadcasted_iota(jnp.int32, (Q, LANES), 1)
        st_ref[...] = jnp.zeros_like(st_ref)
        for p in range(act.shape[1] // LANES):
            cols = slice(p * LANES, (p + 1) * LANES)
            right = pair_stack(gssd[:, cols])
            g_high, g_low = right[:Q, :LANES], right[:Q, LANES:]
            twice = jnp.concatenate([g_high, g_high], axis=1)
            pair = xs_ref[:, cols]
            got = []
            for j in range(2):
                h = p * 2 + j
                gap = cumt[h : h + 1, :] - cum[:, h : h + 1]
                decay = jnp.exp(jnp.where(later_mask, gap, -1e30))
                wide = dg(jnp.concatenate(split(scores_t * decay), axis=1), right, NN)
                got.append(wide[:, :LANES] + wide[:, LANES:])
                mine = (lane < LANES // 2) if j == 0 else (lane >= LANES // 2)
                xh, xl = split(jnp.where(mine, pair, 0.0))
                inner = dg(jnp.concatenate([xh, xl], axis=1), twice, NT) + dg(xh, g_low, NT)
                st_ref[...] = st_ref[...] + decay * inner
            u_ref[:, cols] = jnp.where(lane < LANES // 2, got[0], got[1])
        u = u_ref[...] + u_state
        sc = st_ref[...]
        g_scaled = g * spread(jnp.exp(cumv), hot)
        gstates = jnp.concatenate(
            [
                dot3(sc, cmat, NN) + dot3(xs * to_end, adj, NT),
                dot3(sc.T, bmat, NN) + dot3(g_scaled, state, NT),
            ],
            axis=1,
        )
        gsact = gstates * (ssg * (1.0 + sactv * (1.0 - ssg)))
        gact = (step_wide * u + skip * g) * (sg * (1.0 + actv * (1.0 - sg)))
        u_ref[...] = gact
        sext[Q + HALO :, :] = gsact
        small_a[4:5, :] = small_a[4:5, :] + jnp.sum(gact, axis=0, keepdims=True)
        small_b[4:5, :] = small_b[4:5, :] + jnp.sum(gsact, axis=0, keepdims=True)
        direct = gather(x * u, hot)
        flow = gather(g * (y[...] - skip * x), hot) - stepv * direct
        ends_heads = gather(jnp.broadcast_to(ends, (HALO, ends.shape[1])), hot)[:1]
        da = tri_sum(False, flow) + ends_heads
        slope = (direct + rate * da) * sigmoid(step_pre[...] + params[7:8, LANES : 2 * LANES])
        gstep[Q:, :] = slope.astype(BF16)
        small_a[7:8, :LANES] = small_a[7:8, :LANES] + jnp.sum(
            stepv * rate * da, axis=0, keepdims=True
        )
        small_a[7:8, LANES : 2 * LANES] = small_a[7:8, LANES : 2 * LANES] + jnp.sum(
            slope, axis=0, keepdims=True
        )

    @pl.when(c == 0)
    def _():
        halo_send[...] = u_ref[:HALO, :]
        shalo_send[...] = sext[Q + HALO : Q + 2 * HALO, :]

        @pl.when(seq > 0)
        def _():
            halo(halo_send, halo_got, 0).start()
            halo(shalo_send, shalo_got, 2).start()

    @pl.when(c == count)
    def _():
        @pl.when(seq < ns - 1)
        def _():
            halo(halo_send, halo_got, 0).wait_recv()
            halo(shalo_send, shalo_got, 2).wait_recv()
            u_ref[:HALO, :] = halo_got[...]
            sext[Q + HALO : Q + 2 * HALO, :] = shalo_got[...]

        @pl.when(seq == ns - 1)
        def _():
            u_ref[:HALO, :] = jnp.zeros((HALO, u_ref.shape[1]), F32)
            sext[Q + HALO : Q + 2 * HALO, :] = jnp.zeros((HALO, two), F32)

        @pl.when(seq > 0)
        def _():
            halo(halo_send, halo_got, 0).wait_send()
            halo(shalo_send, shalo_got, 2).wait_send()

    @pl.when(c >= 1)
    def _():
        gext[Q:, :] = u_ref[:HALO, :]
        sext[Q : Q + HALO, :] = sext[Q + HALO : Q + 2 * HALO, :]
        pext[:HALO, :] = jnp.where(c == 1, pre_halo[...], pre_prev[...])
        pext[HALO:, :] = pre[...]
        spext[:HALO, :] = jnp.where(c == 1, spre_halo[...], spre_prev[...])
        spext[HALO:, :] = spre[...]

        def conv_back(ext, ext_pre, taps_at, size, sums):
            g = ext[:Q, :]
            total = params[taps_at + taps - 1 : taps_at + taps, :size] * g
            for k in range(taps - 1):
                start = taps - 1 - k
                total = total + params[taps_at + k : taps_at + k + 1, :size] * ext[start : start + Q, :]
            for k in range(taps):
                start = HALO - taps + 1 + k
                sums[k : k + 1, :] = sums[k : k + 1, :] + jnp.sum(
                    g * ext_pre[start : start + Q, :], axis=0, keepdims=True
                )
            return total

        inner = gext.shape[1]
        gin_o[:, :inner] = conv_back(gext, pext, 0, inner, small_a).astype(BF16)
        gin_o[:, inner:] = gstep[:Q, :]
        mine = conv_back(sext, spext, 8, two, small_b)
        psum[chunk_rows(c - 1), :] = mine

        @pl.when((c - 1) % n != me)
        def _():
            to_owner(c - 1).start()

    @pl.when((c >= 0) & (c < count))
    def _():
        gext[:Q, :] = u_ref[...]
        gstep[:Q, :] = gstep[Q:, :]
        sext[:Q, :] = sext[Q + HALO :, :]

    for g in range(groups):

        @pl.when(c == min((g + 1) * n + 2, total_chunks))
        def _():
            own = chunk_rows(g * n + me)
            total = psum[own, :]
            for k in range(1, n):
                j = (me + k) % n
                from_other(j, g).wait_recv()
                total = total + pgot[j, g * Q : (g + 1) * Q, :]
            gsb_o[own, :] = total.astype(BF16)
            for k in range(1, n):
                give(k, g, False).start()

    @pl.when(c == count)
    def _():
        for g in range(groups):
            for k in range(1, n):
                give(k, g, True).wait_recv()
        gsb_out[...] = gsb_o[...]
        for g in range(groups):
            for k in range(1, n):
                give(k, g, False).wait_send()
        for k in range(total_chunks):

            @pl.when(k % n != me)
            def _():
                to_owner(k).wait_send()

    slots, last_step = slots_of(n), count + 1
    for t in range(3, slots):

        @pl.when(i == 1 + (t - 3) * last_step // (slots - 3))
        def _():
            slot(t)

    @pl.when(i == last_step)
    def _():
        drain()
        code_out[...] = all_ref[...]


def matmul_low(left, right):
    return jnp.dot(left, right, preferred_element_type=F32)


def times_transposed(left, right):
    return dg(left, right, NT)


def transposed_times(left, right):
    return dg(left, right, TN)


def on_device(
    hidden,
    in_gain,
    proj_gate,
    proj_input,
    proj_states,
    proj_step,
    conv_input,
    conv_input_bias,
    conv_states,
    conv_states_bias,
    step_bias,
    decay_log,
    skip_gain,
    gate_gain,
    proj_output,
    cotangent,
):
    seg_count = lax.axis_size("seq")
    seg_index = lax.axis_index("seq")
    head_index = lax.axis_index("head")
    is_first = seg_index == 0
    tokens, width = hidden.shape
    heads = proj_step.shape[1]
    inner = proj_gate.shape[1]
    state_size = conv_states.shape[1] // 2
    head_dim = inner // heads
    row_width = proj_states.shape[0]
    count = tokens // Q
    gain_full = in_gain.astype(F32)

    def pad_heads(value):
        return jnp.pad(value, [(0, 0)] * (value.ndim - 1) + [(0, LANES - heads)])

    n, ns = lax.axis_size("head"), seg_count

    def turned(value, k):
        return lax.ppermute(value, "head", [(i, (i + k) % n) for i in range(n)])

    pieces = [proj_states] + [turned(proj_states, k) for k in range(1, n)]
    hidden_halo = shifted(hidden[tokens - HALO :], "seq", 1)

    def norm(rows_):
        value = rows_.astype(F32)
        inv = lax.rsqrt(jnp.mean(value * value, axis=-1, keepdims=True) + EPS)
        return inv, (value * inv * gain_full[None, :]).astype(BF16)

    inv_rms, normed = norm(hidden)
    normed_halo = norm(hidden_halo)[1]
    keep = jnp.where(is_first, 0.0, 1.0)
    proj_step_wide = pad_heads(proj_step)
    input_pre = matmul_low(normed, proj_input)
    input_halo = matmul_low(normed_halo, proj_input) * keep
    gate_pre = matmul_low(normed, proj_gate)
    grad_ynorm = times_transposed(cotangent, proj_output)
    two = 2 * state_size
    flat = jnp.concatenate(
        [
            pad_heads(decay_log),
            pad_heads(step_bias),
            pad_heads(skip_gain),
            conv_input_bias.astype(F32),
            gate_gain.astype(F32),
            conv_states_bias.astype(F32),
        ]
    )
    flat = jnp.pad(flat, (0, -flat.shape[0] % 1024))
    vec = flat.reshape(-1, LANES)
    onehot = jnp.asarray(
        np.arange(LANES)[:, None] == np.arange(inner)[None, :] // head_dim, dtype=BF16
    )
    hot = (onehot, whole((LANES, inner)))
    state_rows = pl.BlockSpec((state_size, inner), lambda c: (c, 0))
    packed_shape = (state_size + HALO, inner)
    (
        act, sact, states_pre, states_halo, step_pre, step, cum, cumt, sin, packed, total_log,
        before_log, params,
    ) = call(
        functools.partial(states_kernel, n),
        (count,),
        [
            (input_pre, rows(inner)),
            (input_pre, before(inner)),
            (input_halo, whole((HALO, inner))),
            (normed, rows(width)),
            (normed_halo, whole((HALO, width))),
            (proj_step_wide, whole((width, LANES))),
            (vec, whole(vec.shape)),
            (conv_input, whole(conv_input.shape)),
            (conv_states, whole(conv_states.shape)),
            hot,
        ]
        + [(piece, whole(piece.shape)) for piece in pieces],
        [
            (sds((tokens, inner)), rows(inner)),
            (sds((tokens, two)), rows(two)),
            (sds((tokens, two)), rows(two)),
            (sds((HALO, two)), whole((HALO, two))),
            (sds((tokens, LANES)), rows(LANES)),
            (sds((tokens, LANES)), rows(LANES)),
            (sds((tokens, LANES)), rows(LANES)),
            (sds((tokens, LANES)), rows(LANES)),
            (sds((count * state_size, inner)), state_rows),
            (sds(packed_shape), whole(packed_shape)),
            (sds((1, LANES)), whole((1, LANES))),
            (sds((count, 1, LANES)), pl.BlockSpec((None, 1, LANES), lambda c: (c, 0, 0))),
            (sds((16, inner)), whole((16, inner))),
        ],
        scratch=[
            pltpu.VMEM((Q + HALO, inner), F32),
            pltpu.VMEM((Q + HALO, two), F32),
            pltpu.VMEM((state_size, inner), F32),
            pltpu.VMEM((1, LANES), F32),
            pltpu.VMEM((width, two), BF16),
        ],
        flops=10 * tokens * inner * state_size,
    )
    par = (params, whole((16, inner)))
    packed, gate_pre, grad_ynorm = lax.optimization_barrier((packed, gate_pre, grad_ynorm))
    yloc, incoming = call(
        functools.partial(intra_kernel, ns),
        (count,),
        [
            (act, rows(inner)),
            (sact, rows(two)),
            (step, rows(LANES)),
            (cum, rows(LANES)),
            (cumt, rows(LANES)),
            par,
            hot,
            (packed, whole(packed_shape)),
        ],
        [
            (sds((tokens, inner)), rows(inner)),
            (sds((state_size, inner)), whole((state_size, inner))),
        ],
        scratch=[pltpu.VMEM((Q, inner), F32), pltpu.VMEM((state_size, inner), F32)]
        + swap_scratch(ns, (state_size, inner)),
        flops=12 * tokens * inner * Q,
        collective=5,
    )

    def both(i):
        return jnp.where(i < count, i, 2 * count - 1 - i)

    def fore(i):
        return jnp.minimum(i, count - 1)

    def aft(i):
        return jnp.minimum(2 * count - 1 - i, count - 1)

    def at(size, which, height=Q):
        return pl.BlockSpec((height, size), lambda i: (which(i), 0))

    y, ynorm, grad_gate_pre, grad_ssd, dout, packed_back, grad_rows = call(
        functools.partial(middle_kernel, n),
        (2 * count,),
        [
            (yloc, at(inner, fore)),
            (act, at(inner, aft)),
            (sact, at(two, both)),
            (cum, at(LANES, both)),
            (sin, at(inner, fore, state_size)),
            (before_log, pl.BlockSpec((None, 1, LANES), lambda i: (fore(i), 0, 0))),
            (total_log, whole((1, LANES))),
            (incoming, whole((state_size, inner))),
            (gate_pre, at(inner, both)),
            (grad_ynorm, at(inner, both)),
            par,
            hot,
        ],
        [
            (sds((tokens, inner)), at(inner, fore)),
            (sds((tokens, inner), BF16), at(inner, aft)),
            (sds((tokens, inner), BF16), at(inner, aft)),
            (sds((tokens, inner)), at(inner, aft)),
            (sds((count * state_size, inner)), at(inner, aft, state_size)),
            (sds(packed_shape), whole(packed_shape)),
            (sds((HALO, inner)), whole((HALO, inner))),
        ],
        scratch=[
            pltpu.VMEM((tokens, inner), F32),
            pltpu.VMEM((HALO, tokens), F32),
            pltpu.VMEM((n, HALO, tokens), F32),
            pltpu.VMEM((state_size, inner), F32),
            pltpu.SemaphoreType.DMA((n,)),
            pltpu.SemaphoreType.DMA((n,)),
        ],
        flops=12 * tokens * inner * state_size,
        collective=3,
    )
    local_proj_output = transposed_times(cotangent, ynorm)
    local_proj_gate = transposed_times(normed, grad_gate_pre)
    summed_out = lax.psum_scatter(
        local_proj_output, "seq", scatter_dimension=0, tiled=True
    )
    grad_proj_output = pl.pallas_call(
        turn_kernel, out_shape=sds(summed_out.shape[::-1]), name="turn"
    )(summed_out)
    grad_proj_gate = lax.psum_scatter(
        local_proj_gate, "seq", scatter_dimension=0, tiled=True
    )

    def now(i):
        return jnp.clip(i - 1, 0, count - 1)

    def past(i):
        return jnp.maximum(i - 2, 0)

    def held(size, height=Q):
        return pl.BlockSpec((height, size), lambda i: (now(i), 0))

    def prior(size):
        return pl.BlockSpec((Q, size), lambda i: (past(i), 0))

    def prior_edge(size):
        return pl.BlockSpec(
            (HALO, size), lambda i: (jnp.maximum(past(i) * (Q // HALO) - 1, 0), 0)
        )

    def once(shape):
        return pl.BlockSpec(shape, lambda i: (0, 0), pipeline_mode=pl.Buffered(1))

    dma = pltpu.SemaphoreType.DMA
    groups = count // n
    grad_in_b, grad_states_b, small_a, small_b, branch_code = call(
        functools.partial(back_kernel, n, ns),
        (count + 2,),
        [
            (act, held(inner)),
            (sact, held(two)),
            (y, held(inner)),
            (grad_ssd, held(inner)),
            (step, held(LANES)),
            (step_pre, held(LANES)),
            (cum, held(LANES)),
            (cumt, held(LANES)),
            (sin, held(inner, state_size)),
            (dout, held(inner, state_size)),
            (
                before_log,
                pl.BlockSpec((None, 1, LANES), lambda i: (now(i), 0, 0)),
            ),
            (total_log, whole((1, LANES))),
            (incoming, once((state_size, inner))),
            (ynorm, once((tokens, inner))),
            (proj_output, once((inner, width))),
            (packed_back, once(packed_shape)),
            par,
            hot,
            (grad_rows, whole((HALO, inner))),
            (input_pre, prior(inner)),
            (input_pre, prior_edge(inner)),
            (input_halo, whole((HALO, inner))),
            (states_pre, prior(two)),
            (states_pre, prior_edge(two)),
            (states_halo, whole((HALO, two))),
        ],
        [
            (sds((tokens, inner + LANES), BF16), prior(inner + LANES)),
            (sds((tokens, two), BF16), whole((tokens, two))),
            (sds((16, inner)), whole((16, inner))),
            (sds((HALO, two)), whole((HALO, two))),
            (sds((tokens, width + LANES), BF16), once((tokens, width + LANES))),
        ],
        scratch=[
            pltpu.VMEM((tokens, two), BF16),
            pltpu.VMEM((2 * Q, LANES), BF16),
            pltpu.VMEM((Q, inner), F32),
            pltpu.VMEM((Q, inner), F32),
            pltpu.VMEM((Q, Q), F32),
            pltpu.VMEM((Q + HALO, inner), F32),
            pltpu.VMEM((2 * Q + HALO, two), F32),
            pltpu.VMEM((Q + HALO, inner), F32),
            pltpu.VMEM((Q + HALO, two), F32),
            pltpu.VMEM((HALO, inner), F32),
            pltpu.VMEM((HALO, inner), F32),
            pltpu.VMEM((HALO, two), F32),
            pltpu.VMEM((HALO, two), F32),
            pltpu.VMEM((tokens, two), F32),
            pltpu.VMEM((n, groups * Q, two), F32),
            dma((4,)),
            dma((count,)),
            dma((n, groups)),
            dma((n, groups)),
            dma((n, groups)),
            pltpu.VMEM((state_size, inner), F32),
            *swap_scratch(ns, (state_size, inner)),
            pltpu.VMEM((tokens, width + LANES), BF16),
            *chain_scratch(tokens, width, n),
        ],
        flops=40 * tokens * inner * Q,
        collective=4,
    )
    result = call(
        result_kernel,
        (count,),
        [(branch_code, rows(width + LANES)), (hidden, rows(width))],
        [(sds((tokens, width)), rows(width))],
        flops=20 * tokens * width,
    )[0]
    row_start = head_index * row_width
    own_states = lax.dynamic_update_slice_in_dim(
        jnp.zeros((width, two), BF16), proj_states, row_start, 0
    )
    normed_rows = lax.dynamic_slice_in_dim(normed, row_start, row_width, 1)
    local_proj_in = transposed_times(normed, grad_in_b)
    local_proj_states = transposed_times(grad_states_b, normed_rows)
    summed_in = lax.psum_scatter(local_proj_in, "seq", scatter_dimension=0, tiled=True)
    grad_code, sum_a, sum_b, grad_proj_states = reduce_over_heads(
        [
            (grad_gate_pre, proj_gate),
            (grad_in_b, proj_input),
            (grad_in_b, proj_step_wide),
            (grad_states_b, own_states),
        ],
        [NT] * 4,
        (None, (0, inner), (inner, inner + LANES), None),
        2,
        (hidden, inv_rms, small_a, small_b, local_proj_states),
    )
    grad_hidden = call(
        hidden_kernel,
        (count,),
        [
            (grad_code, rows(width + LANES)),
            (hidden, rows(width)),
            (cotangent, rows(width)),
            (inv_rms, rows(1)),
            (gain_full[None, :], whole((1, width))),
        ],
        [(sds((tokens, width)), rows(width))],
        flops=20 * tokens * width,
    )[0]
    return (
        result,
        grad_hidden,
        sum_b[0],
        grad_proj_gate,
        summed_in[:, :inner],
        grad_proj_states.T,
        summed_in[:, inner : inner + heads],
        sum_a[:TAPS],
        sum_a[4],
        sum_b[8 : 8 + TAPS, :two],
        sum_b[12, :two],
        sum_a[7, LANES : LANES + heads],
        sum_a[7, :heads],
        jnp.sum(sum_a[6].reshape(heads, head_dim), axis=1),
        sum_a[5],
        grad_proj_output,
    )


def solution(mesh):
    in_specs = (
        P("seq", None),
        P(),
        P(None, "head"),
        P(None, "head"),
        P("head", None),
        P(None, "head"),
        P(None, "head"),
        P("head"),
        P(),
        P(),
        P("head"),
        P("head"),
        P("head"),
        P("head"),
        P("head", None),
        P("seq", None),
    )
    out_specs = (
        P("seq", None),
        P("seq", None),
        P(),
        P("seq", "head"),
        P("seq", "head"),
        P("head", "seq"),
        P("seq", "head"),
        P(None, "head"),
        P("head"),
        P(),
        P(),
        P("head"),
        P("head"),
        P("head"),
        P("head"),
        P("head", "seq"),
    )

    return jax.shard_map(
        on_device, mesh=mesh, in_specs=in_specs, out_specs=out_specs, check_vma=False
    )
```

```python
import functools

import jax
import jax.numpy as jnp
import numpy as np
from jax import lax
from jax.experimental import pallas as pl
from jax.experimental.pallas import tpu as pltpu
from jax.sharding import PartitionSpec as P


DI = 3072
EPS = 1e-05
Q = 128
LANES = 128
HALO = 8
TAPS = 4
GROUP = 2

F32 = jnp.float32
BF16 = jnp.bfloat16
NN = (((1,), (0,)), ((), ()))
NT = (((1,), (1,)), ((), ()))
TN = (((0,), (0,)), ((), ()))
VMEM_LIMIT = 60 * 1024 * 1024
MESH_ID = pl.DeviceIdType.MESH


def dg(left, right, dims):
    return lax.dot_general(left, right, dims, preferred_element_type=F32)


def split(value):
    high = value.astype(BF16)
    return high, (value - high.astype(F32)).astype(BF16)


def dot3(left, right, dims):
    (lh, ll), (rh, rl) = split(left), split(right)
    return dg(lh, rh, dims) + (dg(lh, rl, dims) + dg(ll, rh, dims))


def spread(heads, onehot):
    high, low = split(heads)
    return dg(high, onehot, NN) + dg(low, onehot, NN)


def gather(wide, onehot):
    high, low = split(wide)
    return dg(high, onehot, NT) + dg(low, onehot, NT)


def sigmoid(value):
    return 0.5 * jnp.tanh(0.5 * value) + 0.5


def silu(value):
    return value * sigmoid(value)


def call(kernel, grid, ins, outs, scratch=(), flops=0, collective=None):
    in_specs = [spec for _, spec in ins]
    size = sum(a.size * a.dtype.itemsize for a, _ in ins) + sum(
        s.size * s.dtype.itemsize for s, _ in outs
    )
    return pl.pallas_call(
        kernel,
        grid=grid,
        in_specs=in_specs,
        out_specs=[spec for _, spec in outs],
        out_shape=[shape for shape, _ in outs],
        scratch_shapes=list(scratch),
        cost_estimate=pl.CostEstimate(flops=flops, bytes_accessed=size, transcendentals=0),
        compiler_params=pltpu.CompilerParams(vmem_limit_bytes=VMEM_LIMIT)
        if collective is None
        else pltpu.CompilerParams(
            vmem_limit_bytes=VMEM_LIMIT, collective_id=collective, has_side_effects=True
        ),
    )(*[a for a, _ in ins])


def sds(shape, dtype=F32):
    return jax.ShapeDtypeStruct(shape, dtype)


def rows(width, height=Q):
    return pl.BlockSpec((height, width), lambda c: (c, 0))


def whole(shape):
    return pl.BlockSpec(shape, lambda c: (0,) * len(shape))


def before(width, height):
    return pl.BlockSpec((HALO, width), lambda c: (jnp.maximum(c * (height // HALO) - 1, 0), 0))


def triangle(lower):
    a = lax.broadcasted_iota(jnp.int32, (Q, Q), 0)
    b = lax.broadcasted_iota(jnp.int32, (Q, Q), 1)
    return a >= b if lower else a <= b


def tri_sum(lower, value):
    mask = triangle(lower).astype(BF16)
    high = value.astype(BF16)
    rest = value - high.astype(F32)
    mid = rest.astype(BF16)
    low = (rest - mid.astype(F32)).astype(BF16)
    return dg(mask, high, NN) + (dg(mask, mid, NN) + dg(mask, low, NN))


def conv_act(pre, ext_ref, params, at):
    size = ext_ref.shape[1]
    height = pre.shape[0]
    ext_ref[HALO:, :] = pre
    total = params[at + TAPS : at + TAPS + 1, :size] + params[at + TAPS - 1 : at + TAPS, :size] * pre
    for k in range(TAPS - 1):
        start = HALO - TAPS + 1 + k
        total = total + params[at + k : at + k + 1, :size] * ext_ref[start : start + height, :]
    return total


def front_kernel(
    n, ns, hidden, cotangent, tail, gain, proj_input, proj_gate, proj_output, piece,
    normed_o, inv_o, pre_o, gate_o, gyn_o, full_o, nhalo_o, halo_o,
    full, halo, s_sem, r_sem, h_sem,
):
    c = pl.program_id(0)
    me, seq = lax.axis_index("head"), lax.axis_index("seq")
    height = piece.shape[0]

    def slab(j):
        return pl.ds(pl.multiple_of(j * height, height), height)

    def give(k, arriving):
        other = (me + k) % n
        owner = other if arriving else me
        return pltpu.make_async_remote_copy(
            src_ref=piece,
            dst_ref=full.at[slab(owner)],
            send_sem=s_sem.at[k],
            recv_sem=r_sem.at[owner],
            device_id={"head": other},
            device_id_type=MESH_ID,
        )

    def edge():
        return pltpu.make_async_remote_copy(
            src_ref=tail,
            dst_ref=halo,
            send_sem=h_sem.at[0],
            recv_sem=h_sem.at[1],
            device_id={"seq": (seq + 1) % ns},
            device_id_type=MESH_ID,
        )

    def norm(value):
        value = value.astype(F32)
        inv = lax.rsqrt(jnp.mean(value * value, axis=-1, keepdims=True) + EPS)
        return inv, (value * inv * gain[...]).astype(BF16)

    @pl.when(c == 0)
    def _():
        barrier = greet(n, ns)
        pl.semaphore_wait(barrier, n + ns - 2)
        for k in range(1, n):
            give(k, False).start()

        @pl.when(seq < ns - 1)
        def _():
            edge().start()

        full[slab(me), :] = piece[...]

    inv, normed = norm(hidden[...])
    inv_o[...] = inv
    normed_o[...] = normed
    pre_o[...] = dg(normed, proj_input[...], NN)
    gate_o[...] = dg(normed, proj_gate[...], NN)
    gyn_o[...] = dg(cotangent[...], proj_output[...], NT)

    @pl.when(c == pl.num_programs(0) - 1)
    def _():
        @pl.when(seq > 0)
        def _():
            edge().wait_recv()

        @pl.when(seq == 0)
        def _():
            halo[...] = jnp.zeros_like(halo)

        before_first = norm(halo[...])[1]
        nhalo_o[...] = before_first
        halo_o[...] = dg(before_first, proj_input[...], NN)[16 - HALO :, :]

        @pl.when(seq < ns - 1)
        def _():
            edge().wait_send()

        for k in range(1, n):
            give(k, True).wait_recv()
        full_o[...] = full[...]
        for k in range(1, n):
            give(k, False).wait_send()


def states_kernel(
    pre, pre_prev, pre_halo, normed, normed_halo, step_w, vec, taps_in, taps_st, full, onehot, *refs
):
    act_o, sact_o, spre_o, shalo_o, spre_step_o, step_o, cum_o, cumt_o, sin_o, dev_o, total_o = refs[:11]
    before_o, params = refs[11:13]
    ext, sext, state, total = refs[13:]
    c = pl.program_id(0)
    state_size = bmat_width(sact_o)
    inner = pre.shape[1]
    two = 2 * state_size
    hot = onehot[...]

    def line(first, size):
        return jnp.concatenate([vec[r : r + 1, :] for r in range(first, first + size // LANES)], axis=1)

    height = pre.shape[0]

    @pl.when(c == 0)
    def _():
        state[...] = jnp.zeros_like(state)
        total[...] = jnp.zeros_like(total)
        params[...] = jnp.zeros_like(params)
        per = inner // LANES
        params[0:TAPS, :] = taps_in[...].astype(F32)
        params[4:5, :] = line(3, inner)
        params[5:6, :] = line(3 + per, inner)
        params[6:7, :] = spread(jnp.broadcast_to(vec[2:3, :], (HALO, LANES)), hot)[:1]
        params[7:8, :LANES] = -jnp.exp(vec[0:1, :])
        params[7:8, LANES : 2 * LANES] = vec[1:2, :]
        params[8 : 8 + TAPS, :two] = taps_st[...].astype(F32)
        params[12:13, :two] = line(3 + 2 * per, two)
        shalo_o[...] = dg(normed_halo[...], full[...], NN)[16 - HALO :, :]
        sext[height:, :] = shalo_o[...]
        ext[:HALO, :] = pre_halo[...]

    @pl.when(c > 0)
    def _():
        ext[:HALO, :] = pre_prev[...]

    sext[:HALO, :] = sext[height:, :]
    spre = dg(normed[...], full[...], NN)
    spre_o[...] = spre
    step_pre = dg(normed[...], step_w[...], NN)
    spre_step_o[...] = step_pre
    act = conv_act(pre[...], ext, params, 0)
    sact = conv_act(spre, sext, params, 8)
    act_o[...] = act
    sact_o[...] = sact
    step = jax.nn.softplus(step_pre + params[7:8, LANES : 2 * LANES])
    step_o[...] = step
    x = silu(act)
    bmat_all = silu(sact[:, :state_size])
    for j in range(height // Q):
        part = slice(j * Q, (j + 1) * Q)
        cum = tri_sum(True, step[part] * params[7:8, :LANES])
        cum_o[part, :] = cum
        cumt_o[part, :] = cum.T
        last = cum[Q - 1 :, :]
        xw = x[part] * spread(step[part] * jnp.exp(last - cum), hot)
        sin_o[j * state_size : (j + 1) * state_size, :] = state[...]
        before_o[j] = total[...]
        decay = spread(jnp.broadcast_to(jnp.exp(last), (HALO, LANES)), hot)[:1]
        state[...] = state[...] * decay + dot3(bmat_all[part], xw, TN)
        total[...] = total[...] + last
    dev_o[...] = state[...]
    total_o[...] = jnp.broadcast_to(total[...], (HALO, LANES))


def bmat_width(ref):
    return ref.shape[1] // 2


def pair_stack(value):
    high, low = split(value)
    return jnp.concatenate(
        [
            jnp.concatenate([high, low], axis=1),
            jnp.concatenate([high, jnp.zeros_like(high)], axis=1),
        ],
        axis=0,
    )


def intra_kernel(
    ns, act, sact, step, cum, cumt, params, onehot, packed, logs, out, incoming,
    xs_ref, entered, got_s, got_d, prefix, sems,
):
    c = pl.program_id(0)
    count = pl.num_programs(0)
    seq = lax.axis_index("seq")
    begin, turn, end = swap_states(
        ns, packed, logs, onehot, entered, got_s, got_d, prefix, sems, False
    )
    barrier = pltpu.get_barrier_semaphore()

    @pl.when(c == 0)
    def _():
        for k in range(1, ns):
            pl.semaphore_signal(
                barrier, inc=1, device_id={"seq": (seq + k) % ns}, device_id_type=MESH_ID
            )
        pl.semaphore_wait(barrier, ns - 1)
        begin()

    state_size = bmat_width(sact)
    x = silu(act[...])
    xs_ref[...] = x * spread(step[...], onehot[...])
    out[...] = x * params[6:7, :]

    @pl.loop(0, act.shape[0] // Q)
    def _(chunk):
        here = pl.ds(pl.multiple_of(chunk * Q, Q), Q)
        sconv = silu(sact[here, :])
        bmat, cmat = sconv[:, :state_size], sconv[:, state_size:]
        scores = dot3(cmat, bmat, NT)
        causal = triangle(True)
        lane = lax.broadcasted_iota(jnp.int32, (Q, LANES), 1)
        sums, turned = cum.at[here], cumt.at[here]
        for p in range(act.shape[1] // LANES):
            cols = slice(p * LANES, (p + 1) * LANES)
            right = pair_stack(xs_ref[here, cols])
            got = []
            for j in range(2):
                h = p * 2 + j
                gap = sums[:, h : h + 1] - turned[h : h + 1, :]
                mixing = scores * jnp.exp(jnp.where(causal, gap, -1e30))
                wide = dg(jnp.concatenate(split(mixing), axis=1), right, NN)
                got.append(wide[:, :LANES] + wide[:, LANES:])
            out[here, cols] = out[here, cols] + jnp.where(lane < LANES // 2, got[0], got[1])

    @pl.when(c == count // 2)
    def _():
        turn()

    @pl.when(c == count - 1)
    def _():
        end()
        incoming[...] = entered[...]


STREAMS = 8
SPAN = 83.0


def encode(value):
    top = jnp.max(jnp.abs(value), axis=1, keepdims=True)
    scale = (top * 1.004 + 1e-30).astype(BF16)
    code = jnp.exp(value * (SPAN / scale.astype(F32))).astype(BF16)
    return code, jnp.broadcast_to(scale, (value.shape[0], LANES))


def decode(block, width):
    scale = block[:, width : width + 1].astype(F32) * (1.0 / SPAN)
    return jnp.log(block[:, :width].astype(F32)) * scale


def swap_states(ns, packed, logs, onehot, out, got_s, got_d, prefix, sems, reverse):
    seq = lax.axis_index("seq")
    own = out.shape[0] // ns

    def rows_of(j):
        return pl.ds(pl.multiple_of(j * own, own), own)

    def remote(src, dst, send, recv, to):
        return pltpu.make_async_remote_copy(
            src_ref=src,
            dst_ref=dst,
            send_sem=send,
            recv_sem=recv,
            device_id={"seq": to},
            device_id_type=MESH_ID,
        )

    def copies(k, arriving):
        other = (seq + k) % ns
        slot = other if arriving else seq
        part = packed.at[rows_of(other)]
        return (
            remote(part, got_s.at[slot], sems.at[0, k], sems.at[1, slot], other),
            remote(logs, got_d.at[slot], sems.at[2, k], sems.at[3, slot], other),
        )

    def answer(k, arriving):
        other = (seq + k) % ns
        slot = other if arriving else seq
        return remote(
            prefix.at[other], out.at[rows_of(slot)], sems.at[4, k], sems.at[5, slot], other
        )

    def begin():
        for k in range(1, ns):
            for copy in copies(k, False):
                copy.start()

    def turn():
        got_s[seq] = packed[rows_of(seq), :]
        got_d[seq] = logs[...]
        for k in range(1, ns):
            for copy in copies(k, True):
                copy.wait_recv()
        carry = jnp.zeros((own, out.shape[1]), F32)
        for i in reversed(range(ns)) if reverse else range(ns):
            prefix[i] = carry
            carry = carry * spread(jnp.exp(got_d[i]), onehot[...])[:1] + got_s[i]
        for k in range(1, ns):
            answer(k, False).start()
        out[rows_of(seq), :] = prefix[seq]

    def end():
        for k in range(1, ns):
            answer(k, True).wait_recv()
        for k in range(1, ns):
            answer(k, False).wait_send()
            for copy in copies(k, False):
                copy.wait_send()

    return begin, turn, end


def swap_scratch(ns, shape):
    own = shape[0] // ns
    return [
        pltpu.VMEM((ns, own, shape[1]), F32),
        pltpu.VMEM((ns, HALO, LANES), F32),
        pltpu.VMEM((ns, own, shape[1]), F32),
        pltpu.SemaphoreType.DMA((6, ns)),
    ]


def put(ref, where, value):
    code, scale = encode(value)
    width = value.shape[1]
    ref[where, :width] = code
    ref[where, width:] = scale


def chain_scratch(tokens, width, n):
    coded = pltpu.VMEM((tokens, width + LANES), BF16)
    return [pltpu.VMEM((tokens, width), F32), coded, coded, coded] + [
        pltpu.SemaphoreType.DMA((STREAMS, n))
    ] * 6


def chains(n, all_ref, part, code, got_r, got_l, s_sem, rr_sem, rl_sem, ar_sem, al_sem, ag_sem):
    me = lax.axis_index("head")
    tokens, width = part.shape
    span = tokens // STREAMS
    rows_own = span // n
    has_right, has_left = me < n - 1, me > 0

    def at(d, h):
        return pl.ds(pl.multiple_of(h * span + d * rows_own, rows_own), rows_own)

    def step(d, h, right):
        return pltpu.make_async_remote_copy(
            src_ref=code.at[at(d, h)],
            dst_ref=(got_r if right else got_l).at[at(d, h)],
            send_sem=s_sem.at[h, d],
            recv_sem=(rr_sem if right else rl_sem).at[h, d],
            device_id={"head": me + 1 if right else me - 1},
            device_id_type=MESH_ID,
        )

    def hand_on(b, h, right):
        return pltpu.make_async_remote_copy(
            src_ref=all_ref.at[at(b, h)],
            dst_ref=all_ref.at[at(b, h)],
            send_sem=(ar_sem if right else al_sem).at[h, b],
            recv_sem=ag_sem.at[h, b],
            device_id={"head": me + 1 if right else me - 1},
            device_id_type=MESH_ID,
        )

    def chain(h, u):
        for right in (True, False):
            d = me + (n - 1 - u) if right else me - (n - 1 - u)
            got = got_r if right else got_l
            inside = d <= n - 1 if right else d >= 0
            fed = has_left if right else has_right

            @pl.when(inside & fed)
            def _():
                step(d, h, right).wait_recv()
                put(code, at(d, h), part[at(d, h), :] + decode(got[at(d, h), :], width))
                step(d, h, right).start()

            @pl.when(inside & jnp.logical_not(fed))
            def _():
                put(code, at(d, h), part[at(d, h), :])
                step(d, h, right).start()

    def finish(h):
        own = at(me, h)

        @pl.when(has_left)
        def _():
            step(me, h, True).wait_recv()
            part[own, :] = part[own, :] + decode(got_r[own, :], width)

        @pl.when(has_right)
        def _():
            step(me, h, False).wait_recv()
            part[own, :] = part[own, :] + decode(got_l[own, :], width)

        put(all_ref, own, part[own, :])

        @pl.when(has_right)
        def _():
            hand_on(me, h, True).start()

        @pl.when(has_left)
        def _():
            hand_on(me, h, False).start()

    def relay(h, s):
        @pl.when(me - s >= 0)
        def _():
            hand_on(me - s, h, True).wait_recv()

            @pl.when(has_right)
            def _():
                hand_on(me - s, h, True).start()

        @pl.when(me + s < n)
        def _():
            hand_on(me + s, h, False).wait_recv()

            @pl.when(has_left)
            def _():
                hand_on(me + s, h, False).start()

    def slot(t):
        for u in range(2 * n - 2, -1, -1):
            h = t - u

            @pl.when((h >= 0) & (h < STREAMS))
            def _():
                if u < n - 1:
                    chain(h, u)
                elif u == n - 1:
                    finish(h)
                else:
                    relay(h, u - n + 1)

    def drain():
        @pl.loop(0, STREAMS)
        def _(h):
            for i in range(n):

                @pl.when(i > me)
                def _():
                    step(i, h, True).wait_send()

                @pl.when(i < me)
                def _():
                    step(i, h, False).wait_send()

                @pl.when(has_right & (i <= me))
                def _():
                    hand_on(i, h, True).wait_send()

                @pl.when(has_left & (i >= me))
                def _():
                    hand_on(i, h, False).wait_send()

    return slot, drain


def slots_of(n):
    return STREAMS - 1 + 2 * n - 1


def greet(n, ns):
    barrier = pltpu.get_barrier_semaphore()
    me, seq = lax.axis_index("head"), lax.axis_index("seq")
    for k in range(1, n):
        pl.semaphore_signal(
            barrier, inc=1, device_id={"head": (me + k) % n}, device_id_type=MESH_ID
        )
    for k in range(1, ns):
        pl.semaphore_signal(
            barrier, inc=1, device_id={"seq": (seq + k) % ns}, device_id_type=MESH_ID
        )
    return barrier


def reduce_kernel(n, ns, dims, cols, *refs):
    terms = len(dims)
    lefts, rights = refs[:terms], refs[terms : 2 * terms]
    refs = refs[2 * terms :]
    hidden_ref, inv_ref, small_a, small_b, states_ref, out_ref, sum_a, sum_b, sum_s = refs[:9]
    slot, drain = chains(n, out_ref, *refs[9:19])
    part = refs[9]
    got_a, got_b, got_s, got_c, mine_b = refs[19:24]
    sa_sem, ra_sem, sb_sem, rb_sem, ss_sem, rs_sem, sc_sem, rc_sem = refs[24:]
    me, seq = lax.axis_index("head"), lax.axis_index("seq")
    tokens, _ = part.shape
    span = tokens // STREAMS
    barrier = greet(n, ns)

    def to_seq(src, dst, ssem, rsem, k):
        return pltpu.make_async_remote_copy(
            src_ref=src,
            dst_ref=dst.at[seq],
            send_sem=ssem.at[k],
            recv_sem=rsem.at[seq],
            device_id={"seq": (seq + k) % ns},
            device_id_type=MESH_ID,
        )

    def from_seq(src, dst, ssem, rsem, k):
        other = (seq + k) % ns
        return pltpu.make_async_remote_copy(
            src_ref=src,
            dst_ref=dst.at[other],
            send_sem=ssem.at[k],
            recv_sem=rsem.at[other],
            device_id={"seq": other},
            device_id_type=MESH_ID,
        )

    def states_at(j):
        own = sum_s.shape[0]
        return states_ref.at[pl.ds(pl.multiple_of(j * own, own), own)]

    def compute(h):
        where = pl.ds(pl.multiple_of(h * span, span), span)
        total = None
        for left, right, dim, col in zip(lefts, rights, dims, cols):
            value = left[where, :] if col is None else left[where, col[0] : col[1]]
            term = dg(value, right[...], dim)
            total = term if total is None else total + term
        part[where, :] = total
        seen = total * (hidden_ref[where, :].astype(F32) * inv_ref[where, :])
        mine_b[0:1, :] = mine_b[0:1, :] + jnp.sum(seen, axis=0, keepdims=True)

    mine_b[...] = jnp.zeros_like(mine_b)
    mine_b[8:16, : small_b.shape[1]] = small_b[...]
    compute(0)
    pl.semaphore_wait(barrier, n + ns - 2)
    for k in range(1, ns):
        to_seq(small_a, got_a, sa_sem, ra_sem, k).start()
        to_seq(states_at((seq + k) % ns), got_s, ss_sem, rs_sem, k).start()

    @pl.loop(0, STREAMS - 1)
    def _(t):
        slot(t)
        compute(t + 1)

    for k in range(1, ns):
        to_seq(mine_b, got_b, sb_sem, rb_sem, k).start()

    @pl.loop(STREAMS - 1, slots_of(n) - 2)
    def _(t):
        slot(t)

    total = small_a[...]
    for k in range(1, ns):
        from_seq(small_a, got_a, sa_sem, ra_sem, k).wait_recv()
        total = total + got_a[(seq + k) % ns]
    sum_a[...] = total
    total = states_at(seq)[...]
    for k in range(1, ns):
        from_seq(states_at(seq), got_s, ss_sem, rs_sem, k).wait_recv()
        total = total + got_s[(seq + k) % ns]
    sum_s[...] = total
    total = mine_b[...]
    for k in range(1, ns):
        from_seq(mine_b, got_b, sb_sem, rb_sem, k).wait_recv()
        total = total + got_b[(seq + k) % ns]
    sum_b[...] = total

    def to_head(k):
        return pltpu.make_async_remote_copy(
            src_ref=sum_b,
            dst_ref=got_c.at[me],
            send_sem=sc_sem.at[k],
            recv_sem=rc_sem.at[me],
            device_id={"head": (me + k) % n},
            device_id_type=MESH_ID,
        )

    def from_head(k):
        other = (me + k) % n
        return pltpu.make_async_remote_copy(
            src_ref=sum_b,
            dst_ref=got_c.at[other],
            send_sem=sc_sem.at[k],
            recv_sem=rc_sem.at[other],
            device_id={"head": other},
            device_id_type=MESH_ID,
        )

    for k in range(1, n):
        to_head(k).start()

    @pl.loop(slots_of(n) - 2, slots_of(n))
    def _(t):
        slot(t)

    total = sum_b[...]
    for k in range(1, n):
        from_head(k).wait_recv()
    for k in range(1, n):
        to_head(k).wait_send()
        total = total + got_c[(me + k) % n]
    sum_b[...] = total
    for k in range(1, ns):
        to_seq(small_a, got_a, sa_sem, ra_sem, k).wait_send()
        to_seq(states_at((seq + k) % ns), got_s, ss_sem, rs_sem, k).wait_send()
        to_seq(mine_b, got_b, sb_sem, rb_sem, k).wait_send()
    drain()


def reduce_over_heads(products, dims, cols, collective, sums):
    n, ns = lax.axis_size("head"), lax.axis_size("seq")
    tokens, width = sums[0].shape
    lefts, rights = [a for a, _ in products], [b for _, b in products]
    dma = pltpu.SemaphoreType.DMA
    small_a = sums[2].shape
    states = (sums[4].shape[0] // ns, sums[4].shape[1])
    out_shape = [sds((tokens, width + LANES), BF16), sds(small_a), sds((16, width)), sds(states)]
    scratch = chain_scratch(tokens, width, n) + [
        pltpu.VMEM((ns, *small_a), F32),
        pltpu.VMEM((ns, 16, width), F32),
        pltpu.VMEM((ns, *states), F32),
        pltpu.VMEM((n, 16, width), F32),
        pltpu.VMEM((16, width), F32),
    ]
    scratch += [dma((ns,))] * 6 + [dma((n,))] * 2
    vmem = pl.BlockSpec(memory_space=pltpu.VMEM)
    return pl.pallas_call(
        functools.partial(reduce_kernel, n, ns, dims, cols),
        in_specs=[vmem] * (len(lefts) + len(rights) + len(sums)),
        out_specs=[vmem] * len(out_shape),
        out_shape=out_shape,
        scratch_shapes=scratch,
        compiler_params=pltpu.CompilerParams(
            collective_id=collective, has_side_effects=True, vmem_limit_bytes=VMEM_LIMIT
        ),
        cost_estimate=pl.CostEstimate(
            flops=2 * tokens * width * sum(a.shape[1] for a in lefts),
            bytes_accessed=100 * tokens * width,
            transcendentals=0,
        ),
        name="reduce_heads",
    )(*lefts, *rights, *sums)


def turn_kernel(value, out):
    high = value.shape[0]
    more = jnp.zeros((-high % LANES, value.shape[1]), F32)
    out[...] = jnp.concatenate([value[...], more], axis=0).T[:, :high]


def finish_kernel(branch, code, hidden, cotangent, inv, gain, result, out):
    width = out.shape[1]
    resid = hidden[...].astype(F32)
    result[...] = resid + decode(branch[...], width)
    grad = decode(code[...], width) * gain[...]
    scale = inv[...]
    dots = jnp.sum(grad * resid, axis=1, keepdims=True) * (1.0 / width)
    out[...] = (
        cotangent[...].astype(F32) + scale * grad - resid * (scale * scale * scale * dots)
    )


def rows_of_sums(square, cross):
    first = jnp.sum(square, axis=1, keepdims=True)
    second = jnp.sum(cross, axis=1, keepdims=True)
    lane = lax.broadcasted_iota(jnp.int32, (square.shape[0], LANES), 1)
    columns = jnp.where(lane == 0, first, jnp.where(lane == 1, second, 0.0))
    parts = [columns[r : r + Q].T[:HALO] for r in range(0, square.shape[0], Q)]
    return jnp.concatenate(parts, axis=1)


def middle_kernel(
    n, yloc, act, sact, cum, sin, before_log, incoming, gate, gyn, params, onehot,
    y_o, ynorm_o, gpre_o, gssd_o, dout_o, dev_o, rows_o,
    keep, mine, got, adj, ssem, rsem,
):
    i = pl.program_id(0)
    count = pl.num_programs(0) // 2
    c = jnp.where(i < count, i, 2 * count - 1 - i)
    me = lax.axis_index("head")
    state_size = bmat_width(sact)
    hot = onehot[...]
    gain = params[5:6, :]
    height = gate.shape[0]
    where = pl.ds(pl.multiple_of(c * height, height), height)
    barrier = pltpu.get_barrier_semaphore()

    def copy(k, arriving):
        other = (me + k) % n
        return pltpu.make_async_remote_copy(
            src_ref=mine,
            dst_ref=got.at[other if arriving else me],
            send_sem=ssem.at[k],
            recv_sem=rsem.at[other if arriving else me],
            device_id={"head": other},
            device_id_type=MESH_ID,
        )

    @pl.when(i == 0)
    def _():
        for k in range(1, n):
            pl.semaphore_signal(
                barrier, inc=1, device_id={"head": (me + k) % n}, device_id_type=MESH_ID
            )

    cmat = silu(sact[:, state_size:])
    gv = gate[...]
    sg = sigmoid(gv)
    gsilu = gv * sg
    growth = spread(jnp.exp(cum[...]), hot)

    @pl.when(i < count)
    def _():
        ahead = []
        for j in range(height // Q):
            part = slice(j * Q, (j + 1) * Q)
            carry = spread(jnp.broadcast_to(jnp.exp(before_log[j]), (HALO, LANES)), hot)[:1]
            state = sin[j * state_size : (j + 1) * state_size, :] + carry * incoming[...]
            ahead.append(dot3(cmat[part], state, NN))
        y = yloc[...] + growth * jnp.concatenate(ahead, axis=0)
        y_o[...] = y
        keep[where, :] = y
        gated = y * gsilu
        mine[:, where] = rows_of_sums(gated * gated, gyn[...] * gain * gated)

    @pl.when(i == count - 1)
    def _():
        pl.semaphore_wait(barrier, n - 1)
        for k in range(1, n):
            copy(k, False).start()

    @pl.when(i == count)
    def _():
        adj[...] = jnp.zeros_like(adj)
        rows_o[...] = jnp.zeros_like(rows_o)
        total = mine[...]
        for k in range(1, n):
            copy(k, True).wait_recv()
        for k in range(1, n):
            copy(k, False).wait_send()
            total = total + got[(me + k) % n]
        mine[...] = total

    @pl.when(i >= count)
    def _():
        total = mine[:, where]
        blank = jnp.zeros((Q - HALO, Q), F32)
        columns = jnp.concatenate(
            [
                jnp.concatenate([total[:, r : r + Q], blank], axis=0).T
                for r in range(0, height, Q)
            ],
            axis=0,
        )
        inv = lax.rsqrt(columns[:, 0:1] / DI + EPS)
        cross = columns[:, 1:2] / DI
        yv = keep[where, :]
        gated = yv * gsilu
        normed = gated * inv
        ynorm_o[...] = (normed * gain).astype(BF16)
        rows_o[0:1, :] = rows_o[0:1, :] + jnp.sum(gyn[...] * normed, axis=0, keepdims=True)
        ggated = inv * (gyn[...] * gain) - normed * (inv * inv * cross)
        gpre_o[...] = (ggated * yv * sg * (1.0 + gv * (1.0 - sg))).astype(BF16)
        gssd = ggated * gsilu
        gssd_o[...] = gssd
        rows_o[1:2, :] = rows_o[1:2, :] + jnp.sum(gssd * silu(act[...]), axis=0, keepdims=True)
        scaled = gssd * growth
        for j in reversed(range(height // Q)):
            part = slice(j * Q, (j + 1) * Q)
            dout_o[j * state_size : (j + 1) * state_size, :] = adj[...]
            last = cum[(j + 1) * Q - 1 : (j + 1) * Q, :]
            decay = spread(jnp.broadcast_to(jnp.exp(last), (HALO, LANES)), hot)[:1]
            adj[...] = adj[...] * decay + dot3(cmat[part], scaled[part], TN)

    @pl.when(i == 2 * count - 1)
    def _():
        dev_o[...] = adj[...]


def back_kernel(
    n, ns, act, sact, y, gssd, step, step_pre, cum, cumt, sin, dout, before_log, total_log, incoming,
    ynorm, proj_output, packed, normed,
    params, onehot, rows_in, pre, pre_prev, pre_halo, spre, spre_prev, spre_halo,
    gin_o, gsb_out, small_a, small_b, code_out, win_o,
    gin_all, gsb_o, gstep, xs_ref, u_ref, st_ref, gext, sext, pext, spext, halo_send, halo_got, shalo_send, shalo_got,
    psum, psend, pgot, h_sem, p_send, p_recv, g_send, g_recv,
    later, got_states, got_decays, prefix, swap_sems, all_ref, part, *chain_refs,
):
    i = pl.program_id(0)
    c = i - 1
    count = pl.num_programs(0) - 2
    total_chunks = psum.shape[0] // Q
    begin, turn, end = swap_states(
        ns, packed, total_log, onehot, later, got_states, got_decays, prefix, swap_sems, True
    )
    slot, drain = chains(n, all_ref, part, *chain_refs)
    span = part.shape[0] // STREAMS
    groups = total_chunks // n
    taps = TAPS
    me, seq = lax.axis_index("head"), lax.axis_index("seq")
    state_size = bmat_width(sact)
    two = 2 * state_size

    def halo(src, dst, k):
        return pltpu.make_async_remote_copy(
            src_ref=src,
            dst_ref=dst,
            send_sem=h_sem.at[k],
            recv_sem=h_sem.at[k + 1],
            device_id={"seq": (seq + ns - 1) % ns},
            device_id_type=MESH_ID,
        )

    def chunk_rows(k):
        return pl.ds(pl.multiple_of(k * Q, Q), Q)

    def code_rows(k):
        return pl.ds(pl.multiple_of(k * (Q + 16), 16), Q + 16)

    def to_owner(k):
        return pltpu.make_async_remote_copy(
            src_ref=psend.at[code_rows(k)],
            dst_ref=pgot.at[me, code_rows(k // n)],
            send_sem=p_send.at[k],
            recv_sem=p_recv.at[me, k // n],
            device_id={"head": k % n},
            device_id_type=MESH_ID,
        )

    def from_other(j, g):
        return pltpu.make_async_remote_copy(
            src_ref=psend.at[code_rows(g)],
            dst_ref=pgot.at[j, code_rows(g)],
            send_sem=p_send.at[g],
            recv_sem=p_recv.at[j, g],
            device_id={"head": j},
            device_id_type=MESH_ID,
        )

    def give(k, g, arriving):
        other = (me + k) % n
        owner = other if arriving else me
        where = chunk_rows(g * n + owner)
        return pltpu.make_async_remote_copy(
            src_ref=gsb_o.at[where],
            dst_ref=gsb_o.at[where],
            send_sem=g_send.at[k, g],
            recv_sem=g_recv.at[owner, g],
            device_id={"head": other},
            device_id_type=MESH_ID,
        )

    @pl.when(i == 0)
    def _():
        barrier = greet(n, ns)
        small_a[...] = jnp.zeros_like(small_a)
        small_b[...] = jnp.zeros_like(small_b)
        small_a[5:7, :] = rows_in[0:2, :]

        def compute(h):
            where = pl.ds(pl.multiple_of(h * span, span), span)
            part[where, :] = dg(ynorm[where, :], proj_output[...], NN)

        compute(0)
        pl.semaphore_wait(barrier, n + ns - 2)
        begin()

        @pl.loop(0, 2)
        def _(t):
            slot(t)
            compute(t + 1)

        @pl.loop(3, STREAMS)
        def _(h):
            compute(h)

        turn()
        slot(2)
        end()

    @pl.when((c >= 0) & (c < count))
    def _():
        hot = onehot[...]
        skip = params[6:7, :]
        rate = params[7:8, :LANES]
        sactv = sact[...]
        ssg = sigmoid(sactv)
        sconv = sactv * ssg
        bmat, cmat = sconv[:, :state_size], sconv[:, state_size:]
        actv = act[...]
        sg = sigmoid(actv)
        x = actv * sg
        cumv, stepv = cum[...], step[...]
        last = cumv[Q - 1 :, :]
        step_wide = spread(stepv, hot)
        xs = x * step_wide
        xs_ref[...] = xs
        g = gssd[...]

        def row(value):
            return spread(jnp.broadcast_to(jnp.exp(value), (HALO, LANES)), hot)[:1]

        state = sin[...] + row(before_log[...]) * incoming[...]
        adj = dout[...] + row(total_log[0:1, :] - before_log[...] - last) * later[...]
        to_end = spread(jnp.exp(last - cumv), hot)
        u_state = to_end * dot3(bmat, adj, NN)
        ends = row(last) * jnp.sum(adj * state, axis=0, keepdims=True) + jnp.sum(
            xs * u_state, axis=0, keepdims=True
        )
        scores_t = dot3(bmat, cmat, NT)
        later_mask = triangle(False)
        lane = lax.broadcasted_iota(jnp.int32, (Q, LANES), 1)
        st_ref[...] = jnp.zeros_like(st_ref)
        for p in range(act.shape[1] // LANES):
            cols = slice(p * LANES, (p + 1) * LANES)
            right = pair_stack(gssd[:, cols])
            g_high, g_low = right[:Q, :LANES], right[:Q, LANES:]
            twice = jnp.concatenate([g_high, g_high], axis=1)
            pair = xs_ref[:, cols]
            got = []
            for j in range(2):
                h = p * 2 + j
                gap = cumt[h : h + 1, :] - cum[:, h : h + 1]
                decay = jnp.exp(jnp.where(later_mask, gap, -1e30))
                wide = dg(jnp.concatenate(split(scores_t * decay), axis=1), right, NN)
                got.append(wide[:, :LANES] + wide[:, LANES:])
                mine = (lane < LANES // 2) if j == 0 else (lane >= LANES // 2)
                xh, xl = split(jnp.where(mine, pair, 0.0))
                inner = dg(jnp.concatenate([xh, xl], axis=1), twice, NT) + dg(xh, g_low, NT)
                st_ref[...] = st_ref[...] + decay * inner
            u_ref[:, cols] = jnp.where(lane < LANES // 2, got[0], got[1])
        u = u_ref[...] + u_state
        sc = st_ref[...]
        g_scaled = g * spread(jnp.exp(cumv), hot)
        gstates = jnp.concatenate(
            [
                dot3(sc, cmat, NN) + dot3(xs * to_end, adj, NT),
                dot3(sc.T, bmat, NN) + dot3(g_scaled, state, NT),
            ],
            axis=1,
        )
        gsact = gstates * (ssg * (1.0 + sactv * (1.0 - ssg)))
        gact = (step_wide * u + skip * g) * (sg * (1.0 + actv * (1.0 - sg)))
        u_ref[...] = gact
        sext[Q + HALO :, :] = gsact
        small_a[4:5, :] = small_a[4:5, :] + jnp.sum(gact, axis=0, keepdims=True)
        small_b[4:5, :] = small_b[4:5, :] + jnp.sum(gsact, axis=0, keepdims=True)
        direct = gather(x * u, hot)
        flow = gather(g * (y[...] - skip * x), hot) - stepv * direct
        ends_heads = gather(jnp.broadcast_to(ends, (HALO, ends.shape[1])), hot)[:1]
        da = tri_sum(False, flow) + ends_heads
        slope = (direct + rate * da) * sigmoid(step_pre[...] + params[7:8, LANES : 2 * LANES])
        gstep[Q:, :] = slope.astype(BF16)
        small_a[7:8, :LANES] = small_a[7:8, :LANES] + jnp.sum(
            stepv * rate * da, axis=0, keepdims=True
        )
        small_a[7:8, LANES : 2 * LANES] = small_a[7:8, LANES : 2 * LANES] + jnp.sum(
            slope, axis=0, keepdims=True
        )

    @pl.when(c == 0)
    def _():
        halo_send[...] = u_ref[:HALO, :]
        shalo_send[...] = sext[Q + HALO : Q + 2 * HALO, :]

        @pl.when(seq > 0)
        def _():
            halo(halo_send, halo_got, 0).start()
            halo(shalo_send, shalo_got, 2).start()

    @pl.when(c == count)
    def _():
        @pl.when(seq < ns - 1)
        def _():
            halo(halo_send, halo_got, 0).wait_recv()
            halo(shalo_send, shalo_got, 2).wait_recv()
            u_ref[:HALO, :] = halo_got[...]
            sext[Q + HALO : Q + 2 * HALO, :] = shalo_got[...]

        @pl.when(seq == ns - 1)
        def _():
            u_ref[:HALO, :] = jnp.zeros((HALO, u_ref.shape[1]), F32)
            sext[Q + HALO : Q + 2 * HALO, :] = jnp.zeros((HALO, two), F32)

        @pl.when(seq > 0)
        def _():
            halo(halo_send, halo_got, 0).wait_send()
            halo(shalo_send, shalo_got, 2).wait_send()

    @pl.when(c >= 1)
    def _():
        gext[Q:, :] = u_ref[:HALO, :]
        sext[Q : Q + HALO, :] = sext[Q + HALO : Q + 2 * HALO, :]
        pext[:HALO, :] = jnp.where(c == 1, pre_halo[...], pre_prev[...])
        pext[HALO:, :] = pre[...]
        spext[:HALO, :] = jnp.where(c == 1, spre_halo[...], spre_prev[...])
        spext[HALO:, :] = spre[...]

        def conv_back(ext, ext_pre, taps_at, size, sums):
            g = ext[:Q, :]
            total = params[taps_at + taps - 1 : taps_at + taps, :size] * g
            for k in range(taps - 1):
                start = taps - 1 - k
                total = total + params[taps_at + k : taps_at + k + 1, :size] * ext[start : start + Q, :]
            for k in range(taps):
                start = HALO - taps + 1 + k
                sums[k : k + 1, :] = sums[k : k + 1, :] + jnp.sum(
                    g * ext_pre[start : start + Q, :], axis=0, keepdims=True
                )
            return total

        inner = gext.shape[1]
        gin_o[:, :inner] = conv_back(gext, pext, 0, inner, small_a).astype(BF16)
        gin_o[:, inner:] = gstep[:Q, :]
        gin_all[chunk_rows(c - 1), :] = gin_o[...]
        mine = conv_back(sext, spext, 8, two, small_b)
        psum[chunk_rows(c - 1), :] = mine

        @pl.when((c - 1) % n != me)
        def _():
            top = jnp.max(jnp.abs(mine), axis=0, keepdims=True)
            scale = (top * 1.004 + 1e-30).astype(BF16)
            first = pl.multiple_of((c - 1) * (Q + 16), 16)
            psend[pl.ds(first, Q), :] = jnp.exp(mine * (SPAN / scale.astype(F32))).astype(BF16)
            psend[pl.ds(first + Q, 16), :] = jnp.broadcast_to(scale, (16, two))
            to_owner(c - 1).start()

    @pl.when((c >= 0) & (c < count))
    def _():
        gext[:Q, :] = u_ref[...]
        gstep[:Q, :] = gstep[Q:, :]
        sext[:Q, :] = sext[Q + HALO :, :]

    @pl.when(c == count)
    def _():
        @pl.loop(0, win_o.shape[0] // 256)
        def _(m):
            cols = pl.ds(pl.multiple_of(m * 256, 256), 256)
            win_o[cols, :] = dg(normed[:, cols], gin_all[...], TN)

    for g in range(groups):

        @pl.when(c == min((g + 1) * n + 2, total_chunks))
        def _():
            own = chunk_rows(g * n + me)
            total = psum[own, :]
            for k in range(1, n):
                j = (me + k) % n
                from_other(j, g).wait_recv()
                first = g * (Q + 16)
                scale = pgot[j, first + Q : first + Q + 16, :].astype(F32)[:1] * (1.0 / SPAN)
                total = total + jnp.log(pgot[j, first : first + Q, :].astype(F32)) * scale
            gsb_o[own, :] = total.astype(BF16)
            for k in range(1, n):
                give(k, g, False).start()

    @pl.when(c == count)
    def _():
        for g in range(groups):
            for k in range(1, n):
                give(k, g, True).wait_recv()
        gsb_out[...] = gsb_o[...]
        for g in range(groups):
            for k in range(1, n):
                give(k, g, False).wait_send()
        for k in range(total_chunks):

            @pl.when(k % n != me)
            def _():
                to_owner(k).wait_send()

    last_step = count + 1
    more = slots_of(n) - 3

    @pl.when(i >= 1)
    def _():
        @pl.loop(3 + (i - 1) * more // last_step, 3 + i * more // last_step)
        def _(t):
            slot(t)

    @pl.when(i == last_step)
    def _():
        drain()
        code_out[...] = all_ref[...]


def transposed_times(left, right):
    return dg(left, right, TN)


def on_device(
    hidden,
    in_gain,
    proj_gate,
    proj_input,
    proj_states,
    proj_step,
    conv_input,
    conv_input_bias,
    conv_states,
    conv_states_bias,
    step_bias,
    decay_log,
    skip_gain,
    gate_gain,
    proj_output,
    cotangent,
):
    seg_count = lax.axis_size("seq")
    head_index = lax.axis_index("head")
    tokens, width = hidden.shape
    heads = proj_step.shape[1]
    inner = proj_gate.shape[1]
    state_size = conv_states.shape[1] // 2
    head_dim = inner // heads
    row_width = proj_states.shape[0]
    count = tokens // Q
    gain_full = in_gain.astype(F32)

    def pad_heads(value):
        return jnp.pad(value, [(0, 0)] * (value.ndim - 1) + [(0, LANES - heads)])

    n, ns = lax.axis_size("head"), seg_count

    stripe = 256

    def striped(size):
        return pl.BlockSpec((stripe, size), lambda c: (c, 0))

    def fixed(shape, at=0):
        return pl.BlockSpec(shape, lambda c: (at, 0), pipeline_mode=pl.Buffered(1))

    (
        normed, inv_rms, input_pre, gate_pre, grad_ynorm, proj_states_full, normed_halo, input_halo,
    ) = call(
        functools.partial(front_kernel, n, ns),
        (tokens // stripe,),
        [
            (hidden, striped(width)),
            (cotangent, striped(width)),
            (hidden, fixed((16, width), tokens // 16 - 1)),
            (gain_full[None, :], fixed((1, width))),
            (proj_input, fixed((width, inner))),
            (proj_gate, fixed((width, inner))),
            (proj_output, fixed((inner, width))),
            (proj_states, fixed((row_width, 2 * state_size))),
        ],
        [
            (sds((tokens, width), BF16), striped(width)),
            (sds((tokens, 1)), striped(1)),
            (sds((tokens, inner)), striped(inner)),
            (sds((tokens, inner)), striped(inner)),
            (sds((tokens, inner)), striped(inner)),
            (sds((width, 2 * state_size), BF16), whole((width, 2 * state_size))),
            (sds((16, width), BF16), whole((16, width))),
            (sds((HALO, inner)), whole((HALO, inner))),
        ],
        scratch=[
            pltpu.VMEM((width, 2 * state_size), BF16),
            pltpu.VMEM((16, width), BF16),
            pltpu.SemaphoreType.DMA((n,)),
            pltpu.SemaphoreType.DMA((n,)),
            pltpu.SemaphoreType.DMA((2,)),
        ],
        flops=6 * tokens * inner * width,
        collective=6,
    )
    proj_step_wide = pad_heads(proj_step)
    two = 2 * state_size
    flat = jnp.concatenate(
        [
            pad_heads(decay_log),
            pad_heads(step_bias),
            pad_heads(skip_gain),
            conv_input_bias.astype(F32),
            gate_gain.astype(F32),
            conv_states_bias.astype(F32),
        ]
    )
    flat = jnp.pad(flat, (0, -flat.shape[0] % 1024))
    vec = flat.reshape(-1, LANES)
    onehot = jnp.asarray(
        np.arange(LANES)[:, None] == np.arange(inner)[None, :] // head_dim, dtype=BF16
    )
    hot = (onehot, whole((LANES, inner)))
    state_rows = pl.BlockSpec((state_size, inner), lambda c: (c, 0))
    packed_shape = (state_size, inner)
    logs_shape = (HALO, LANES)
    big = GROUP * Q
    (
        act, sact, states_pre, states_halo, step_pre, step, cum, cumt, sin, packed, total_log,
        before_log, params,
    ) = call(
        states_kernel,
        (count // GROUP,),
        [
            (input_pre, rows(inner, big)),
            (input_pre, before(inner, big)),
            (input_halo, whole((HALO, inner))),
            (normed, rows(width, big)),
            (normed_halo, whole((16, width))),
            (proj_step_wide, whole((width, LANES))),
            (vec, whole(vec.shape)),
            (conv_input, whole(conv_input.shape)),
            (conv_states, whole(conv_states.shape)),
            (proj_states_full, whole((width, two))),
            hot,
        ],
        [
            (sds((tokens, inner)), rows(inner, big)),
            (sds((tokens, two)), rows(two, big)),
            (sds((tokens, two)), rows(two, big)),
            (sds((HALO, two)), whole((HALO, two))),
            (sds((tokens, LANES)), rows(LANES, big)),
            (sds((tokens, LANES)), rows(LANES, big)),
            (sds((tokens, LANES)), rows(LANES, big)),
            (sds((tokens, LANES)), rows(LANES, big)),
            (sds((count * state_size, inner)), pl.BlockSpec((GROUP * state_size, inner), lambda c: (c, 0))),
            (sds(packed_shape), whole(packed_shape)),
            (sds((HALO, LANES)), whole((HALO, LANES))),
            (sds((count, 1, LANES)), pl.BlockSpec((GROUP, 1, LANES), lambda c: (c, 0, 0))),
            (sds((16, inner)), whole((16, inner))),
        ],
        scratch=[
            pltpu.VMEM((big + HALO, inner), F32),
            pltpu.VMEM((big + HALO, two), F32),
            pltpu.VMEM((state_size, inner), F32),
            pltpu.VMEM((1, LANES), F32),
        ],
        flops=10 * tokens * inner * state_size,
    )
    par = (params, whole((16, inner)))
    yloc, incoming = call(
        functools.partial(intra_kernel, ns),
        (count // GROUP,),
        [
            (act, rows(inner, big)),
            (sact, rows(two, big)),
            (step, rows(LANES, big)),
            (cum, rows(LANES, big)),
            (cumt, rows(LANES, big)),
            par,
            hot,
            (packed, whole(packed_shape)),
            (total_log, whole(logs_shape)),
        ],
        [
            (sds((tokens, inner)), rows(inner, big)),
            (sds((state_size, inner)), whole((state_size, inner))),
        ],
        scratch=[pltpu.VMEM((big, inner), F32), pltpu.VMEM((state_size, inner), F32)]
        + swap_scratch(ns, (state_size, inner)),
        flops=12 * tokens * inner * Q,
        collective=5,
    )

    half = count // GROUP

    def both(i):
        return jnp.where(i < half, i, 2 * half - 1 - i)

    def fore(i):
        return jnp.minimum(i, half - 1)

    def aft(i):
        return jnp.minimum(2 * half - 1 - i, half - 1)

    def at(size, which, height=big):
        return pl.BlockSpec((height, size), lambda i: (which(i), 0))

    y, ynorm, grad_gate_pre, grad_ssd, dout, packed_back, grad_rows = call(
        functools.partial(middle_kernel, n),
        (2 * half,),
        [
            (yloc, at(inner, fore)),
            (act, at(inner, aft)),
            (sact, at(two, both)),
            (cum, at(LANES, both)),
            (sin, at(inner, fore, GROUP * state_size)),
            (before_log, pl.BlockSpec((GROUP, 1, LANES), lambda i: (fore(i), 0, 0))),
            (incoming, whole((state_size, inner))),
            (gate_pre, at(inner, both)),
            (grad_ynorm, at(inner, both)),
            par,
            hot,
        ],
        [
            (sds((tokens, inner)), at(inner, fore)),
            (sds((tokens, inner), BF16), at(inner, aft)),
            (sds((tokens, inner), BF16), at(inner, aft)),
            (sds((tokens, inner)), at(inner, aft)),
            (sds((count * state_size, inner)), at(inner, aft, GROUP * state_size)),
            (sds(packed_shape), whole(packed_shape)),
            (sds((HALO, inner)), whole((HALO, inner))),
        ],
        scratch=[
            pltpu.VMEM((tokens, inner), F32),
            pltpu.VMEM((HALO, tokens), F32),
            pltpu.VMEM((n, HALO, tokens), F32),
            pltpu.VMEM((state_size, inner), F32),
            pltpu.SemaphoreType.DMA((n,)),
            pltpu.SemaphoreType.DMA((n,)),
        ],
        flops=12 * tokens * inner * state_size,
        collective=3,
    )
    local_proj_output = transposed_times(cotangent, ynorm)
    local_proj_gate = transposed_times(normed, grad_gate_pre)
    summed_out = lax.psum_scatter(
        local_proj_output, "seq", scatter_dimension=0, tiled=True
    )
    grad_proj_output = pl.pallas_call(
        turn_kernel, out_shape=sds(summed_out.shape[::-1]), name="turn"
    )(summed_out)
    grad_proj_gate = lax.psum_scatter(
        local_proj_gate, "seq", scatter_dimension=0, tiled=True
    )

    def now(i):
        return jnp.clip(i - 1, 0, count - 1)

    def past(i):
        return jnp.maximum(i - 2, 0)

    def held(size, height=Q):
        return pl.BlockSpec((height, size), lambda i: (now(i), 0))

    def prior(size):
        return pl.BlockSpec((Q, size), lambda i: (past(i), 0))

    def prior_edge(size):
        return pl.BlockSpec(
            (HALO, size), lambda i: (jnp.maximum(past(i) * (Q // HALO) - 1, 0), 0)
        )

    def once(shape):
        return pl.BlockSpec(shape, lambda i: (0, 0), pipeline_mode=pl.Buffered(1))

    dma = pltpu.SemaphoreType.DMA
    groups = count // n
    grad_in_b, grad_states_b, small_a, small_b, branch_code, local_proj_in = call(
        functools.partial(back_kernel, n, ns),
        (count + 2,),
        [
            (act, held(inner)),
            (sact, held(two)),
            (y, held(inner)),
            (grad_ssd, held(inner)),
            (step, held(LANES)),
            (step_pre, held(LANES)),
            (cum, held(LANES)),
            (cumt, held(LANES)),
            (sin, held(inner, state_size)),
            (dout, held(inner, state_size)),
            (
                before_log,
                pl.BlockSpec((None, 1, LANES), lambda i: (now(i), 0, 0)),
            ),
            (total_log, whole(logs_shape)),
            (incoming, once((state_size, inner))),
            (ynorm, once((tokens, inner))),
            (proj_output, once((inner, width))),
            (packed_back, once(packed_shape)),
            (normed, once((tokens, width))),
            par,
            hot,
            (grad_rows, whole((HALO, inner))),
            (input_pre, prior(inner)),
            (input_pre, prior_edge(inner)),
            (input_halo, whole((HALO, inner))),
            (states_pre, prior(two)),
            (states_pre, prior_edge(two)),
            (states_halo, whole((HALO, two))),
        ],
        [
            (sds((tokens, inner + LANES), BF16), prior(inner + LANES)),
            (sds((tokens, two), BF16), whole((tokens, two))),
            (sds((16, inner)), whole((16, inner))),
            (sds((HALO, two)), whole((HALO, two))),
            (sds((tokens, width + LANES), BF16), once((tokens, width + LANES))),
            (sds((width, inner + LANES)), once((width, inner + LANES))),
        ],
        scratch=[
            pltpu.VMEM((tokens, inner + LANES), BF16),
            pltpu.VMEM((tokens, two), BF16),
            pltpu.VMEM((2 * Q, LANES), BF16),
            pltpu.VMEM((Q, inner), F32),
            pltpu.VMEM((Q, inner), F32),
            pltpu.VMEM((Q, Q), F32),
            pltpu.VMEM((Q + HALO, inner), F32),
            pltpu.VMEM((2 * Q + HALO, two), F32),
            pltpu.VMEM((Q + HALO, inner), F32),
            pltpu.VMEM((Q + HALO, two), F32),
            pltpu.VMEM((HALO, inner), F32),
            pltpu.VMEM((HALO, inner), F32),
            pltpu.VMEM((HALO, two), F32),
            pltpu.VMEM((HALO, two), F32),
            pltpu.VMEM((tokens, two), F32),
            pltpu.VMEM((count * (Q + 16), two), BF16),
            pltpu.VMEM((n, groups * (Q + 16), two), BF16),
            dma((4,)),
            dma((count,)),
            dma((n, groups)),
            dma((n, groups)),
            dma((n, groups)),
            pltpu.VMEM((state_size, inner), F32),
            *swap_scratch(ns, (state_size, inner)),
            pltpu.VMEM((tokens, width + LANES), BF16),
            *chain_scratch(tokens, width, n),
        ],
        flops=40 * tokens * inner * Q,
        collective=4,
    )
    row_start = head_index * row_width
    own_states = lax.dynamic_update_slice_in_dim(
        jnp.zeros((width, two), BF16), proj_states, row_start, 0
    )
    normed_rows = lax.dynamic_slice_in_dim(normed, row_start, row_width, 1)
    local_proj_states = transposed_times(grad_states_b, normed_rows)
    summed_in = lax.psum_scatter(local_proj_in, "seq", scatter_dimension=0, tiled=True)
    grad_code, sum_a, sum_b, grad_proj_states = reduce_over_heads(
        [
            (grad_gate_pre, proj_gate),
            (grad_in_b, proj_input),
            (grad_in_b, proj_step_wide),
            (grad_states_b, own_states),
        ],
        [NT] * 4,
        (None, (0, inner), (inner, inner + LANES), None),
        2,
        (hidden, inv_rms, small_a, small_b, local_proj_states),
    )
    result, grad_hidden = call(
        finish_kernel,
        (tokens // stripe,),
        [
            (branch_code, striped(width + LANES)),
            (grad_code, striped(width + LANES)),
            (hidden, striped(width)),
            (cotangent, striped(width)),
            (inv_rms, striped(1)),
            (gain_full[None, :], fixed((1, width))),
        ],
        [(sds((tokens, width)), striped(width)), (sds((tokens, width)), striped(width))],
        flops=40 * tokens * width,
    )
    return (
        result,
        grad_hidden,
        sum_b[0],
        grad_proj_gate,
        summed_in[:, :inner],
        grad_proj_states.T,
        summed_in[:, inner : inner + heads],
        sum_a[:TAPS],
        sum_a[4],
        sum_b[8 : 8 + TAPS, :two],
        sum_b[12, :two],
        sum_a[7, LANES : LANES + heads],
        sum_a[7, :heads],
        jnp.sum(sum_a[6].reshape(heads, head_dim), axis=1),
        sum_a[5],
        grad_proj_output,
    )


def solution(mesh):
    in_specs = (
        P("seq", None),
        P(),
        P(None, "head"),
        P(None, "head"),
        P("head", None),
        P(None, "head"),
        P(None, "head"),
        P("head"),
        P(),
        P(),
        P("head"),
        P("head"),
        P("head"),
        P("head"),
        P("head", None),
        P("seq", None),
    )
    out_specs = (
        P("seq", None),
        P("seq", None),
        P(),
        P("seq", "head"),
        P("seq", "head"),
        P("head", "seq"),
        P("seq", "head"),
        P(None, "head"),
        P("head"),
        P(),
        P(),
        P("head"),
        P("head"),
        P("head"),
        P("head"),
        P("head", "seq"),
    )

    return jax.shard_map(
        on_device, mesh=mesh, in_specs=in_specs, out_specs=out_specs, check_vma=False
    )
```

```python
import functools

import jax
import jax.numpy as jnp
import numpy as np
from jax import lax
from jax.experimental import pallas as pl
from jax.experimental.pallas import tpu as pltpu
from jax.sharding import PartitionSpec as P


DI = 3072
EPS = 1e-05
Q = 128
LANES = 128
HALO = 8
TAPS = 4
GROUP = 2

F32 = jnp.float32
BF16 = jnp.bfloat16
NN = (((1,), (0,)), ((), ()))
NT = (((1,), (1,)), ((), ()))
TN = (((0,), (0,)), ((), ()))
VMEM_LIMIT = 63 * 1024 * 1024
MESH_ID = pl.DeviceIdType.MESH


def dg(left, right, dims):
    return lax.dot_general(left, right, dims, preferred_element_type=F32)


def split(value):
    high = value.astype(BF16)
    return high, (value - high.astype(F32)).astype(BF16)


def dot3(left, right, dims):
    (lh, ll), (rh, rl) = split(left), split(right)
    return dg(lh, rh, dims) + (dg(lh, rl, dims) + dg(ll, rh, dims))


def spread(heads, onehot):
    high, low = split(heads)
    return dg(high, onehot, NN) + dg(low, onehot, NN)


def gather(wide, onehot):
    high, low = split(wide)
    return dg(high, onehot, NT) + dg(low, onehot, NT)


def sigmoid(value):
    return 0.5 * jnp.tanh(0.5 * value) + 0.5


def silu(value):
    return value * sigmoid(value)


def call(kernel, grid, ins, outs, scratch=(), flops=0, collective=None):
    in_specs = [spec for _, spec in ins]
    size = sum(a.size * a.dtype.itemsize for a, _ in ins) + sum(
        s.size * s.dtype.itemsize for s, _ in outs
    )
    return pl.pallas_call(
        kernel,
        grid=grid,
        in_specs=in_specs,
        out_specs=[spec for _, spec in outs],
        out_shape=[shape for shape, _ in outs],
        scratch_shapes=list(scratch),
        cost_estimate=pl.CostEstimate(flops=flops, bytes_accessed=size, transcendentals=0),
        compiler_params=pltpu.CompilerParams(vmem_limit_bytes=VMEM_LIMIT)
        if collective is None
        else pltpu.CompilerParams(
            vmem_limit_bytes=VMEM_LIMIT, collective_id=collective, has_side_effects=True
        ),
    )(*[a for a, _ in ins])


def sds(shape, dtype=F32):
    return jax.ShapeDtypeStruct(shape, dtype)


def rows(width, height=Q):
    return pl.BlockSpec((height, width), lambda c: (c, 0))


def whole(shape):
    return pl.BlockSpec(shape, lambda c: (0,) * len(shape))


def before(width, height):
    return pl.BlockSpec((HALO, width), lambda c: (jnp.maximum(c * (height // HALO) - 1, 0), 0))


def triangle(lower):
    a = lax.broadcasted_iota(jnp.int32, (Q, Q), 0)
    b = lax.broadcasted_iota(jnp.int32, (Q, Q), 1)
    return a >= b if lower else a <= b


def tri_sum(lower, value):
    mask = triangle(lower).astype(BF16)
    high = value.astype(BF16)
    rest = value - high.astype(F32)
    mid = rest.astype(BF16)
    low = (rest - mid.astype(F32)).astype(BF16)
    return dg(mask, high, NN) + (dg(mask, mid, NN) + dg(mask, low, NN))


def conv_act(pre, ext_ref, params, at):
    size = ext_ref.shape[1]
    height = pre.shape[0]
    ext_ref[HALO:, :] = pre
    total = params[at + TAPS : at + TAPS + 1, :size] + params[at + TAPS - 1 : at + TAPS, :size] * pre
    for k in range(TAPS - 1):
        start = HALO - TAPS + 1 + k
        total = total + params[at + k : at + k + 1, :size] * ext_ref[start : start + height, :]
    return total


def line(vec, first, size):
    return jnp.concatenate([vec[r : r + 1, :] for r in range(first, first + size // LANES)], axis=1)


def front_kernel(
    n, ns, hidden, cotangent, tail, vec, proj_input, proj_gate, proj_output, piece,
    normed_o, inv_o, pre_o, gate_o, gyn_o, full_o, nhalo_o, halo_o,
    full, halo, s_sem, r_sem, w_sem, v_sem, h_sem,
):
    c = pl.program_id(0)
    me, seq = lax.axis_index("head"), lax.axis_index("seq")
    height = piece.shape[0]
    short = height // 2
    odd = seq % 2
    last = pl.num_programs(0) - 1

    def slab(j):
        return pl.ds(pl.multiple_of(j * height, height), height)

    def part(j, which):
        return pl.ds(pl.multiple_of(j * height + which * short, short), short)

    def give(k, arriving):
        other = (me + k) % n
        owner = other if arriving else me
        return pltpu.make_async_remote_copy(
            src_ref=piece.at[pl.ds(pl.multiple_of(odd * short, short), short)],
            dst_ref=full.at[part(owner, odd)],
            send_sem=s_sem.at[k],
            recv_sem=r_sem.at[owner],
            device_id={"head": other},
            device_id_type=MESH_ID,
        )

    def swap(k, arriving):
        owner = (me + k) % n
        where = part(owner, 1 - odd if arriving else odd)
        return pltpu.make_async_remote_copy(
            src_ref=full.at[where],
            dst_ref=full.at[where],
            send_sem=w_sem.at[k],
            recv_sem=v_sem.at[k],
            device_id={"seq": seq + 1 - 2 * odd},
            device_id_type=MESH_ID,
        )

    def edge():
        return pltpu.make_async_remote_copy(
            src_ref=tail,
            dst_ref=halo,
            send_sem=h_sem.at[0],
            recv_sem=h_sem.at[1],
            device_id={"seq": (seq + 1) % ns},
            device_id_type=MESH_ID,
        )

    def norm(value):
        value = value.astype(F32)
        inv = lax.rsqrt(jnp.mean(value * value, axis=-1, keepdims=True) + EPS)
        return inv, (value * inv * gain).astype(BF16)

    first = 3 + (2 * pre_o.shape[1] + piece.shape[1]) // LANES
    gain = line(vec, first, hidden.shape[1])
    barrier = pltpu.get_barrier_semaphore()

    @pl.when(c == 0)
    def _():
        greet(n, ns)

    inv, normed = norm(hidden[...])
    inv_o[...] = inv
    normed_o[...] = normed
    pre_o[...] = dg(normed, proj_input[...], NN)

    @pl.when(c == 0)
    def _():
        pl.semaphore_wait(barrier, n + ns - 2)
        for k in range(1, n):
            give(k, False).start()

        @pl.when(seq < ns - 1)
        def _():
            edge().start()

        full[slab(me), :] = piece[...]

    gate_o[...] = dg(normed, proj_gate[...], NN)
    gyn_o[...] = dg(cotangent[...], proj_output[...], NT)

    @pl.when(c == jnp.maximum(last - 1, 0))
    def _():
        for k in range(1, n):
            give(k, True).wait_recv()
            swap(k, False).start()

    @pl.when(c == last)
    def _():
        @pl.when(seq > 0)
        def _():
            edge().wait_recv()

        @pl.when(seq == 0)
        def _():
            halo[...] = jnp.zeros_like(halo)

        before_first = norm(halo[...])[1]
        nhalo_o[...] = before_first
        halo_o[...] = dg(before_first, proj_input[...], NN)[16 - HALO :, :]

        @pl.when(seq < ns - 1)
        def _():
            edge().wait_send()

        for k in range(1, n):
            swap(k, True).wait_recv()
        full_o[...] = full[...]
        for k in range(1, n):
            swap(k, False).wait_send()
            give(k, False).wait_send()


def states_kernel(
    pre, pre_prev, pre_halo, normed, normed_halo, step_w, vec, taps_in, taps_st, full, onehot, *refs
):
    act_o, sact_o, spre_o, shalo_o, spre_step_o, step_o, cum_o, cumt_o, sin_o, dev_o, total_o = refs[:11]
    before_o, params = refs[11:13]
    ext, sext, state, total = refs[13:]
    c = pl.program_id(0)
    state_size = bmat_width(sact_o)
    inner = pre.shape[1]
    two = 2 * state_size
    hot = onehot[...]

    height = pre.shape[0]

    @pl.when(c == 0)
    def _():
        state[...] = jnp.zeros_like(state)
        total[...] = jnp.zeros_like(total)
        params[...] = jnp.zeros_like(params)
        per = inner // LANES
        params[0:TAPS, :] = taps_in[...].astype(F32)
        params[4:5, :] = line(vec, 3, inner)
        params[5:6, :] = line(vec, 3 + per, inner)
        params[6:7, :] = spread(jnp.broadcast_to(vec[2:3, :], (HALO, LANES)), hot)[:1]
        params[7:8, :LANES] = -jnp.exp(vec[0:1, :])
        params[7:8, LANES : 2 * LANES] = vec[1:2, :]
        params[8 : 8 + TAPS, :two] = taps_st[...].astype(F32)
        params[12:13, :two] = line(vec, 3 + 2 * per, two)
        shalo_o[...] = dg(normed_halo[...], full[...], NN)[16 - HALO :, :]
        sext[height:, :] = shalo_o[...]
        ext[:HALO, :] = pre_halo[...]

    @pl.when(c > 0)
    def _():
        ext[:HALO, :] = pre_prev[...]

    sext[:HALO, :] = sext[height:, :]
    spre = dg(normed[...], full[...], NN)
    spre_o[...] = spre
    step_pre = dg(normed[...], step_w[...], NT)
    spre_step_o[...] = step_pre
    act = conv_act(pre[...], ext, params, 0)
    sact = conv_act(spre, sext, params, 8)
    act_o[...] = act
    sact_o[...] = sact
    step = jax.nn.softplus(step_pre + params[7:8, LANES : 2 * LANES])
    step_o[...] = step
    x = silu(act)
    bmat_all = silu(sact[:, :state_size])
    for j in range(height // Q):
        part = slice(j * Q, (j + 1) * Q)
        cum = tri_sum(True, step[part] * params[7:8, :LANES])
        cum_o[part, :] = cum
        cumt_o[part, :] = cum.T
        last = cum[Q - 1 :, :]
        xw = x[part] * spread(step[part] * jnp.exp(last - cum), hot)
        sin_o[j * state_size : (j + 1) * state_size, :] = state[...]
        before_o[j] = total[...]
        decay = spread(jnp.broadcast_to(jnp.exp(last), (HALO, LANES)), hot)[:1]
        state[...] = state[...] * decay + dot3(bmat_all[part], xw, TN)
        total[...] = total[...] + last
    dev_o[...] = state[...]
    total_o[...] = jnp.broadcast_to(total[...], (HALO, LANES))


def bmat_width(ref):
    return ref.shape[1] // 2


def pair_stack(value):
    high, low = split(value)
    return jnp.concatenate(
        [
            jnp.concatenate([high, low], axis=1),
            jnp.concatenate([high, jnp.zeros_like(high)], axis=1),
        ],
        axis=0,
    )


def intra_kernel(
    ns, act, sact, step, cum, cumt, params, onehot, packed, logs, out, incoming,
    xs_ref, entered, got_s, got_d, prefix, sems,
):
    c = pl.program_id(0)
    count = pl.num_programs(0)
    seq = lax.axis_index("seq")
    begin, turn, end = swap_states(
        ns, packed, logs, onehot, entered, got_s, got_d, prefix, sems, False
    )
    barrier = pltpu.get_barrier_semaphore()

    @pl.when(c == 0)
    def _():
        for k in range(1, ns):
            pl.semaphore_signal(
                barrier, inc=1, device_id={"seq": (seq + k) % ns}, device_id_type=MESH_ID
            )
        pl.semaphore_wait(barrier, ns - 1)
        begin()

    state_size = bmat_width(sact)
    x = silu(act[...])
    xs_ref[...] = x * spread(step[...], onehot[...])
    out[...] = x * params[6:7, :]

    @pl.loop(0, act.shape[0] // Q)
    def _(chunk):
        here = pl.ds(pl.multiple_of(chunk * Q, Q), Q)
        sconv = silu(sact[here, :])
        bmat, cmat = sconv[:, :state_size], sconv[:, state_size:]
        scores = dot3(cmat, bmat, NT)
        causal = triangle(True)
        lane = lax.broadcasted_iota(jnp.int32, (Q, LANES), 1)
        sums, turned = cum.at[here], cumt.at[here]
        for p in range(act.shape[1] // LANES):
            cols = slice(p * LANES, (p + 1) * LANES)
            right = pair_stack(xs_ref[here, cols])
            got = []
            for j in range(2):
                h = p * 2 + j
                gap = sums[:, h : h + 1] - turned[h : h + 1, :]
                mixing = scores * jnp.exp(jnp.where(causal, gap, -1e30))
                wide = dg(jnp.concatenate(split(mixing), axis=1), right, NN)
                got.append(wide[:, :LANES] + wide[:, LANES:])
            out[here, cols] = out[here, cols] + jnp.where(lane < LANES // 2, got[0], got[1])

    @pl.when(c == count // 2)
    def _():
        turn()

    @pl.when(c == count - 1)
    def _():
        end()
        incoming[...] = entered[...]


STREAMS = 8
SPAN = 83.0


def encode(value):
    top = jnp.max(jnp.abs(value), axis=1, keepdims=True)
    scale = (top * 1.004 + 1e-30).astype(BF16)
    code = jnp.exp(value * (SPAN / scale.astype(F32))).astype(BF16)
    return code, jnp.broadcast_to(scale, (value.shape[0], LANES))


def decode(block, width):
    scale = block[:, width : width + 1].astype(F32) * (1.0 / SPAN)
    return jnp.log(block[:, :width].astype(F32)) * scale


def swap_states(ns, packed, logs, onehot, out, got_s, got_d, prefix, sems, reverse):
    seq = lax.axis_index("seq")
    own = out.shape[0] // ns

    def rows_of(j):
        return pl.ds(pl.multiple_of(j * own, own), own)

    def remote(src, dst, send, recv, to):
        return pltpu.make_async_remote_copy(
            src_ref=src,
            dst_ref=dst,
            send_sem=send,
            recv_sem=recv,
            device_id={"seq": to},
            device_id_type=MESH_ID,
        )

    def copies(k, arriving):
        other = (seq + k) % ns
        slot = other if arriving else seq
        part = packed.at[rows_of(other)]
        return (
            remote(part, got_s.at[slot], sems.at[0, k], sems.at[1, slot], other),
            remote(logs, got_d.at[slot], sems.at[2, k], sems.at[3, slot], other),
        )

    def answer(k, arriving):
        other = (seq + k) % ns
        slot = other if arriving else seq
        return remote(
            prefix.at[other], out.at[rows_of(slot)], sems.at[4, k], sems.at[5, slot], other
        )

    def begin():
        for k in range(1, ns):
            for copy in copies(k, False):
                copy.start()

    def turn():
        got_s[seq] = packed[rows_of(seq), :]
        got_d[seq] = logs[...]
        for k in range(1, ns):
            for copy in copies(k, True):
                copy.wait_recv()
        carry = jnp.zeros((own, out.shape[1]), F32)
        for i in reversed(range(ns)) if reverse else range(ns):
            prefix[i] = carry
            carry = carry * spread(jnp.exp(got_d[i]), onehot[...])[:1] + got_s[i]
        for k in range(1, ns):
            answer(k, False).start()
        out[rows_of(seq), :] = prefix[seq]

    def end():
        for k in range(1, ns):
            answer(k, True).wait_recv()
        for k in range(1, ns):
            answer(k, False).wait_send()
            for copy in copies(k, False):
                copy.wait_send()

    return begin, turn, end


def swap_scratch(ns, shape):
    own = shape[0] // ns
    return [
        pltpu.VMEM((ns, own, shape[1]), F32),
        pltpu.VMEM((ns, HALO, LANES), F32),
        pltpu.VMEM((ns, own, shape[1]), F32),
        pltpu.SemaphoreType.DMA((6, ns)),
    ]


def put(ref, where, value):
    code, scale = encode(value)
    width = value.shape[1]
    ref[where, :width] = code
    ref[where, width:] = scale


def chain_scratch(tokens, width, n):
    coded = pltpu.VMEM((tokens, width + LANES), BF16)
    return [pltpu.VMEM((tokens, width), F32), coded, coded, coded] + [
        pltpu.SemaphoreType.DMA((STREAMS, n))
    ] * 6


def chains(n, all_ref, part, code, got_r, got_l, s_sem, rr_sem, rl_sem, ar_sem, al_sem, ag_sem):
    me = lax.axis_index("head")
    tokens, width = part.shape
    span = tokens // STREAMS
    rows_own = span // n
    has_right, has_left = me < n - 1, me > 0

    def at(d, h):
        return pl.ds(pl.multiple_of(h * span + d * rows_own, rows_own), rows_own)

    def step(d, h, right):
        return pltpu.make_async_remote_copy(
            src_ref=code.at[at(d, h)],
            dst_ref=(got_r if right else got_l).at[at(d, h)],
            send_sem=s_sem.at[h, d],
            recv_sem=(rr_sem if right else rl_sem).at[h, d],
            device_id={"head": me + 1 if right else me - 1},
            device_id_type=MESH_ID,
        )

    def hand_on(b, h, right):
        return pltpu.make_async_remote_copy(
            src_ref=all_ref.at[at(b, h)],
            dst_ref=all_ref.at[at(b, h)],
            send_sem=(ar_sem if right else al_sem).at[h, b],
            recv_sem=ag_sem.at[h, b],
            device_id={"head": me + 1 if right else me - 1},
            device_id_type=MESH_ID,
        )

    def chain(h, u):
        for right in (True, False):
            d = me + (n - 1 - u) if right else me - (n - 1 - u)
            got = got_r if right else got_l
            inside = d <= n - 1 if right else d >= 0
            fed = has_left if right else has_right

            @pl.when(inside & fed)
            def _():
                step(d, h, right).wait_recv()
                put(code, at(d, h), part[at(d, h), :] + decode(got[at(d, h), :], width))
                step(d, h, right).start()

            @pl.when(inside & jnp.logical_not(fed))
            def _():
                put(code, at(d, h), part[at(d, h), :])
                step(d, h, right).start()

    def finish(h):
        own = at(me, h)

        @pl.when(has_left)
        def _():
            step(me, h, True).wait_recv()
            part[own, :] = part[own, :] + decode(got_r[own, :], width)

        @pl.when(has_right)
        def _():
            step(me, h, False).wait_recv()
            part[own, :] = part[own, :] + decode(got_l[own, :], width)

        put(all_ref, own, part[own, :])

        @pl.when(has_right)
        def _():
            hand_on(me, h, True).start()

        @pl.when(has_left)
        def _():
            hand_on(me, h, False).start()

    def relay(h, s):
        @pl.when(me - s >= 0)
        def _():
            hand_on(me - s, h, True).wait_recv()

            @pl.when(has_right)
            def _():
                hand_on(me - s, h, True).start()

        @pl.when(me + s < n)
        def _():
            hand_on(me + s, h, False).wait_recv()

            @pl.when(has_left)
            def _():
                hand_on(me + s, h, False).start()

    def slot(t):
        for u in range(2 * n - 2, -1, -1):
            h = t - u

            @pl.when((h >= 0) & (h < STREAMS))
            def _():
                if u < n - 1:
                    chain(h, u)
                elif u == n - 1:
                    finish(h)
                else:
                    relay(h, u - n + 1)

    def drain():
        @pl.loop(0, STREAMS)
        def _(h):
            for i in range(n):

                @pl.when(i > me)
                def _():
                    step(i, h, True).wait_send()

                @pl.when(i < me)
                def _():
                    step(i, h, False).wait_send()

                @pl.when(has_right & (i <= me))
                def _():
                    hand_on(i, h, True).wait_send()

                @pl.when(has_left & (i >= me))
                def _():
                    hand_on(i, h, False).wait_send()

    return slot, drain


def slots_of(n):
    return STREAMS - 1 + 2 * n - 1


def greet(n, ns):
    barrier = pltpu.get_barrier_semaphore()
    me, seq = lax.axis_index("head"), lax.axis_index("seq")
    for k in range(1, n):
        pl.semaphore_signal(
            barrier, inc=1, device_id={"head": (me + k) % n}, device_id_type=MESH_ID
        )
    for k in range(1, ns):
        pl.semaphore_signal(
            barrier, inc=1, device_id={"seq": (seq + k) % ns}, device_id_type=MESH_ID
        )
    return barrier


def reduce_kernel(n, ns, dims, cols, *refs):
    terms = len(dims)
    lefts, rights = refs[:terms], refs[terms : 2 * terms]
    refs = refs[2 * terms :]
    hidden_ref, inv_ref, small_a, small_b, states_ref, out_ref, sum_a, sum_b, sum_s = refs[:9]
    slot, drain = chains(n, out_ref, *refs[9:19])
    part = refs[9]
    got_a, got_b, got_s, got_c, mine_b = refs[19:24]
    sa_sem, ra_sem, sb_sem, rb_sem, ss_sem, rs_sem, sc_sem, rc_sem = refs[24:]
    me, seq = lax.axis_index("head"), lax.axis_index("seq")
    tokens, _ = part.shape
    span = tokens // STREAMS
    barrier = greet(n, ns)

    def to_seq(src, dst, ssem, rsem, k):
        return pltpu.make_async_remote_copy(
            src_ref=src,
            dst_ref=dst.at[seq],
            send_sem=ssem.at[k],
            recv_sem=rsem.at[seq],
            device_id={"seq": (seq + k) % ns},
            device_id_type=MESH_ID,
        )

    def from_seq(src, dst, ssem, rsem, k):
        other = (seq + k) % ns
        return pltpu.make_async_remote_copy(
            src_ref=src,
            dst_ref=dst.at[other],
            send_sem=ssem.at[k],
            recv_sem=rsem.at[other],
            device_id={"seq": other},
            device_id_type=MESH_ID,
        )

    def states_at(j):
        own = sum_s.shape[0]
        return states_ref.at[pl.ds(pl.multiple_of(j * own, own), own)]

    def compute(h):
        where = pl.ds(pl.multiple_of(h * span, span), span)
        total = None
        for left, right, dim, col in zip(lefts, rights, dims, cols):
            value = left[where, :] if col is None else left[where, col[0] : col[1]]
            term = dg(value, right[...], dim)
            total = term if total is None else total + term
        part[where, :] = total
        seen = total * (hidden_ref[where, :].astype(F32) * inv_ref[where, :])
        mine_b[0:1, :] = mine_b[0:1, :] + jnp.sum(seen, axis=0, keepdims=True)

    mine_b[...] = jnp.zeros_like(mine_b)
    mine_b[8:16, : small_b.shape[1]] = small_b[...]
    compute(0)
    pl.semaphore_wait(barrier, n + ns - 2)
    for k in range(1, ns):
        to_seq(small_a, got_a, sa_sem, ra_sem, k).start()
        to_seq(states_at((seq + k) % ns), got_s, ss_sem, rs_sem, k).start()

    @pl.loop(0, STREAMS - 1)
    def _(t):
        slot(t)
        compute(t + 1)

    for k in range(1, ns):
        to_seq(mine_b, got_b, sb_sem, rb_sem, k).start()

    @pl.loop(STREAMS - 1, slots_of(n) - 2)
    def _(t):
        slot(t)

    total = small_a[...]
    for k in range(1, ns):
        from_seq(small_a, got_a, sa_sem, ra_sem, k).wait_recv()
        total = total + got_a[(seq + k) % ns]
    sum_a[...] = total
    total = states_at(seq)[...]
    for k in range(1, ns):
        from_seq(states_at(seq), got_s, ss_sem, rs_sem, k).wait_recv()
        total = total + got_s[(seq + k) % ns]
    sum_s[...] = total
    total = mine_b[...]
    for k in range(1, ns):
        from_seq(mine_b, got_b, sb_sem, rb_sem, k).wait_recv()
        total = total + got_b[(seq + k) % ns]
    sum_b[...] = total

    def to_head(k):
        return pltpu.make_async_remote_copy(
            src_ref=sum_b,
            dst_ref=got_c.at[me],
            send_sem=sc_sem.at[k],
            recv_sem=rc_sem.at[me],
            device_id={"head": (me + k) % n},
            device_id_type=MESH_ID,
        )

    def from_head(k):
        other = (me + k) % n
        return pltpu.make_async_remote_copy(
            src_ref=sum_b,
            dst_ref=got_c.at[other],
            send_sem=sc_sem.at[k],
            recv_sem=rc_sem.at[other],
            device_id={"head": other},
            device_id_type=MESH_ID,
        )

    for k in range(1, n):
        to_head(k).start()

    @pl.loop(slots_of(n) - 2, slots_of(n))
    def _(t):
        slot(t)

    total = sum_b[...]
    for k in range(1, n):
        from_head(k).wait_recv()
    for k in range(1, n):
        to_head(k).wait_send()
        total = total + got_c[(me + k) % n]
    sum_b[...] = total
    for k in range(1, ns):
        to_seq(small_a, got_a, sa_sem, ra_sem, k).wait_send()
        to_seq(states_at((seq + k) % ns), got_s, ss_sem, rs_sem, k).wait_send()
        to_seq(mine_b, got_b, sb_sem, rb_sem, k).wait_send()
    drain()


def reduce_over_heads(products, dims, cols, collective, sums):
    n, ns = lax.axis_size("head"), lax.axis_size("seq")
    tokens, width = sums[0].shape
    lefts, rights = [a for a, _ in products], [b for _, b in products]
    dma = pltpu.SemaphoreType.DMA
    small_a = sums[2].shape
    states = (sums[4].shape[0] // ns, sums[4].shape[1])
    out_shape = [sds((tokens, width + LANES), BF16), sds(small_a), sds((16, width)), sds(states)]
    scratch = chain_scratch(tokens, width, n) + [
        pltpu.VMEM((ns, *small_a), F32),
        pltpu.VMEM((ns, 16, width), F32),
        pltpu.VMEM((ns, *states), F32),
        pltpu.VMEM((n, 16, width), F32),
        pltpu.VMEM((16, width), F32),
    ]
    scratch += [dma((ns,))] * 6 + [dma((n,))] * 2
    vmem = pl.BlockSpec(memory_space=pltpu.VMEM)
    return pl.pallas_call(
        functools.partial(reduce_kernel, n, ns, dims, cols),
        in_specs=[vmem] * (len(lefts) + len(rights) + len(sums)),
        out_specs=[vmem] * len(out_shape),
        out_shape=out_shape,
        scratch_shapes=scratch,
        compiler_params=pltpu.CompilerParams(
            collective_id=collective, has_side_effects=True, vmem_limit_bytes=VMEM_LIMIT
        ),
        cost_estimate=pl.CostEstimate(
            flops=2 * tokens * width * sum(a.shape[1] for a in lefts),
            bytes_accessed=100 * tokens * width,
            transcendentals=0,
        ),
        name="reduce_heads",
    )(*lefts, *rights, *sums)


def transposed(value):
    high, wide = value.shape
    value = jnp.concatenate([value, jnp.zeros((-high % LANES, wide), F32)], axis=0)
    return value.T[:, :high]


def finish_kernel(
    branch, code, hidden, cotangent, inv, vec, sum_a, sum_b, sum_s, out_grad, in_grad,
    result, out, grad_out, grad_in, grad_step, grad_states, taps_in, taps_st,
):
    width = out.shape[1]
    inner = grad_in.shape[1]
    heads = grad_step.shape[0]
    gain = line(vec, 3 + (2 * inner + taps_st.shape[1]) // LANES, width)
    resid = hidden[...].astype(F32)
    result[...] = resid + decode(branch[...], width)
    grad = decode(code[...], width) * gain
    scale = inv[...]
    dots = jnp.sum(grad * resid, axis=1, keepdims=True) * (1.0 / width)
    out[...] = (
        cotangent[...].astype(F32) + scale * grad - resid * (scale * scale * scale * dots)
    )

    @pl.when(pl.program_id(0) == 0)
    def _():
        grad_out[...] = out_grad[...]
        grad_in[...] = in_grad[:, :inner]
        grad_step[...] = transposed(in_grad[:, inner:])[:heads]
        grad_states[...] = sum_s[...]
        taps_in[...] = sum_a[:TAPS, :]
        taps_st[...] = sum_b[8 : 8 + TAPS, : taps_st.shape[1]]


def rows_of_sums(square, cross):
    first = jnp.sum(square, axis=1, keepdims=True)
    second = jnp.sum(cross, axis=1, keepdims=True)
    lane = lax.broadcasted_iota(jnp.int32, (square.shape[0], LANES), 1)
    columns = jnp.where(lane == 0, first, jnp.where(lane == 1, second, 0.0))
    parts = [columns[r : r + Q].T[:HALO] for r in range(0, square.shape[0], Q)]
    return jnp.concatenate(parts, axis=1)


def middle_kernel(
    n, yloc, act, sact, cum, sin, before_log, incoming, gate, gyn, params, onehot,
    y_o, ynorm_o, gpre_o, gssd_o, dout_o, dev_o, rows_o,
    keep, mine, got, adj, ssem, rsem,
):
    i = pl.program_id(0)
    count = pl.num_programs(0) // 2
    c = jnp.where(i < count, i, 2 * count - 1 - i)
    me = lax.axis_index("head")
    state_size = bmat_width(sact)
    hot = onehot[...]
    gain = params[5:6, :]
    height = gate.shape[0]
    where = pl.ds(pl.multiple_of(c * height, height), height)
    barrier = pltpu.get_barrier_semaphore()

    def copy(k, arriving):
        other = (me + k) % n
        return pltpu.make_async_remote_copy(
            src_ref=mine,
            dst_ref=got.at[other if arriving else me],
            send_sem=ssem.at[k],
            recv_sem=rsem.at[other if arriving else me],
            device_id={"head": other},
            device_id_type=MESH_ID,
        )

    @pl.when(i == 0)
    def _():
        for k in range(1, n):
            pl.semaphore_signal(
                barrier, inc=1, device_id={"head": (me + k) % n}, device_id_type=MESH_ID
            )

    cmat = silu(sact[:, state_size:])
    gv = gate[...]
    sg = sigmoid(gv)
    gsilu = gv * sg
    growth = spread(jnp.exp(cum[...]), hot)

    @pl.when(i < count)
    def _():
        ahead = []
        for j in range(height // Q):
            part = slice(j * Q, (j + 1) * Q)
            carry = spread(jnp.broadcast_to(jnp.exp(before_log[j]), (HALO, LANES)), hot)[:1]
            state = sin[j * state_size : (j + 1) * state_size, :] + carry * incoming[...]
            ahead.append(dot3(cmat[part], state, NN))
        y = yloc[...] + growth * jnp.concatenate(ahead, axis=0)
        y_o[...] = y
        keep[where, :] = y
        gated = y * gsilu
        mine[:, where] = rows_of_sums(gated * gated, gyn[...] * gain * gated)

    @pl.when(i == count - 1)
    def _():
        pl.semaphore_wait(barrier, n - 1)
        for k in range(1, n):
            copy(k, False).start()

    @pl.when(i == count)
    def _():
        adj[...] = jnp.zeros_like(adj)
        rows_o[...] = jnp.zeros_like(rows_o)
        total = mine[...]
        for k in range(1, n):
            copy(k, True).wait_recv()
        for k in range(1, n):
            copy(k, False).wait_send()
            total = total + got[(me + k) % n]
        mine[...] = total

    @pl.when(i >= count)
    def _():
        total = mine[:, where]
        blank = jnp.zeros((Q - HALO, Q), F32)
        columns = jnp.concatenate(
            [
                jnp.concatenate([total[:, r : r + Q], blank], axis=0).T
                for r in range(0, height, Q)
            ],
            axis=0,
        )
        inv = lax.rsqrt(columns[:, 0:1] / DI + EPS)
        cross = columns[:, 1:2] / DI
        yv = keep[where, :]
        gated = yv * gsilu
        normed = gated * inv
        ynorm_o[...] = (normed * gain).astype(BF16)
        rows_o[0:1, :] = rows_o[0:1, :] + jnp.sum(gyn[...] * normed, axis=0, keepdims=True)
        ggated = inv * (gyn[...] * gain) - normed * (inv * inv * cross)
        gpre_o[...] = (ggated * yv * sg * (1.0 + gv * (1.0 - sg))).astype(BF16)
        gssd = ggated * gsilu
        gssd_o[...] = gssd
        rows_o[1:2, :] = rows_o[1:2, :] + jnp.sum(gssd * silu(act[...]), axis=0, keepdims=True)
        scaled = gssd * growth
        for j in reversed(range(height // Q)):
            part = slice(j * Q, (j + 1) * Q)
            dout_o[j * state_size : (j + 1) * state_size, :] = adj[...]
            last = cum[(j + 1) * Q - 1 : (j + 1) * Q, :]
            decay = spread(jnp.broadcast_to(jnp.exp(last), (HALO, LANES)), hot)[:1]
            adj[...] = adj[...] * decay + dot3(cmat[part], scaled[part], TN)

    @pl.when(i == 2 * count - 1)
    def _():
        dev_o[...] = adj[...]


def back_kernel(
    n, ns, act, sact, y, gssd, step, step_pre, cum, cumt, sin, dout, before_log, total_log, incoming,
    ynorm, proj_output, packed, normed, cotangent,
    params, onehot, rows_in, pre, pre_prev, pre_halo, spre, spre_prev, spre_halo,
    gin_o, gsb_out, small_a, small_b, code_out, win_o, wout_o,
    gin_all, gsb_o, gstep, xs_ref, u_ref, st_ref, gext, sext, pext, spext, halo_send, halo_got, shalo_send, shalo_got,
    psum, psend, pgot, h_sem, p_send, p_recv, g_send, g_recv,
    later, got_states, got_decays, prefix, swap_sems, all_ref, part, *chain_refs,
):
    i = pl.program_id(0)
    c = i - 1
    count = pl.num_programs(0) - 2
    total_chunks = psum.shape[0] // Q
    begin, turn, end = swap_states(
        ns, packed, total_log, onehot, later, got_states, got_decays, prefix, swap_sems, True
    )
    slot, drain = chains(n, all_ref, part, *chain_refs)
    span = part.shape[0] // STREAMS
    groups = total_chunks // n
    taps = TAPS
    me, seq = lax.axis_index("head"), lax.axis_index("seq")
    state_size = bmat_width(sact)
    two = 2 * state_size

    def halo(src, dst, k):
        return pltpu.make_async_remote_copy(
            src_ref=src,
            dst_ref=dst,
            send_sem=h_sem.at[k],
            recv_sem=h_sem.at[k + 1],
            device_id={"seq": (seq + ns - 1) % ns},
            device_id_type=MESH_ID,
        )

    def chunk_rows(k):
        return pl.ds(pl.multiple_of(k * Q, Q), Q)

    def code_rows(k):
        return pl.ds(pl.multiple_of(k * (Q + 16), 16), Q + 16)

    def to_owner(k):
        return pltpu.make_async_remote_copy(
            src_ref=psend.at[code_rows(k)],
            dst_ref=pgot.at[me, code_rows(k // n)],
            send_sem=p_send.at[k],
            recv_sem=p_recv.at[me, k // n],
            device_id={"head": k % n},
            device_id_type=MESH_ID,
        )

    def from_other(j, g):
        return pltpu.make_async_remote_copy(
            src_ref=psend.at[code_rows(g)],
            dst_ref=pgot.at[j, code_rows(g)],
            send_sem=p_send.at[g],
            recv_sem=p_recv.at[j, g],
            device_id={"head": j},
            device_id_type=MESH_ID,
        )

    def give(k, g, arriving):
        other = (me + k) % n
        owner = other if arriving else me
        where = chunk_rows(g * n + owner)
        return pltpu.make_async_remote_copy(
            src_ref=gsb_o.at[where],
            dst_ref=gsb_o.at[where],
            send_sem=g_send.at[k, g],
            recv_sem=g_recv.at[owner, g],
            device_id={"head": other},
            device_id_type=MESH_ID,
        )

    @pl.when(i == 0)
    def _():
        barrier = greet(n, ns)
        small_a[...] = jnp.zeros_like(small_a)
        small_b[...] = jnp.zeros_like(small_b)
        small_a[5:7, :] = rows_in[0:2, :]

        def compute(h):
            where = pl.ds(pl.multiple_of(h * span, span), span)
            part[where, :] = dg(ynorm[where, :], proj_output[...], NN)

        compute(0)
        pl.semaphore_wait(barrier, n + ns - 2)
        begin()

        @pl.loop(0, 2)
        def _(t):
            slot(t)
            compute(t + 1)

        def product(m):
            cols = pl.ds(pl.multiple_of(m * 256, 256), 256)
            wout_o[cols, :] = dg(cotangent[:, cols], ynorm[...], TN)

        tiles = wout_o.shape[0] // 256

        @pl.loop(3, STREAMS)
        def _(h):
            compute(h)

        @pl.loop(0, tiles // 2)
        def _(m):
            product(m)

        turn()
        slot(2)

        @pl.loop(tiles // 2, tiles)
        def _(m):
            product(m)

        end()

    @pl.when((c >= 0) & (c < count))
    def _():
        hot = onehot[...]
        skip = params[6:7, :]
        rate = params[7:8, :LANES]
        sactv = sact[...]
        ssg = sigmoid(sactv)
        sconv = sactv * ssg
        bmat, cmat = sconv[:, :state_size], sconv[:, state_size:]
        actv = act[...]
        sg = sigmoid(actv)
        x = actv * sg
        cumv, stepv = cum[...], step[...]
        last = cumv[Q - 1 :, :]
        step_wide = spread(stepv, hot)
        xs = x * step_wide
        xs_ref[...] = xs
        g = gssd[...]

        def row(value):
            return spread(jnp.broadcast_to(jnp.exp(value), (HALO, LANES)), hot)[:1]

        state = sin[...] + row(before_log[...]) * incoming[...]
        adj = dout[...] + row(total_log[0:1, :] - before_log[...] - last) * later[...]
        to_end = spread(jnp.exp(last - cumv), hot)
        u_state = to_end * dot3(bmat, adj, NN)
        ends = row(last) * jnp.sum(adj * state, axis=0, keepdims=True) + jnp.sum(
            xs * u_state, axis=0, keepdims=True
        )
        scores_t = dot3(bmat, cmat, NT)
        later_mask = triangle(False)
        lane = lax.broadcasted_iota(jnp.int32, (Q, LANES), 1)
        st_ref[...] = jnp.zeros_like(st_ref)
        for p in range(act.shape[1] // LANES):
            cols = slice(p * LANES, (p + 1) * LANES)
            right = pair_stack(gssd[:, cols])
            g_high, g_low = right[:Q, :LANES], right[:Q, LANES:]
            twice = jnp.concatenate([g_high, g_high], axis=1)
            pair = xs_ref[:, cols]
            got = []
            for j in range(2):
                h = p * 2 + j
                gap = cumt[h : h + 1, :] - cum[:, h : h + 1]
                decay = jnp.exp(jnp.where(later_mask, gap, -1e30))
                wide = dg(jnp.concatenate(split(scores_t * decay), axis=1), right, NN)
                got.append(wide[:, :LANES] + wide[:, LANES:])
                mine = (lane < LANES // 2) if j == 0 else (lane >= LANES // 2)
                xh, xl = split(jnp.where(mine, pair, 0.0))
                inner = dg(jnp.concatenate([xh, xl], axis=1), twice, NT) + dg(xh, g_low, NT)
                st_ref[...] = st_ref[...] + decay * inner
            u_ref[:, cols] = jnp.where(lane < LANES // 2, got[0], got[1])
        u = u_ref[...] + u_state
        sc = st_ref[...]
        g_scaled = g * spread(jnp.exp(cumv), hot)
        gstates = jnp.concatenate(
            [
                dot3(sc, cmat, NN) + dot3(xs * to_end, adj, NT),
                dot3(sc.T, bmat, NN) + dot3(g_scaled, state, NT),
            ],
            axis=1,
        )
        gsact = gstates * (ssg * (1.0 + sactv * (1.0 - ssg)))
        gact = (step_wide * u + skip * g) * (sg * (1.0 + actv * (1.0 - sg)))
        u_ref[...] = gact
        sext[Q + HALO :, :] = gsact
        small_a[4:5, :] = small_a[4:5, :] + jnp.sum(gact, axis=0, keepdims=True)
        small_b[4:5, :] = small_b[4:5, :] + jnp.sum(gsact, axis=0, keepdims=True)
        direct = gather(x * u, hot)
        flow = gather(g * (y[...] - skip * x), hot) - stepv * direct
        ends_heads = gather(jnp.broadcast_to(ends, (HALO, ends.shape[1])), hot)[:1]
        da = tri_sum(False, flow) + ends_heads
        slope = (direct + rate * da) * sigmoid(step_pre[...] + params[7:8, LANES : 2 * LANES])
        gstep[Q:, :] = slope.astype(BF16)
        small_a[7:8, :LANES] = small_a[7:8, :LANES] + jnp.sum(
            stepv * rate * da, axis=0, keepdims=True
        )
        small_a[7:8, LANES : 2 * LANES] = small_a[7:8, LANES : 2 * LANES] + jnp.sum(
            slope, axis=0, keepdims=True
        )

    @pl.when(c == 0)
    def _():
        halo_send[...] = u_ref[:HALO, :]
        shalo_send[...] = sext[Q + HALO : Q + 2 * HALO, :]

        @pl.when(seq > 0)
        def _():
            halo(halo_send, halo_got, 0).start()
            halo(shalo_send, shalo_got, 2).start()

    @pl.when(c == count)
    def _():
        @pl.when(seq < ns - 1)
        def _():
            halo(halo_send, halo_got, 0).wait_recv()
            halo(shalo_send, shalo_got, 2).wait_recv()
            u_ref[:HALO, :] = halo_got[...]
            sext[Q + HALO : Q + 2 * HALO, :] = shalo_got[...]

        @pl.when(seq == ns - 1)
        def _():
            u_ref[:HALO, :] = jnp.zeros((HALO, u_ref.shape[1]), F32)
            sext[Q + HALO : Q + 2 * HALO, :] = jnp.zeros((HALO, two), F32)

        @pl.when(seq > 0)
        def _():
            halo(halo_send, halo_got, 0).wait_send()
            halo(shalo_send, shalo_got, 2).wait_send()

    @pl.when(c >= 1)
    def _():
        gext[Q:, :] = u_ref[:HALO, :]
        sext[Q : Q + HALO, :] = sext[Q + HALO : Q + 2 * HALO, :]
        pext[:HALO, :] = jnp.where(c == 1, pre_halo[...], pre_prev[...])
        pext[HALO:, :] = pre[...]
        spext[:HALO, :] = jnp.where(c == 1, spre_halo[...], spre_prev[...])
        spext[HALO:, :] = spre[...]

        def conv_back(ext, ext_pre, taps_at, size, sums):
            g = ext[:Q, :]
            total = params[taps_at + taps - 1 : taps_at + taps, :size] * g
            for k in range(taps - 1):
                start = taps - 1 - k
                total = total + params[taps_at + k : taps_at + k + 1, :size] * ext[start : start + Q, :]
            for k in range(taps):
                start = HALO - taps + 1 + k
                sums[k : k + 1, :] = sums[k : k + 1, :] + jnp.sum(
                    g * ext_pre[start : start + Q, :], axis=0, keepdims=True
                )
            return total

        inner = gext.shape[1]
        gin_o[:, :inner] = conv_back(gext, pext, 0, inner, small_a).astype(BF16)
        gin_o[:, inner:] = gstep[:Q, :]
        gin_all[chunk_rows(c - 1), :] = gin_o[...]
        mine = conv_back(sext, spext, 8, two, small_b)
        psum[chunk_rows(c - 1), :] = mine

        @pl.when((c - 1) % n != me)
        def _():
            top = jnp.max(jnp.abs(mine), axis=0, keepdims=True)
            scale = (top * 1.004 + 1e-30).astype(BF16)
            first = pl.multiple_of((c - 1) * (Q + 16), 16)
            psend[pl.ds(first, Q), :] = jnp.exp(mine * (SPAN / scale.astype(F32))).astype(BF16)
            psend[pl.ds(first + Q, 16), :] = jnp.broadcast_to(scale, (16, two))
            to_owner(c - 1).start()

    @pl.when((c >= 0) & (c < count))
    def _():
        gext[:Q, :] = u_ref[...]
        gstep[:Q, :] = gstep[Q:, :]
        sext[:Q, :] = sext[Q + HALO :, :]

    last_step = count + 1
    tail_slot = slots_of(n) - 3
    more = tail_slot - 3

    @pl.when((i >= 1) & (i < last_step))
    def _():
        @pl.loop(3 + (i - 1) * more // count, 3 + i * more // count)
        def _(t):
            slot(t)

    @pl.when(i == last_step)
    def _():
        slot(tail_slot)

        @pl.loop(0, win_o.shape[0] // 256)
        def _(m):
            cols = pl.ds(pl.multiple_of(m * 256, 256), 256)
            win_o[cols, :] = dg(normed[:, cols], gin_all[...], TN)

    for g in range(groups):

        @pl.when(c == min((g + 1) * n + 2, total_chunks))
        def _():
            own = chunk_rows(g * n + me)
            total = psum[own, :]
            for k in range(1, n):
                j = (me + k) % n
                from_other(j, g).wait_recv()
                first = g * (Q + 16)
                scale = pgot[j, first + Q : first + Q + 16, :].astype(F32)[:1] * (1.0 / SPAN)
                total = total + jnp.log(pgot[j, first : first + Q, :].astype(F32)) * scale
            gsb_o[own, :] = total.astype(BF16)
            for k in range(1, n):
                give(k, g, False).start()

    @pl.when(i == last_step)
    def _():
        slot(tail_slot + 1)
        slot(tail_slot + 2)
        for g in range(groups):
            for k in range(1, n):
                give(k, g, True).wait_recv()
        gsb_out[...] = gsb_o[...]
        for g in range(groups):
            for k in range(1, n):
                give(k, g, False).wait_send()
        for k in range(total_chunks):

            @pl.when(k % n != me)
            def _():
                to_owner(k).wait_send()

    @pl.when(i == last_step)
    def _():
        drain()
        code_out[...] = all_ref[...]


def transposed_times(left, right):
    return dg(left, right, TN)


def on_device(
    hidden,
    in_gain,
    proj_gate,
    proj_input,
    proj_states,
    proj_step,
    conv_input,
    conv_input_bias,
    conv_states,
    conv_states_bias,
    step_bias,
    decay_log,
    skip_gain,
    gate_gain,
    proj_output,
    cotangent,
):
    seg_count = lax.axis_size("seq")
    head_index = lax.axis_index("head")
    tokens, width = hidden.shape
    heads = proj_step.shape[1]
    inner = proj_gate.shape[1]
    state_size = conv_states.shape[1] // 2
    head_dim = inner // heads
    row_width = proj_states.shape[0]
    count = tokens // Q

    def pad_heads(value):
        return jnp.pad(value, [(0, 0)] * (value.ndim - 1) + [(0, LANES - heads)])

    n, ns = lax.axis_size("head"), seg_count

    two = 2 * state_size
    fields = [
        (decay_log, LANES),
        (step_bias, LANES),
        (skip_gain, LANES),
        (conv_input_bias, inner),
        (gate_gain, inner),
        (conv_states_bias, two),
        (in_gain, width),
    ]
    used = sum(size for _, size in fields)
    used += -used % 1024
    flat, place = jnp.zeros((used,), F32), 0
    for value, size in fields:
        flat = flat + jnp.pad(value.astype(F32), (place, used - place - value.shape[0]))
        place += size
    vec = flat.reshape(-1, LANES)
    stripe = 256

    def striped(size):
        return pl.BlockSpec((stripe, size), lambda c: (c, 0))

    def fixed(shape, at=0):
        return pl.BlockSpec(shape, lambda c: (at, 0), pipeline_mode=pl.Buffered(1))

    (
        normed, inv_rms, input_pre, gate_pre, grad_ynorm, proj_states_full, normed_halo, input_halo,
    ) = call(
        functools.partial(front_kernel, n, ns),
        (tokens // stripe,),
        [
            (hidden, striped(width)),
            (cotangent, striped(width)),
            (hidden, fixed((16, width), tokens // 16 - 1)),
            (vec, fixed(vec.shape)),
            (proj_input, fixed((width, inner))),
            (proj_gate, fixed((width, inner))),
            (proj_output, fixed((inner, width))),
            (proj_states, fixed((row_width, 2 * state_size))),
        ],
        [
            (sds((tokens, width), BF16), striped(width)),
            (sds((tokens, 1)), striped(1)),
            (sds((tokens, inner)), striped(inner)),
            (sds((tokens, inner)), striped(inner)),
            (sds((tokens, inner)), striped(inner)),
            (sds((width, 2 * state_size), BF16), whole((width, 2 * state_size))),
            (sds((16, width), BF16), whole((16, width))),
            (sds((HALO, inner)), whole((HALO, inner))),
        ],
        scratch=[
            pltpu.VMEM((width, 2 * state_size), BF16),
            pltpu.VMEM((16, width), BF16),
            pltpu.SemaphoreType.DMA((n,)),
            pltpu.SemaphoreType.DMA((n,)),
            pltpu.SemaphoreType.DMA((n,)),
            pltpu.SemaphoreType.DMA((n,)),
            pltpu.SemaphoreType.DMA((2,)),
        ],
        flops=6 * tokens * inner * width,
        collective=6,
    )
    proj_step_tall = pad_heads(proj_step).T
    onehot = jnp.asarray(
        np.arange(LANES)[:, None] == np.arange(inner)[None, :] // head_dim, dtype=BF16
    )
    hot = (onehot, whole((LANES, inner)))
    state_rows = pl.BlockSpec((state_size, inner), lambda c: (c, 0))
    packed_shape = (state_size, inner)
    logs_shape = (HALO, LANES)
    big = GROUP * Q
    (
        act, sact, states_pre, states_halo, step_pre, step, cum, cumt, sin, packed, total_log,
        before_log, params,
    ) = call(
        states_kernel,
        (count // GROUP,),
        [
            (input_pre, rows(inner, big)),
            (input_pre, before(inner, big)),
            (input_halo, whole((HALO, inner))),
            (normed, rows(width, big)),
            (normed_halo, whole((16, width))),
            (proj_step_tall, whole((LANES, width))),
            (vec, whole(vec.shape)),
            (conv_input, whole(conv_input.shape)),
            (conv_states, whole(conv_states.shape)),
            (proj_states_full, whole((width, two))),
            hot,
        ],
        [
            (sds((tokens, inner)), rows(inner, big)),
            (sds((tokens, two)), rows(two, big)),
            (sds((tokens, two)), rows(two, big)),
            (sds((HALO, two)), whole((HALO, two))),
            (sds((tokens, LANES)), rows(LANES, big)),
            (sds((tokens, LANES)), rows(LANES, big)),
            (sds((tokens, LANES)), rows(LANES, big)),
            (sds((tokens, LANES)), rows(LANES, big)),
            (sds((count * state_size, inner)), pl.BlockSpec((GROUP * state_size, inner), lambda c: (c, 0))),
            (sds(packed_shape), whole(packed_shape)),
            (sds((HALO, LANES)), whole((HALO, LANES))),
            (sds((count, 1, LANES)), pl.BlockSpec((GROUP, 1, LANES), lambda c: (c, 0, 0))),
            (sds((16, inner)), whole((16, inner))),
        ],
        scratch=[
            pltpu.VMEM((big + HALO, inner), F32),
            pltpu.VMEM((big + HALO, two), F32),
            pltpu.VMEM((state_size, inner), F32),
            pltpu.VMEM((1, LANES), F32),
        ],
        flops=10 * tokens * inner * state_size,
    )
    par = (params, whole((16, inner)))
    yloc, incoming = call(
        functools.partial(intra_kernel, ns),
        (count // GROUP,),
        [
            (act, rows(inner, big)),
            (sact, rows(two, big)),
            (step, rows(LANES, big)),
            (cum, rows(LANES, big)),
            (cumt, rows(LANES, big)),
            par,
            hot,
            (packed, whole(packed_shape)),
            (total_log, whole(logs_shape)),
        ],
        [
            (sds((tokens, inner)), rows(inner, big)),
            (sds((state_size, inner)), whole((state_size, inner))),
        ],
        scratch=[pltpu.VMEM((big, inner), F32), pltpu.VMEM((state_size, inner), F32)]
        + swap_scratch(ns, (state_size, inner)),
        flops=12 * tokens * inner * Q,
        collective=5,
    )

    half = count // GROUP

    def both(i):
        return jnp.where(i < half, i, 2 * half - 1 - i)

    def fore(i):
        return jnp.minimum(i, half - 1)

    def aft(i):
        return jnp.minimum(2 * half - 1 - i, half - 1)

    def at(size, which, height=big):
        return pl.BlockSpec((height, size), lambda i: (which(i), 0))

    y, ynorm, grad_gate_pre, grad_ssd, dout, packed_back, grad_rows = call(
        functools.partial(middle_kernel, n),
        (2 * half,),
        [
            (yloc, at(inner, fore)),
            (act, at(inner, aft)),
            (sact, at(two, both)),
            (cum, at(LANES, both)),
            (sin, at(inner, fore, GROUP * state_size)),
            (before_log, pl.BlockSpec((GROUP, 1, LANES), lambda i: (fore(i), 0, 0))),
            (incoming, whole((state_size, inner))),
            (gate_pre, at(inner, both)),
            (grad_ynorm, at(inner, both)),
            par,
            hot,
        ],
        [
            (sds((tokens, inner)), at(inner, fore)),
            (sds((tokens, inner), BF16), at(inner, aft)),
            (sds((tokens, inner), BF16), at(inner, aft)),
            (sds((tokens, inner)), at(inner, aft)),
            (sds((count * state_size, inner)), at(inner, aft, GROUP * state_size)),
            (sds(packed_shape), whole(packed_shape)),
            (sds((HALO, inner)), whole((HALO, inner))),
        ],
        scratch=[
            pltpu.VMEM((tokens, inner), F32),
            pltpu.VMEM((HALO, tokens), F32),
            pltpu.VMEM((n, HALO, tokens), F32),
            pltpu.VMEM((state_size, inner), F32),
            pltpu.SemaphoreType.DMA((n,)),
            pltpu.SemaphoreType.DMA((n,)),
        ],
        flops=12 * tokens * inner * state_size,
        collective=3,
    )
    local_proj_gate = transposed_times(normed, grad_gate_pre)
    grad_proj_gate = lax.psum_scatter(
        local_proj_gate, "seq", scatter_dimension=0, tiled=True
    )

    def now(i):
        return jnp.clip(i - 1, 0, count - 1)

    def past(i):
        return jnp.maximum(i - 2, 0)

    def held(size, height=Q):
        return pl.BlockSpec((height, size), lambda i: (now(i), 0))

    def prior(size):
        return pl.BlockSpec((Q, size), lambda i: (past(i), 0))

    def prior_edge(size):
        return pl.BlockSpec(
            (HALO, size), lambda i: (jnp.maximum(past(i) * (Q // HALO) - 1, 0), 0)
        )

    def once(shape):
        return pl.BlockSpec(shape, lambda i: (0, 0), pipeline_mode=pl.Buffered(1))

    dma = pltpu.SemaphoreType.DMA
    groups = count // n
    grad_in_b, grad_states_b, small_a, small_b, branch_code, local_proj_in, local_proj_output = call(
        functools.partial(back_kernel, n, ns),
        (count + 2,),
        [
            (act, held(inner)),
            (sact, held(two)),
            (y, held(inner)),
            (grad_ssd, held(inner)),
            (step, held(LANES)),
            (step_pre, held(LANES)),
            (cum, held(LANES)),
            (cumt, held(LANES)),
            (sin, held(inner, state_size)),
            (dout, held(inner, state_size)),
            (
                before_log,
                pl.BlockSpec((None, 1, LANES), lambda i: (now(i), 0, 0)),
            ),
            (total_log, whole(logs_shape)),
            (incoming, once((state_size, inner))),
            (ynorm, once((tokens, inner))),
            (proj_output, once((inner, width))),
            (packed_back, once(packed_shape)),
            (normed, once((tokens, width))),
            (cotangent, once((tokens, width))),
            par,
            hot,
            (grad_rows, whole((HALO, inner))),
            (input_pre, prior(inner)),
            (input_pre, prior_edge(inner)),
            (input_halo, whole((HALO, inner))),
            (states_pre, prior(two)),
            (states_pre, prior_edge(two)),
            (states_halo, whole((HALO, two))),
        ],
        [
            (sds((tokens, inner + LANES), BF16), prior(inner + LANES)),
            (sds((tokens, two), BF16), whole((tokens, two))),
            (sds((16, inner)), whole((16, inner))),
            (sds((HALO, two)), whole((HALO, two))),
            (sds((tokens, width + LANES), BF16), once((tokens, width + LANES))),
            (sds((width, inner + LANES)), once((width, inner + LANES))),
            (sds((width, inner)), once((width, inner))),
        ],
        scratch=[
            pltpu.VMEM((tokens, inner + LANES), BF16),
            pltpu.VMEM((tokens, two), BF16),
            pltpu.VMEM((2 * Q, LANES), BF16),
            pltpu.VMEM((Q, inner), F32),
            pltpu.VMEM((Q, inner), F32),
            pltpu.VMEM((Q, Q), F32),
            pltpu.VMEM((Q + HALO, inner), F32),
            pltpu.VMEM((2 * Q + HALO, two), F32),
            pltpu.VMEM((Q + HALO, inner), F32),
            pltpu.VMEM((Q + HALO, two), F32),
            pltpu.VMEM((HALO, inner), F32),
            pltpu.VMEM((HALO, inner), F32),
            pltpu.VMEM((HALO, two), F32),
            pltpu.VMEM((HALO, two), F32),
            pltpu.VMEM((tokens, two), F32),
            pltpu.VMEM((count * (Q + 16), two), BF16),
            pltpu.VMEM((n, groups * (Q + 16), two), BF16),
            dma((4,)),
            dma((count,)),
            dma((n, groups)),
            dma((n, groups)),
            dma((n, groups)),
            pltpu.VMEM((state_size, inner), F32),
            *swap_scratch(ns, (state_size, inner)),
            pltpu.VMEM((tokens, width + LANES), BF16),
            *chain_scratch(tokens, width, n),
        ],
        flops=40 * tokens * inner * Q,
        collective=4,
    )
    row_start = head_index * row_width
    own_states = lax.dynamic_update_slice_in_dim(
        jnp.zeros((width, two), BF16), proj_states, row_start, 0
    )
    normed_rows = lax.dynamic_slice_in_dim(normed, row_start, row_width, 1)
    local_proj_states = transposed_times(grad_states_b, normed_rows)
    summed_out = lax.psum_scatter(
        local_proj_output, "seq", scatter_dimension=0, tiled=True
    )
    summed_in = lax.psum_scatter(local_proj_in, "seq", scatter_dimension=0, tiled=True)
    grad_code, sum_a, sum_b, sum_s = reduce_over_heads(
        [
            (grad_gate_pre, proj_gate),
            (grad_in_b, proj_input),
            (grad_in_b, proj_step_tall),
            (grad_states_b, own_states),
        ],
        [NT, NT, NN, NT],
        (None, (0, inner), (inner, inner + LANES), None),
        2,
        (hidden, inv_rms, small_a, small_b, local_proj_states),
    )

    def ones(value):
        return (value, fixed(value.shape))

    def outs(*shape):
        return (sds(shape), fixed(shape))

    (
        result, grad_hidden, grad_proj_output, grad_proj_input, grad_proj_step, grad_proj_states,
        grad_conv_input, grad_conv_states,
    ) = call(
        finish_kernel,
        (tokens // stripe,),
        [
            (branch_code, striped(width + LANES)),
            (grad_code, striped(width + LANES)),
            (hidden, striped(width)),
            (cotangent, striped(width)),
            (inv_rms, striped(1)),
            ones(vec),
            ones(sum_a),
            ones(sum_b),
            ones(sum_s),
            ones(summed_out),
            ones(summed_in),
        ],
        [
            (sds((tokens, width)), striped(width)),
            (sds((tokens, width)), striped(width)),
            outs(width // ns, inner),
            outs(width // ns, inner),
            outs(heads, width // ns),
            outs(two // ns, row_width),
            outs(TAPS, inner),
            outs(TAPS, two),
        ],
        flops=40 * tokens * width,
    )
    return (
        result,
        grad_hidden,
        sum_b[0],
        grad_proj_gate,
        grad_proj_input,
        grad_proj_states.T,
        grad_proj_step.T,
        grad_conv_input,
        sum_a[4],
        grad_conv_states,
        sum_b[12, :two],
        sum_a[7, LANES : LANES + heads],
        sum_a[7, :heads],
        jnp.sum(sum_a[6].reshape(heads, head_dim), axis=1),
        sum_a[5],
        grad_proj_output.T,
    )


def solution(mesh):
    in_specs = (
        P("seq", None),
        P(),
        P(None, "head"),
        P(None, "head"),
        P("head", None),
        P(None, "head"),
        P(None, "head"),
        P("head"),
        P(),
        P(),
        P("head"),
        P("head"),
        P("head"),
        P("head"),
        P("head", None),
        P("seq", None),
    )
    out_specs = (
        P("seq", None),
        P("seq", None),
        P(),
        P("seq", "head"),
        P("seq", "head"),
        P("head", "seq"),
        P("seq", "head"),
        P(None, "head"),
        P("head"),
        P(),
        P(),
        P("head"),
        P("head"),
        P("head"),
        P("head"),
        P("head", "seq"),
    )

    return jax.shard_map(
        on_device, mesh=mesh, in_specs=in_specs, out_specs=out_specs, check_vma=False
    )
```

```python
import functools

import jax
import jax.numpy as jnp
import numpy as np
from jax import lax
from jax.experimental import pallas as pl
from jax.experimental.pallas import tpu as pltpu
from jax.sharding import PartitionSpec as P


DI = 3072
EPS = 1e-05
Q = 128
LANES = 128
HALO = 8
TAPS = 4
GROUP = 2

F32 = jnp.float32
BF16 = jnp.bfloat16
NN = (((1,), (0,)), ((), ()))
NT = (((1,), (1,)), ((), ()))
TN = (((0,), (0,)), ((), ()))
VMEM_LIMIT = 63 * 1024 * 1024
MESH_ID = pl.DeviceIdType.MESH


def dg(left, right, dims):
    return lax.dot_general(left, right, dims, preferred_element_type=F32)


def split(value):
    high = value.astype(BF16)
    return high, (value - high.astype(F32)).astype(BF16)


def dot3(left, right, dims):
    (lh, ll), (rh, rl) = split(left), split(right)
    return dg(lh, rh, dims) + (dg(lh, rl, dims) + dg(ll, rh, dims))


def spread(heads, onehot):
    high, low = split(heads)
    return dg(high, onehot, NN) + dg(low, onehot, NN)


def gather(wide, onehot):
    high, low = split(wide)
    return dg(high, onehot, NT) + dg(low, onehot, NT)


def sigmoid(value):
    return 0.5 * jnp.tanh(0.5 * value) + 0.5


def silu(value):
    return value * sigmoid(value)


def call(kernel, grid, ins, outs, scratch=(), flops=0, collective=None):
    in_specs = [spec for _, spec in ins]
    size = sum(a.size * a.dtype.itemsize for a, _ in ins) + sum(
        s.size * s.dtype.itemsize for s, _ in outs
    )
    return pl.pallas_call(
        kernel,
        grid=grid,
        in_specs=in_specs,
        out_specs=[spec for _, spec in outs],
        out_shape=[shape for shape, _ in outs],
        scratch_shapes=list(scratch),
        cost_estimate=pl.CostEstimate(flops=flops, bytes_accessed=size, transcendentals=0),
        compiler_params=pltpu.CompilerParams(vmem_limit_bytes=VMEM_LIMIT)
        if collective is None
        else pltpu.CompilerParams(
            vmem_limit_bytes=VMEM_LIMIT, collective_id=collective, has_side_effects=True
        ),
    )(*[a for a, _ in ins])


def sds(shape, dtype=F32):
    return jax.ShapeDtypeStruct(shape, dtype)


def rows(width, height=Q):
    return pl.BlockSpec((height, width), lambda c: (c, 0))


def whole(shape):
    return pl.BlockSpec(shape, lambda c: (0,) * len(shape))


def before(width, height):
    return pl.BlockSpec((HALO, width), lambda c: (jnp.maximum(c * (height // HALO) - 1, 0), 0))


def triangle(lower):
    a = lax.broadcasted_iota(jnp.int32, (Q, Q), 0)
    b = lax.broadcasted_iota(jnp.int32, (Q, Q), 1)
    return a >= b if lower else a <= b


def tri_sum(lower, value):
    mask = triangle(lower).astype(BF16)
    high = value.astype(BF16)
    rest = value - high.astype(F32)
    mid = rest.astype(BF16)
    low = (rest - mid.astype(F32)).astype(BF16)
    return dg(mask, high, NN) + (dg(mask, mid, NN) + dg(mask, low, NN))


def conv_act(pre, ext_ref, params, at):
    size = ext_ref.shape[1]
    height = pre.shape[0]
    ext_ref[HALO:, :] = pre
    total = params[at + TAPS : at + TAPS + 1, :size] + params[at + TAPS - 1 : at + TAPS, :size] * pre
    for k in range(TAPS - 1):
        start = HALO - TAPS + 1 + k
        total = total + params[at + k : at + k + 1, :size] * ext_ref[start : start + height, :]
    return total


def line(vec, first, size):
    return jnp.concatenate([vec[r : r + 1, :] for r in range(first, first + size // LANES)], axis=1)


def front_kernel(
    n, ns, hidden, cotangent, tail, vec, proj_input, proj_gate, proj_output, piece,
    normed_o, inv_o, pre_o, gate_o, gyn_o, full_o, nhalo_o, halo_o,
    full, halo, s_sem, r_sem, w_sem, v_sem, h_sem,
):
    c = pl.program_id(0)
    me, seq = lax.axis_index("head"), lax.axis_index("seq")
    height = piece.shape[0]
    short = height // 2
    odd = seq % 2
    last = pl.num_programs(0) - 1

    def slab(j):
        return pl.ds(pl.multiple_of(j * height, height), height)

    def part(j, which):
        return pl.ds(pl.multiple_of(j * height + which * short, short), short)

    def give(k, arriving):
        other = (me + k) % n
        owner = other if arriving else me
        return pltpu.make_async_remote_copy(
            src_ref=piece.at[pl.ds(pl.multiple_of(odd * short, short), short)],
            dst_ref=full.at[part(owner, odd)],
            send_sem=s_sem.at[k],
            recv_sem=r_sem.at[owner],
            device_id={"head": other},
            device_id_type=MESH_ID,
        )

    def swap(k, arriving):
        owner = (me + k) % n
        where = part(owner, 1 - odd if arriving else odd)
        return pltpu.make_async_remote_copy(
            src_ref=full.at[where],
            dst_ref=full.at[where],
            send_sem=w_sem.at[k],
            recv_sem=v_sem.at[k],
            device_id={"seq": seq + 1 - 2 * odd},
            device_id_type=MESH_ID,
        )

    def edge():
        return pltpu.make_async_remote_copy(
            src_ref=tail,
            dst_ref=halo,
            send_sem=h_sem.at[0],
            recv_sem=h_sem.at[1],
            device_id={"seq": (seq + 1) % ns},
            device_id_type=MESH_ID,
        )

    def norm(value):
        value = value.astype(F32)
        inv = lax.rsqrt(jnp.mean(value * value, axis=-1, keepdims=True) + EPS)
        return inv, (value * inv * gain).astype(BF16)

    first = 3 + (2 * pre_o.shape[1] + piece.shape[1]) // LANES
    gain = line(vec, first, hidden.shape[1])
    barrier = pltpu.get_barrier_semaphore()

    @pl.when(c == 0)
    def _():
        greet(n, ns)

    inv, normed = norm(hidden[...])
    inv_o[...] = inv
    normed_o[...] = normed
    pre_o[...] = dg(normed, proj_input[...], NN)

    @pl.when(c == 0)
    def _():
        pl.semaphore_wait(barrier, n + ns - 2)
        for k in range(1, n):
            give(k, False).start()

        @pl.when(seq < ns - 1)
        def _():
            edge().start()

        full[slab(me), :] = piece[...]

    gate_o[...] = dg(normed, proj_gate[...], NN)
    gyn_o[...] = dg(cotangent[...], proj_output[...], NT)

    @pl.when(c == jnp.maximum(last - 1, 0))
    def _():
        for k in range(1, n):
            give(k, True).wait_recv()
            swap(k, False).start()

    @pl.when(c == last)
    def _():
        @pl.when(seq > 0)
        def _():
            edge().wait_recv()

        @pl.when(seq == 0)
        def _():
            halo[...] = jnp.zeros_like(halo)

        before_first = norm(halo[...])[1]
        nhalo_o[...] = before_first
        halo_o[...] = dg(before_first, proj_input[...], NN)[16 - HALO :, :]

        @pl.when(seq < ns - 1)
        def _():
            edge().wait_send()

        for k in range(1, n):
            swap(k, True).wait_recv()
        full_o[...] = full[...]
        for k in range(1, n):
            swap(k, False).wait_send()
            give(k, False).wait_send()


def states_kernel(
    pre, pre_prev, pre_halo, normed, normed_halo, step_w, vec, taps_in, taps_st, full, onehot, *refs
):
    act_o, sact_o, spre_o, shalo_o, spre_step_o, step_o, cum_o, cumt_o, sin_o, dev_o, total_o = refs[:11]
    before_o, params = refs[11:13]
    ext, sext, state, total = refs[13:]
    c = pl.program_id(0)
    state_size = bmat_width(sact_o)
    inner = pre.shape[1]
    two = 2 * state_size
    hot = onehot[...]

    height = pre.shape[0]

    @pl.when(c == 0)
    def _():
        state[...] = jnp.zeros_like(state)
        total[...] = jnp.zeros_like(total)
        params[...] = jnp.zeros_like(params)
        per = inner // LANES
        params[0:TAPS, :] = taps_in[...].astype(F32)
        params[4:5, :] = line(vec, 3, inner)
        params[5:6, :] = line(vec, 3 + per, inner)
        params[6:7, :] = spread(jnp.broadcast_to(vec[2:3, :], (HALO, LANES)), hot)[:1]
        params[7:8, :LANES] = -jnp.exp(vec[0:1, :])
        params[7:8, LANES : 2 * LANES] = vec[1:2, :]
        params[8 : 8 + TAPS, :two] = taps_st[...].astype(F32)
        params[12:13, :two] = line(vec, 3 + 2 * per, two)
        shalo_o[...] = dg(normed_halo[...], full[...], NN)[16 - HALO :, :]
        sext[height:, :] = shalo_o[...]
        ext[:HALO, :] = pre_halo[...]

    @pl.when(c > 0)
    def _():
        ext[:HALO, :] = pre_prev[...]

    sext[:HALO, :] = sext[height:, :]
    spre = dg(normed[...], full[...], NN)
    spre_o[...] = spre
    step_pre = dg(normed[...], step_w[...], NT)
    spre_step_o[...] = step_pre
    act = conv_act(pre[...], ext, params, 0)
    sact = conv_act(spre, sext, params, 8)
    act_o[...] = act
    sact_o[...] = sact
    step = jax.nn.softplus(step_pre + params[7:8, LANES : 2 * LANES])
    step_o[...] = step
    x = silu(act)
    bmat_all = silu(sact[:, :state_size])
    for j in range(height // Q):
        part = slice(j * Q, (j + 1) * Q)
        cum = tri_sum(True, step[part] * params[7:8, :LANES])
        cum_o[part, :] = cum
        cumt_o[part, :] = cum.T
        last = cum[Q - 1 :, :]
        xw = x[part] * spread(step[part] * jnp.exp(last - cum), hot)
        sin_o[j * state_size : (j + 1) * state_size, :] = state[...]
        before_o[j] = total[...]
        decay = spread(jnp.broadcast_to(jnp.exp(last), (HALO, LANES)), hot)[:1]
        state[...] = state[...] * decay + dot3(bmat_all[part], xw, TN)
        total[...] = total[...] + last
    dev_o[...] = state[...]
    total_o[...] = jnp.broadcast_to(total[...], (HALO, LANES))


def bmat_width(ref):
    return ref.shape[1] // 2


def pair_stack(value):
    high, low = split(value)
    return jnp.concatenate(
        [
            jnp.concatenate([high, low], axis=1),
            jnp.concatenate([high, jnp.zeros_like(high)], axis=1),
        ],
        axis=0,
    )


def intra(base, act, sact, step, cum, cumt, params, onehot, out, xs_ref):
    state_size = bmat_width(sact)
    x = silu(act[...])
    xs_ref[...] = x * spread(step[...], onehot[...])
    height = act.shape[0]
    out[pl.ds(pl.multiple_of(base, height), height), :] = x * params[6:7, :]

    @pl.loop(0, height // Q)
    def _(chunk):
        here = pl.ds(pl.multiple_of(chunk * Q, Q), Q)
        there = pl.ds(pl.multiple_of(base + chunk * Q, Q), Q)
        sconv = silu(sact[here, :])
        bmat, cmat = sconv[:, :state_size], sconv[:, state_size:]
        scores = dot3(cmat, bmat, NT)
        causal = triangle(True)
        lane = lax.broadcasted_iota(jnp.int32, (Q, LANES), 1)
        sums, turned = cum.at[here], cumt.at[here]
        for p in range(act.shape[1] // LANES):
            cols = slice(p * LANES, (p + 1) * LANES)
            right = pair_stack(xs_ref[here, cols])
            got = []
            for j in range(2):
                h = p * 2 + j
                gap = sums[:, h : h + 1] - turned[h : h + 1, :]
                mixing = scores * jnp.exp(jnp.where(causal, gap, -1e30))
                wide = dg(jnp.concatenate(split(mixing), axis=1), right, NN)
                got.append(wide[:, :LANES] + wide[:, LANES:])
            out[there, cols] = out[there, cols] + jnp.where(lane < LANES // 2, got[0], got[1])


STREAMS = 8
OPENING = 4
CLOSING = 0
SPAN = 83.0


def encode(value):
    top = jnp.max(jnp.abs(value), axis=1, keepdims=True)
    scale = (top * 1.004 + 1e-30).astype(BF16)
    code = jnp.exp(value * (SPAN / scale.astype(F32))).astype(BF16)
    return code, jnp.broadcast_to(scale, (value.shape[0], LANES))


def decode(block, width):
    scale = block[:, width : width + 1].astype(F32) * (1.0 / SPAN)
    return jnp.log(block[:, :width].astype(F32)) * scale


def swap_states(ns, packed, logs, onehot, out, got_s, got_d, prefix, sems, reverse):
    seq = lax.axis_index("seq")
    own = out.shape[0] // ns

    def rows_of(j):
        return pl.ds(pl.multiple_of(j * own, own), own)

    def remote(src, dst, send, recv, to):
        return pltpu.make_async_remote_copy(
            src_ref=src,
            dst_ref=dst,
            send_sem=send,
            recv_sem=recv,
            device_id={"seq": to},
            device_id_type=MESH_ID,
        )

    def copies(k, arriving):
        other = (seq + k) % ns
        slot = other if arriving else seq
        part = packed.at[rows_of(other)]
        return (
            remote(part, got_s.at[slot], sems.at[0, k], sems.at[1, slot], other),
            remote(logs, got_d.at[slot], sems.at[2, k], sems.at[3, slot], other),
        )

    def answer(k, arriving):
        other = (seq + k) % ns
        slot = other if arriving else seq
        return remote(
            prefix.at[other], out.at[rows_of(slot)], sems.at[4, k], sems.at[5, slot], other
        )

    def begin():
        for k in range(1, ns):
            for copy in copies(k, False):
                copy.start()

    def turn():
        got_s[seq] = packed[rows_of(seq), :]
        got_d[seq] = logs[...]
        for k in range(1, ns):
            for copy in copies(k, True):
                copy.wait_recv()
        carry = jnp.zeros((own, out.shape[1]), F32)
        for i in reversed(range(ns)) if reverse else range(ns):
            prefix[i] = carry
            carry = carry * spread(jnp.exp(got_d[i]), onehot[...])[:1] + got_s[i]
        for k in range(1, ns):
            answer(k, False).start()
        out[rows_of(seq), :] = prefix[seq]

    def end():
        for k in range(1, ns):
            answer(k, True).wait_recv()
        for k in range(1, ns):
            answer(k, False).wait_send()
            for copy in copies(k, False):
                copy.wait_send()

    return begin, turn, end


def swap_scratch(ns, shape):
    own = shape[0] // ns
    return [
        pltpu.VMEM((ns, own, shape[1]), F32),
        pltpu.VMEM((ns, HALO, LANES), F32),
        pltpu.VMEM((ns, own, shape[1]), F32),
        pltpu.SemaphoreType.DMA((6, ns)),
    ]


def put(ref, where, value):
    code, scale = encode(value)
    width = value.shape[1]
    ref[where, :width] = code
    ref[where, width:] = scale


def chain_scratch(tokens, width, n):
    coded = pltpu.VMEM((tokens, width + LANES), BF16)
    return [pltpu.VMEM((tokens, width), F32), coded, coded, coded] + [
        pltpu.SemaphoreType.DMA((STREAMS, n))
    ] * 6


def chains(n, all_ref, part, code, got_r, got_l, s_sem, rr_sem, rl_sem, ar_sem, al_sem, ag_sem):
    me = lax.axis_index("head")
    tokens, width = part.shape
    span = tokens // STREAMS
    rows_own = span // n
    has_right, has_left = me < n - 1, me > 0

    def at(d, h):
        return pl.ds(pl.multiple_of(h * span + d * rows_own, rows_own), rows_own)

    def step(d, h, right):
        return pltpu.make_async_remote_copy(
            src_ref=code.at[at(d, h)],
            dst_ref=(got_r if right else got_l).at[at(d, h)],
            send_sem=s_sem.at[h, d],
            recv_sem=(rr_sem if right else rl_sem).at[h, d],
            device_id={"head": me + 1 if right else me - 1},
            device_id_type=MESH_ID,
        )

    def hand_on(b, h, right):
        return pltpu.make_async_remote_copy(
            src_ref=all_ref.at[at(b, h)],
            dst_ref=all_ref.at[at(b, h)],
            send_sem=(ar_sem if right else al_sem).at[h, b],
            recv_sem=ag_sem.at[h, b],
            device_id={"head": me + 1 if right else me - 1},
            device_id_type=MESH_ID,
        )

    def chain(h, u):
        for right in (True, False):
            d = me + (n - 1 - u) if right else me - (n - 1 - u)
            got = got_r if right else got_l
            inside = d <= n - 1 if right else d >= 0
            fed = has_left if right else has_right

            @pl.when(inside & fed)
            def _():
                step(d, h, right).wait_recv()
                put(code, at(d, h), part[at(d, h), :] + decode(got[at(d, h), :], width))
                step(d, h, right).start()

            @pl.when(inside & jnp.logical_not(fed))
            def _():
                put(code, at(d, h), part[at(d, h), :])
                step(d, h, right).start()

    def finish(h):
        own = at(me, h)

        @pl.when(has_left)
        def _():
            step(me, h, True).wait_recv()
            part[own, :] = part[own, :] + decode(got_r[own, :], width)

        @pl.when(has_right)
        def _():
            step(me, h, False).wait_recv()
            part[own, :] = part[own, :] + decode(got_l[own, :], width)

        put(all_ref, own, part[own, :])

        @pl.when(has_right)
        def _():
            hand_on(me, h, True).start()

        @pl.when(has_left)
        def _():
            hand_on(me, h, False).start()

    def relay(h, s):
        @pl.when(me - s >= 0)
        def _():
            hand_on(me - s, h, True).wait_recv()

            @pl.when(has_right)
            def _():
                hand_on(me - s, h, True).start()

        @pl.when(me + s < n)
        def _():
            hand_on(me + s, h, False).wait_recv()

            @pl.when(has_left)
            def _():
                hand_on(me + s, h, False).start()

    def slot(t):
        for u in range(2 * n - 2, -1, -1):
            h = t - u

            @pl.when((h >= 0) & (h < STREAMS))
            def _():
                if u < n - 1:
                    chain(h, u)
                elif u == n - 1:
                    finish(h)
                else:
                    relay(h, u - n + 1)

    def drain():
        @pl.loop(0, STREAMS)
        def _(h):
            for i in range(n):

                @pl.when(i > me)
                def _():
                    step(i, h, True).wait_send()

                @pl.when(i < me)
                def _():
                    step(i, h, False).wait_send()

                @pl.when(has_right & (i <= me))
                def _():
                    hand_on(i, h, True).wait_send()

                @pl.when(has_left & (i >= me))
                def _():
                    hand_on(i, h, False).wait_send()

    return slot, drain


def slots_of(n):
    return STREAMS - 1 + 2 * n - 1


def greet(n, ns):
    barrier = pltpu.get_barrier_semaphore()
    me, seq = lax.axis_index("head"), lax.axis_index("seq")
    for k in range(1, n):
        pl.semaphore_signal(
            barrier, inc=1, device_id={"head": (me + k) % n}, device_id_type=MESH_ID
        )
    for k in range(1, ns):
        pl.semaphore_signal(
            barrier, inc=1, device_id={"seq": (seq + k) % ns}, device_id_type=MESH_ID
        )
    return barrier


def reduce_kernel(n, ns, dims, cols, *refs):
    terms = len(dims)
    lefts, rights = refs[:terms], refs[terms : 2 * terms]
    refs = refs[2 * terms :]
    hidden_ref, inv_ref, small_a, small_b, states_ref, out_ref, sum_a, sum_b, sum_s = refs[:9]
    slot, drain = chains(n, out_ref, *refs[9:19])
    part = refs[9]
    got_a, got_b, got_s, got_c, mine_b = refs[19:24]
    sa_sem, ra_sem, sb_sem, rb_sem, ss_sem, rs_sem, sc_sem, rc_sem = refs[24:]
    me, seq = lax.axis_index("head"), lax.axis_index("seq")
    tokens, _ = part.shape
    span = tokens // STREAMS
    barrier = greet(n, ns)

    def to_seq(src, dst, ssem, rsem, k):
        return pltpu.make_async_remote_copy(
            src_ref=src,
            dst_ref=dst.at[seq],
            send_sem=ssem.at[k],
            recv_sem=rsem.at[seq],
            device_id={"seq": (seq + k) % ns},
            device_id_type=MESH_ID,
        )

    def from_seq(src, dst, ssem, rsem, k):
        other = (seq + k) % ns
        return pltpu.make_async_remote_copy(
            src_ref=src,
            dst_ref=dst.at[other],
            send_sem=ssem.at[k],
            recv_sem=rsem.at[other],
            device_id={"seq": other},
            device_id_type=MESH_ID,
        )

    def states_at(j):
        own = sum_s.shape[0]
        return states_ref.at[pl.ds(pl.multiple_of(j * own, own), own)]

    def compute(h):
        where = pl.ds(pl.multiple_of(h * span, span), span)
        total = None
        for left, right, dim, col in zip(lefts, rights, dims, cols):
            value = left[where, :] if col is None else left[where, col[0] : col[1]]
            term = dg(value, right[...], dim)
            total = term if total is None else total + term
        part[where, :] = total
        seen = total * (hidden_ref[where, :].astype(F32) * inv_ref[where, :])
        mine_b[0:1, :] = mine_b[0:1, :] + jnp.sum(seen, axis=0, keepdims=True)

    mine_b[...] = jnp.zeros_like(mine_b)
    mine_b[8:16, : small_b.shape[1]] = small_b[...]
    compute(0)
    pl.semaphore_wait(barrier, n + ns - 2)
    for k in range(1, ns):
        to_seq(small_a, got_a, sa_sem, ra_sem, k).start()
        to_seq(states_at((seq + k) % ns), got_s, ss_sem, rs_sem, k).start()

    @pl.loop(0, STREAMS - 1)
    def _(t):
        slot(t)
        compute(t + 1)

    for k in range(1, ns):
        to_seq(mine_b, got_b, sb_sem, rb_sem, k).start()

    @pl.loop(STREAMS - 1, slots_of(n) - 2)
    def _(t):
        slot(t)

    total = small_a[...]
    for k in range(1, ns):
        from_seq(small_a, got_a, sa_sem, ra_sem, k).wait_recv()
        total = total + got_a[(seq + k) % ns]
    sum_a[...] = total
    total = states_at(seq)[...]
    for k in range(1, ns):
        from_seq(states_at(seq), got_s, ss_sem, rs_sem, k).wait_recv()
        total = total + got_s[(seq + k) % ns]
    sum_s[...] = total
    total = mine_b[...]
    for k in range(1, ns):
        from_seq(mine_b, got_b, sb_sem, rb_sem, k).wait_recv()
        total = total + got_b[(seq + k) % ns]
    sum_b[...] = total

    def to_head(k):
        return pltpu.make_async_remote_copy(
            src_ref=sum_b,
            dst_ref=got_c.at[me],
            send_sem=sc_sem.at[k],
            recv_sem=rc_sem.at[me],
            device_id={"head": (me + k) % n},
            device_id_type=MESH_ID,
        )

    def from_head(k):
        other = (me + k) % n
        return pltpu.make_async_remote_copy(
            src_ref=sum_b,
            dst_ref=got_c.at[other],
            send_sem=sc_sem.at[k],
            recv_sem=rc_sem.at[other],
            device_id={"head": other},
            device_id_type=MESH_ID,
        )

    for k in range(1, n):
        to_head(k).start()

    @pl.loop(slots_of(n) - 2, slots_of(n))
    def _(t):
        slot(t)

    total = sum_b[...]
    for k in range(1, n):
        from_head(k).wait_recv()
    for k in range(1, n):
        to_head(k).wait_send()
        total = total + got_c[(me + k) % n]
    sum_b[...] = total
    for k in range(1, ns):
        to_seq(small_a, got_a, sa_sem, ra_sem, k).wait_send()
        to_seq(states_at((seq + k) % ns), got_s, ss_sem, rs_sem, k).wait_send()
        to_seq(mine_b, got_b, sb_sem, rb_sem, k).wait_send()
    drain()


def reduce_over_heads(products, dims, cols, collective, sums):
    n, ns = lax.axis_size("head"), lax.axis_size("seq")
    tokens, width = sums[0].shape
    lefts, rights = [a for a, _ in products], [b for _, b in products]
    dma = pltpu.SemaphoreType.DMA
    small_a = sums[2].shape
    states = (sums[4].shape[0] // ns, sums[4].shape[1])
    out_shape = [sds((tokens, width + LANES), BF16), sds(small_a), sds((16, width)), sds(states)]
    scratch = chain_scratch(tokens, width, n) + [
        pltpu.VMEM((ns, *small_a), F32),
        pltpu.VMEM((ns, 16, width), F32),
        pltpu.VMEM((ns, *states), F32),
        pltpu.VMEM((n, 16, width), F32),
        pltpu.VMEM((16, width), F32),
    ]
    scratch += [dma((ns,))] * 6 + [dma((n,))] * 2
    vmem = pl.BlockSpec(memory_space=pltpu.VMEM)
    return pl.pallas_call(
        functools.partial(reduce_kernel, n, ns, dims, cols),
        in_specs=[vmem] * (len(lefts) + len(rights) + len(sums)),
        out_specs=[vmem] * len(out_shape),
        out_shape=out_shape,
        scratch_shapes=scratch,
        compiler_params=pltpu.CompilerParams(
            collective_id=collective, has_side_effects=True, vmem_limit_bytes=VMEM_LIMIT
        ),
        cost_estimate=pl.CostEstimate(
            flops=2 * tokens * width * sum(a.shape[1] for a in lefts),
            bytes_accessed=100 * tokens * width,
            transcendentals=0,
        ),
        name="reduce_heads",
    )(*lefts, *rights, *sums)


def transposed(value):
    high, wide = value.shape
    value = jnp.concatenate([value, jnp.zeros((-high % LANES, wide), F32)], axis=0)
    return value.T[:, :high]


def finish_kernel(
    branch, code, hidden, cotangent, inv, vec, sum_a, sum_b, sum_s, out_grad,
    result, out, grad_out, grad_states, taps_in, taps_st,
):
    width = out.shape[1]
    inner = taps_in.shape[1]
    gain = line(vec, 3 + (2 * inner + taps_st.shape[1]) // LANES, width)
    resid = hidden[...].astype(F32)
    result[...] = resid + decode(branch[...], width)
    grad = decode(code[...], width) * gain
    scale = inv[...]
    dots = jnp.sum(grad * resid, axis=1, keepdims=True) * (1.0 / width)
    out[...] = (
        cotangent[...].astype(F32) + scale * grad - resid * (scale * scale * scale * dots)
    )

    @pl.when(pl.program_id(0) == 0)
    def _():
        grad_out[...] = out_grad[...]
        grad_states[...] = sum_s[...]
        taps_in[...] = sum_a[:TAPS, :]
        taps_st[...] = sum_b[8 : 8 + TAPS, : taps_st.shape[1]]


def part_kernel(in_grad, grad_in, grad_step):
    inner = grad_in.shape[1]
    grad_in[...] = in_grad[:, :inner]
    grad_step[...] = transposed(in_grad[:, inner:])[: grad_step.shape[0]]


def rows_of_sums(square, cross):
    first = jnp.sum(square, axis=1, keepdims=True)
    second = jnp.sum(cross, axis=1, keepdims=True)
    lane = lax.broadcasted_iota(jnp.int32, (square.shape[0], LANES), 1)
    columns = jnp.where(lane == 0, first, jnp.where(lane == 1, second, 0.0))
    parts = [columns[r : r + Q].T[:HALO] for r in range(0, square.shape[0], Q)]
    return jnp.concatenate(parts, axis=1)


def middle_kernel(
    n, ns, act, sact, step, cum, cumt, sin, before_log, gate, gyn, params, onehot, packed, logs,
    y_o, ynorm_o, gpre_o, gssd_o, dout_o, dev_o, rows_o, incoming_o,
    keep, mine, got, adj, xs_ref, incoming, got_s, got_d, prefix, swap_sems, ssem, rsem,
):
    i = pl.program_id(0)
    half = pl.num_programs(0) // 3
    c = jnp.where(i < half, i, jnp.where(i < 2 * half, i - half, 3 * half - 1 - i))
    me = lax.axis_index("head")
    state_size = bmat_width(sact)
    gain = params[5:6, :]
    height = gate.shape[0]
    where = pl.ds(pl.multiple_of(c * height, height), height)
    begin, turn, end = swap_states(
        ns, packed, logs, onehot, incoming, got_s, got_d, prefix, swap_sems, False
    )

    def copy(k, arriving):
        other = (me + k) % n
        return pltpu.make_async_remote_copy(
            src_ref=mine,
            dst_ref=got.at[other if arriving else me],
            send_sem=ssem.at[k],
            recv_sem=rsem.at[other if arriving else me],
            device_id={"head": other},
            device_id_type=MESH_ID,
        )

    @pl.when(i == 0)
    def _():
        barrier = greet(n, ns)
        pl.semaphore_wait(barrier, n + ns - 2)
        begin()

    @pl.when(i < half)
    def _():
        intra(c * height, act, sact, step, cum, cumt, params, onehot, keep, xs_ref)

    @pl.when(i == half // 2)
    def _():
        turn()

    @pl.when(i == half - 1)
    def _():
        end()
        incoming_o[...] = incoming[...]

    @pl.when((i >= half) & (i < 2 * half))
    def _():
        hot = onehot[...]
        cmat = silu(sact[:, state_size:])
        growth = spread(jnp.exp(cum[...]), hot)
        ahead = []
        for j in range(height // Q):
            part = slice(j * Q, (j + 1) * Q)
            carry = spread(jnp.broadcast_to(jnp.exp(before_log[j]), (HALO, LANES)), hot)[:1]
            state = sin[j * state_size : (j + 1) * state_size, :] + carry * incoming[...]
            ahead.append(dot3(cmat[part], state, NN))
        y = keep[where, :] + growth * jnp.concatenate(ahead, axis=0)
        y_o[...] = y
        keep[where, :] = y
        gated = y * silu(gate[...])
        mine[:, where] = rows_of_sums(gated * gated, gyn[...] * gain * gated)

    @pl.when(i == 2 * half - 1)
    def _():
        for k in range(1, n):
            copy(k, False).start()

    @pl.when(i == 2 * half)
    def _():
        adj[...] = jnp.zeros_like(adj)
        rows_o[...] = jnp.zeros_like(rows_o)
        total = mine[...]
        for k in range(1, n):
            copy(k, True).wait_recv()
        for k in range(1, n):
            copy(k, False).wait_send()
            total = total + got[(me + k) % n]
        mine[...] = total

    @pl.when(i >= 2 * half)
    def _():
        hot = onehot[...]
        cmat = silu(sact[:, state_size:])
        gv = gate[...]
        sg = sigmoid(gv)
        gsilu = gv * sg
        growth = spread(jnp.exp(cum[...]), hot)
        total = mine[:, where]
        blank = jnp.zeros((Q - HALO, Q), F32)
        columns = jnp.concatenate(
            [
                jnp.concatenate([total[:, r : r + Q], blank], axis=0).T
                for r in range(0, height, Q)
            ],
            axis=0,
        )
        inv = lax.rsqrt(columns[:, 0:1] / DI + EPS)
        cross = columns[:, 1:2] / DI
        yv = keep[where, :]
        gated = yv * gsilu
        normed = gated * inv
        ynorm_o[...] = (normed * gain).astype(BF16)
        rows_o[0:1, :] = rows_o[0:1, :] + jnp.sum(gyn[...] * normed, axis=0, keepdims=True)
        ggated = inv * (gyn[...] * gain) - normed * (inv * inv * cross)
        gpre_o[...] = (ggated * yv * sg * (1.0 + gv * (1.0 - sg))).astype(BF16)
        gssd = ggated * gsilu
        gssd_o[...] = gssd
        rows_o[1:2, :] = rows_o[1:2, :] + jnp.sum(gssd * silu(act[...]), axis=0, keepdims=True)
        scaled = gssd * growth
        for j in reversed(range(height // Q)):
            part = slice(j * Q, (j + 1) * Q)
            dout_o[j * state_size : (j + 1) * state_size, :] = adj[...]
            last = cum[(j + 1) * Q - 1 : (j + 1) * Q, :]
            decay = spread(jnp.broadcast_to(jnp.exp(last), (HALO, LANES)), hot)[:1]
            adj[...] = adj[...] * decay + dot3(cmat[part], scaled[part], TN)

    @pl.when(i == 3 * half - 1)
    def _():
        dev_o[...] = adj[...]


def back_kernel(
    n, ns, act, sact, y, gssd, step, step_pre, cum, cumt, sin, dout, before_log, total_log, incoming,
    ynorm, proj_output, packed, normed_far, cotangent_far,
    params, onehot, rows_in, pre, pre_prev, pre_halo, spre, spre_prev, spre_halo,
    gin_o, gsb_out, small_a, small_b, code_far, win_far, wout_far,
    gin_all, gsb_o, gstep, xs_ref, u_ref, st_ref, gext, sext, pext, spext, halo_send, halo_got, shalo_send, shalo_got,
    psum, psend, pgot, h_sem, p_send, p_recv, g_send, g_recv,
    later, got_states, got_decays, prefix, swap_sems, normed, cotangent, win_o, wout_o, c_sem,
    all_ref, part, *chain_refs,
):
    load_cotangent = pltpu.make_async_copy(cotangent_far, cotangent, c_sem.at[0])
    load_normed = pltpu.make_async_copy(normed_far, normed, c_sem.at[1])
    save_out = pltpu.make_async_copy(wout_o, wout_far, c_sem.at[2])
    save_in = pltpu.make_async_copy(win_o, win_far, c_sem.at[3])
    save_code = pltpu.make_async_copy(all_ref, code_far, c_sem.at[4])
    i = pl.program_id(0)
    c = i - 1
    count = pl.num_programs(0) - 2
    total_chunks = psum.shape[0] // Q
    begin, turn, end = swap_states(
        ns, packed, total_log, onehot, later, got_states, got_decays, prefix, swap_sems, True
    )
    slot, drain = chains(n, all_ref, part, *chain_refs)
    span = part.shape[0] // STREAMS
    groups = total_chunks // n
    taps = TAPS
    me, seq = lax.axis_index("head"), lax.axis_index("seq")
    state_size = bmat_width(sact)
    two = 2 * state_size

    def halo(src, dst, k):
        return pltpu.make_async_remote_copy(
            src_ref=src,
            dst_ref=dst,
            send_sem=h_sem.at[k],
            recv_sem=h_sem.at[k + 1],
            device_id={"seq": (seq + ns - 1) % ns},
            device_id_type=MESH_ID,
        )

    def chunk_rows(k):
        return pl.ds(pl.multiple_of(k * Q, Q), Q)

    def code_rows(k):
        return pl.ds(pl.multiple_of(k * (Q + 16), 16), Q + 16)

    def to_owner(k):
        return pltpu.make_async_remote_copy(
            src_ref=psend.at[code_rows(k)],
            dst_ref=pgot.at[me, code_rows(k // n)],
            send_sem=p_send.at[k],
            recv_sem=p_recv.at[me, k // n],
            device_id={"head": k % n},
            device_id_type=MESH_ID,
        )

    def from_other(j, g):
        return pltpu.make_async_remote_copy(
            src_ref=psend.at[code_rows(g)],
            dst_ref=pgot.at[j, code_rows(g)],
            send_sem=p_send.at[g],
            recv_sem=p_recv.at[j, g],
            device_id={"head": j},
            device_id_type=MESH_ID,
        )

    def give(k, g, arriving):
        other = (me + k) % n
        owner = other if arriving else me
        where = chunk_rows(g * n + owner)
        return pltpu.make_async_remote_copy(
            src_ref=gsb_o.at[where],
            dst_ref=gsb_o.at[where],
            send_sem=g_send.at[k, g],
            recv_sem=g_recv.at[owner, g],
            device_id={"head": other},
            device_id_type=MESH_ID,
        )

    @pl.when(i == 0)
    def _():
        barrier = greet(n, ns)
        load_cotangent.start()
        load_normed.start()
        small_a[...] = jnp.zeros_like(small_a)
        small_b[...] = jnp.zeros_like(small_b)
        small_a[5:7, :] = rows_in[0:2, :]

        def compute(h):
            where = pl.ds(pl.multiple_of(h * span, span), span)
            part[where, :] = dg(ynorm[where, :], proj_output[...], NN)

        compute(0)
        pl.semaphore_wait(barrier, n + ns - 2)
        begin()

        @pl.loop(0, 2)
        def _(t):
            slot(t)
            compute(t + 1)

        def product(m):
            cols = pl.ds(pl.multiple_of(m * 256, 256), 256)
            wout_o[cols, :] = dg(cotangent[:, cols], ynorm[...], TN)

        tiles = wout_o.shape[0] // 256

        @pl.loop(3, STREAMS)
        def _(h):
            compute(h)

        load_cotangent.wait()

        @pl.loop(0, tiles // 2)
        def _(m):
            product(m)

        turn()

        @pl.loop(2, OPENING - 1)
        def _(t):
            slot(t)

        @pl.loop(tiles // 2, tiles)
        def _(m):
            product(m)

        save_out.start()
        slot(OPENING - 1)
        end()

    @pl.when((c >= 0) & (c < count))
    def _():
        hot = onehot[...]
        skip = params[6:7, :]
        rate = params[7:8, :LANES]
        sactv = sact[...]
        ssg = sigmoid(sactv)
        sconv = sactv * ssg
        bmat, cmat = sconv[:, :state_size], sconv[:, state_size:]
        actv = act[...]
        sg = sigmoid(actv)
        x = actv * sg
        cumv, stepv = cum[...], step[...]
        last = cumv[Q - 1 :, :]
        step_wide = spread(stepv, hot)
        xs = x * step_wide
        xs_ref[...] = xs
        g = gssd[...]

        def row(value):
            return spread(jnp.broadcast_to(jnp.exp(value), (HALO, LANES)), hot)[:1]

        state = sin[...] + row(before_log[...]) * incoming[...]
        adj = dout[...] + row(total_log[0:1, :] - before_log[...] - last) * later[...]
        to_end = spread(jnp.exp(last - cumv), hot)
        u_state = to_end * dot3(bmat, adj, NN)
        ends = row(last) * jnp.sum(adj * state, axis=0, keepdims=True) + jnp.sum(
            xs * u_state, axis=0, keepdims=True
        )
        scores_t = dot3(bmat, cmat, NT)
        later_mask = triangle(False)
        lane = lax.broadcasted_iota(jnp.int32, (Q, LANES), 1)
        st_ref[...] = jnp.zeros_like(st_ref)
        for p in range(act.shape[1] // LANES):
            cols = slice(p * LANES, (p + 1) * LANES)
            right = pair_stack(gssd[:, cols])
            g_high, g_low = right[:Q, :LANES], right[:Q, LANES:]
            twice = jnp.concatenate([g_high, g_high], axis=1)
            pair = xs_ref[:, cols]
            got = []
            for j in range(2):
                h = p * 2 + j
                gap = cumt[h : h + 1, :] - cum[:, h : h + 1]
                decay = jnp.exp(jnp.where(later_mask, gap, -1e30))
                wide = dg(jnp.concatenate(split(scores_t * decay), axis=1), right, NN)
                got.append(wide[:, :LANES] + wide[:, LANES:])
                mine = (lane < LANES // 2) if j == 0 else (lane >= LANES // 2)
                xh, xl = split(jnp.where(mine, pair, 0.0))
                inner = dg(jnp.concatenate([xh, xl], axis=1), twice, NT) + dg(xh, g_low, NT)
                st_ref[...] = st_ref[...] + decay * inner
            u_ref[:, cols] = jnp.where(lane < LANES // 2, got[0], got[1])
        u = u_ref[...] + u_state
        sc = st_ref[...]
        g_scaled = g * spread(jnp.exp(cumv), hot)
        gstates = jnp.concatenate(
            [
                dot3(sc, cmat, NN) + dot3(xs * to_end, adj, NT),
                dot3(sc.T, bmat, NN) + dot3(g_scaled, state, NT),
            ],
            axis=1,
        )
        gsact = gstates * (ssg * (1.0 + sactv * (1.0 - ssg)))
        gact = (step_wide * u + skip * g) * (sg * (1.0 + actv * (1.0 - sg)))
        u_ref[...] = gact
        sext[Q + HALO :, :] = gsact
        small_a[4:5, :] = small_a[4:5, :] + jnp.sum(gact, axis=0, keepdims=True)
        small_b[4:5, :] = small_b[4:5, :] + jnp.sum(gsact, axis=0, keepdims=True)
        direct = gather(x * u, hot)
        flow = gather(g * (y[...] - skip * x), hot) - stepv * direct
        ends_heads = gather(jnp.broadcast_to(ends, (HALO, ends.shape[1])), hot)[:1]
        da = tri_sum(False, flow) + ends_heads
        slope = (direct + rate * da) * sigmoid(step_pre[...] + params[7:8, LANES : 2 * LANES])
        gstep[Q:, :] = slope.astype(BF16)
        small_a[7:8, :LANES] = small_a[7:8, :LANES] + jnp.sum(
            stepv * rate * da, axis=0, keepdims=True
        )
        small_a[7:8, LANES : 2 * LANES] = small_a[7:8, LANES : 2 * LANES] + jnp.sum(
            slope, axis=0, keepdims=True
        )

    @pl.when(c == 0)
    def _():
        halo_send[...] = u_ref[:HALO, :]
        shalo_send[...] = sext[Q + HALO : Q + 2 * HALO, :]

        @pl.when(seq > 0)
        def _():
            halo(halo_send, halo_got, 0).start()
            halo(shalo_send, shalo_got, 2).start()

    @pl.when(c == count)
    def _():
        @pl.when(seq < ns - 1)
        def _():
            halo(halo_send, halo_got, 0).wait_recv()
            halo(shalo_send, shalo_got, 2).wait_recv()
            u_ref[:HALO, :] = halo_got[...]
            sext[Q + HALO : Q + 2 * HALO, :] = shalo_got[...]

        @pl.when(seq == ns - 1)
        def _():
            u_ref[:HALO, :] = jnp.zeros((HALO, u_ref.shape[1]), F32)
            sext[Q + HALO : Q + 2 * HALO, :] = jnp.zeros((HALO, two), F32)

        @pl.when(seq > 0)
        def _():
            halo(halo_send, halo_got, 0).wait_send()
            halo(shalo_send, shalo_got, 2).wait_send()

    @pl.when(c >= 1)
    def _():
        gext[Q:, :] = u_ref[:HALO, :]
        sext[Q : Q + HALO, :] = sext[Q + HALO : Q + 2 * HALO, :]
        pext[:HALO, :] = jnp.where(c == 1, pre_halo[...], pre_prev[...])
        pext[HALO:, :] = pre[...]
        spext[:HALO, :] = jnp.where(c == 1, spre_halo[...], spre_prev[...])
        spext[HALO:, :] = spre[...]

        def conv_back(ext, ext_pre, taps_at, size, sums):
            g = ext[:Q, :]
            total = params[taps_at + taps - 1 : taps_at + taps, :size] * g
            for k in range(taps - 1):
                start = taps - 1 - k
                total = total + params[taps_at + k : taps_at + k + 1, :size] * ext[start : start + Q, :]
            for k in range(taps):
                start = HALO - taps + 1 + k
                sums[k : k + 1, :] = sums[k : k + 1, :] + jnp.sum(
                    g * ext_pre[start : start + Q, :], axis=0, keepdims=True
                )
            return total

        inner = gext.shape[1]
        gin_o[:, :inner] = conv_back(gext, pext, 0, inner, small_a).astype(BF16)
        gin_o[:, inner:] = gstep[:Q, :]
        gin_all[chunk_rows(c - 1), :] = gin_o[...]
        mine = conv_back(sext, spext, 8, two, small_b)
        psum[chunk_rows(c - 1), :] = mine

        @pl.when((c - 1) % n != me)
        def _():
            top = jnp.max(jnp.abs(mine), axis=0, keepdims=True)
            scale = (top * 1.004 + 1e-30).astype(BF16)
            first = pl.multiple_of((c - 1) * (Q + 16), 16)
            psend[pl.ds(first, Q), :] = jnp.exp(mine * (SPAN / scale.astype(F32))).astype(BF16)
            psend[pl.ds(first + Q, 16), :] = jnp.broadcast_to(scale, (16, two))
            to_owner(c - 1).start()

    @pl.when((c >= 0) & (c < count))
    def _():
        gext[:Q, :] = u_ref[...]
        gstep[:Q, :] = gstep[Q:, :]
        sext[:Q, :] = sext[Q + HALO :, :]

    last_step = count + 1
    tail_slot = slots_of(n) - CLOSING
    more = tail_slot - OPENING

    @pl.when((i >= 1) & (i < last_step))
    def _():
        @pl.loop(OPENING + (i - 1) * more // count, OPENING + i * more // count)
        def _(t):
            slot(t)

    @pl.when(i == last_step)
    def _():
        @pl.loop(tail_slot, tail_slot + CLOSING // 2)
        def _(t):
            slot(t)

        load_normed.wait()

        @pl.loop(0, win_o.shape[0] // 256)
        def _(m):
            cols = pl.ds(pl.multiple_of(m * 256, 256), 256)
            win_o[cols, :] = dg(normed[:, cols], gin_all[...], TN)

        save_in.start()

    for g in range(groups):

        @pl.when(c == min((g + 1) * n + 2, total_chunks))
        def _():
            own = chunk_rows(g * n + me)
            total = psum[own, :]
            for k in range(1, n):
                j = (me + k) % n
                from_other(j, g).wait_recv()
                first = g * (Q + 16)
                scale = pgot[j, first + Q : first + Q + 16, :].astype(F32)[:1] * (1.0 / SPAN)
                total = total + jnp.log(pgot[j, first : first + Q, :].astype(F32)) * scale
            gsb_o[own, :] = total.astype(BF16)
            for k in range(1, n):
                give(k, g, False).start()

    @pl.when(i == last_step)
    def _():
        @pl.loop(tail_slot + CLOSING // 2, tail_slot + CLOSING)
        def _(t):
            slot(t)

        save_code.start()
        for g in range(groups):
            for k in range(1, n):
                give(k, g, True).wait_recv()
        gsb_out[...] = gsb_o[...]
        for g in range(groups):
            for k in range(1, n):
                give(k, g, False).wait_send()
        for k in range(total_chunks):

            @pl.when(k % n != me)
            def _():
                to_owner(k).wait_send()

    @pl.when(i == last_step)
    def _():
        drain()
        save_code.wait()
        save_out.wait()
        save_in.wait()


def transposed_times(left, right):
    return dg(left, right, TN)


def on_device(
    hidden,
    in_gain,
    proj_gate,
    proj_input,
    proj_states,
    proj_step,
    conv_input,
    conv_input_bias,
    conv_states,
    conv_states_bias,
    step_bias,
    decay_log,
    skip_gain,
    gate_gain,
    proj_output,
    cotangent,
):
    seg_count = lax.axis_size("seq")
    head_index = lax.axis_index("head")
    tokens, width = hidden.shape
    heads = proj_step.shape[1]
    inner = proj_gate.shape[1]
    state_size = conv_states.shape[1] // 2
    head_dim = inner // heads
    row_width = proj_states.shape[0]
    count = tokens // Q

    def pad_heads(value):
        return jnp.pad(value, [(0, 0)] * (value.ndim - 1) + [(0, LANES - heads)])

    n, ns = lax.axis_size("head"), seg_count

    two = 2 * state_size
    fields = [
        (decay_log, LANES),
        (step_bias, LANES),
        (skip_gain, LANES),
        (conv_input_bias, inner),
        (gate_gain, inner),
        (conv_states_bias, two),
        (in_gain, width),
    ]
    used = sum(size for _, size in fields)
    used += -used % 1024
    flat, place = jnp.zeros((used,), F32), 0
    for value, size in fields:
        flat = flat + jnp.pad(value.astype(F32), (place, used - place - value.shape[0]))
        place += size
    vec = flat.reshape(-1, LANES)
    stripe = 256

    def striped(size):
        return pl.BlockSpec((stripe, size), lambda c: (c, 0))

    def fixed(shape, at=0):
        return pl.BlockSpec(shape, lambda c: (at, 0), pipeline_mode=pl.Buffered(1))

    (
        normed, inv_rms, input_pre, gate_pre, grad_ynorm, proj_states_full, normed_halo, input_halo,
    ) = call(
        functools.partial(front_kernel, n, ns),
        (tokens // stripe,),
        [
            (hidden, striped(width)),
            (cotangent, striped(width)),
            (hidden, fixed((16, width), tokens // 16 - 1)),
            (vec, fixed(vec.shape)),
            (proj_input, fixed((width, inner))),
            (proj_gate, fixed((width, inner))),
            (proj_output, fixed((inner, width))),
            (proj_states, fixed((row_width, 2 * state_size))),
        ],
        [
            (sds((tokens, width), BF16), striped(width)),
            (sds((tokens, 1)), striped(1)),
            (sds((tokens, inner)), striped(inner)),
            (sds((tokens, inner)), striped(inner)),
            (sds((tokens, inner)), striped(inner)),
            (sds((width, 2 * state_size), BF16), whole((width, 2 * state_size))),
            (sds((16, width), BF16), whole((16, width))),
            (sds((HALO, inner)), whole((HALO, inner))),
        ],
        scratch=[
            pltpu.VMEM((width, 2 * state_size), BF16),
            pltpu.VMEM((16, width), BF16),
            pltpu.SemaphoreType.DMA((n,)),
            pltpu.SemaphoreType.DMA((n,)),
            pltpu.SemaphoreType.DMA((n,)),
            pltpu.SemaphoreType.DMA((n,)),
            pltpu.SemaphoreType.DMA((2,)),
        ],
        flops=6 * tokens * inner * width,
        collective=6,
    )
    proj_step_tall = pad_heads(proj_step).T
    onehot = jnp.asarray(
        np.arange(LANES)[:, None] == np.arange(inner)[None, :] // head_dim, dtype=BF16
    )
    hot = (onehot, whole((LANES, inner)))
    state_rows = pl.BlockSpec((state_size, inner), lambda c: (c, 0))
    packed_shape = (state_size, inner)
    logs_shape = (HALO, LANES)
    big = GROUP * Q
    (
        act, sact, states_pre, states_halo, step_pre, step, cum, cumt, sin, packed, total_log,
        before_log, params,
    ) = call(
        states_kernel,
        (count // GROUP,),
        [
            (input_pre, rows(inner, big)),
            (input_pre, before(inner, big)),
            (input_halo, whole((HALO, inner))),
            (normed, rows(width, big)),
            (normed_halo, whole((16, width))),
            (proj_step_tall, whole((LANES, width))),
            (vec, whole(vec.shape)),
            (conv_input, whole(conv_input.shape)),
            (conv_states, whole(conv_states.shape)),
            (proj_states_full, whole((width, two))),
            hot,
        ],
        [
            (sds((tokens, inner)), rows(inner, big)),
            (sds((tokens, two)), rows(two, big)),
            (sds((tokens, two)), rows(two, big)),
            (sds((HALO, two)), whole((HALO, two))),
            (sds((tokens, LANES)), rows(LANES, big)),
            (sds((tokens, LANES)), rows(LANES, big)),
            (sds((tokens, LANES)), rows(LANES, big)),
            (sds((tokens, LANES)), rows(LANES, big)),
            (sds((count * state_size, inner)), pl.BlockSpec((GROUP * state_size, inner), lambda c: (c, 0))),
            (sds(packed_shape), whole(packed_shape)),
            (sds((HALO, LANES)), whole((HALO, LANES))),
            (sds((count, 1, LANES)), pl.BlockSpec((GROUP, 1, LANES), lambda c: (c, 0, 0))),
            (sds((16, inner)), whole((16, inner))),
        ],
        scratch=[
            pltpu.VMEM((big + HALO, inner), F32),
            pltpu.VMEM((big + HALO, two), F32),
            pltpu.VMEM((state_size, inner), F32),
            pltpu.VMEM((1, LANES), F32),
        ],
        flops=10 * tokens * inner * state_size,
    )
    par = (params, whole((16, inner)))
    half = count // GROUP

    def zero(i):
        return jnp.minimum(i, half - 1)

    def one(i):
        return jnp.clip(i - half, 0, half - 1)

    def two_(i):
        return jnp.minimum(3 * half - 1 - i, half - 1)

    def both(i):
        return jnp.where(i < 2 * half, one(i), two_(i))

    def ends(i):
        return jnp.where(i < half, i, two_(i))

    def every(i):
        return jnp.where(i < half, i, both(i))

    def at(size, which, height=big):
        return pl.BlockSpec((height, size), lambda i: (which(i), 0))

    y, ynorm, grad_gate_pre, grad_ssd, dout, packed_back, grad_rows, incoming = call(
        functools.partial(middle_kernel, n, ns),
        (3 * half,),
        [
            (act, at(inner, ends)),
            (sact, at(two, every)),
            (step, at(LANES, zero)),
            (cum, at(LANES, every)),
            (cumt, at(LANES, zero)),
            (sin, at(inner, one, GROUP * state_size)),
            (before_log, pl.BlockSpec((GROUP, 1, LANES), lambda i: (one(i), 0, 0))),
            (gate_pre, at(inner, both)),
            (grad_ynorm, at(inner, both)),
            par,
            hot,
            (packed, whole(packed_shape)),
            (total_log, whole(logs_shape)),
        ],
        [
            (sds((tokens, inner)), at(inner, one)),
            (sds((tokens, inner), BF16), at(inner, two_)),
            (sds((tokens, inner), BF16), at(inner, two_)),
            (sds((tokens, inner)), at(inner, two_)),
            (sds((count * state_size, inner)), at(inner, two_, GROUP * state_size)),
            (sds(packed_shape), whole(packed_shape)),
            (sds((HALO, inner)), whole((HALO, inner))),
            (sds((state_size, inner)), whole((state_size, inner))),
        ],
        scratch=[
            pltpu.VMEM((tokens, inner), F32),
            pltpu.VMEM((HALO, tokens), F32),
            pltpu.VMEM((n, HALO, tokens), F32),
            pltpu.VMEM((state_size, inner), F32),
            pltpu.VMEM((big, inner), F32),
            pltpu.VMEM((state_size, inner), F32),
            *swap_scratch(ns, (state_size, inner)),
            pltpu.SemaphoreType.DMA((n,)),
            pltpu.SemaphoreType.DMA((n,)),
        ],
        flops=24 * tokens * inner * state_size,
        collective=3,
    )
    local_proj_gate = transposed_times(normed, grad_gate_pre)
    grad_proj_gate = lax.psum_scatter(
        local_proj_gate, "seq", scatter_dimension=0, tiled=True
    )

    def now(i):
        return jnp.clip(i - 1, 0, count - 1)

    def past(i):
        return jnp.maximum(i - 2, 0)

    def held(size, height=Q):
        return pl.BlockSpec((height, size), lambda i: (now(i), 0))

    def prior(size):
        return pl.BlockSpec((Q, size), lambda i: (past(i), 0))

    def prior_edge(size):
        return pl.BlockSpec(
            (HALO, size), lambda i: (jnp.maximum(past(i) * (Q // HALO) - 1, 0), 0)
        )

    far = pl.BlockSpec(memory_space=pl.ANY)

    def once(shape):
        return pl.BlockSpec(shape, lambda i: (0, 0), pipeline_mode=pl.Buffered(1))

    dma = pltpu.SemaphoreType.DMA
    groups = count // n
    grad_in_b, grad_states_b, small_a, small_b, branch_code, local_proj_in, local_proj_output = call(
        functools.partial(back_kernel, n, ns),
        (count + 2,),
        [
            (act, held(inner)),
            (sact, held(two)),
            (y, held(inner)),
            (grad_ssd, held(inner)),
            (step, held(LANES)),
            (step_pre, held(LANES)),
            (cum, held(LANES)),
            (cumt, held(LANES)),
            (sin, held(inner, state_size)),
            (dout, held(inner, state_size)),
            (
                before_log,
                pl.BlockSpec((None, 1, LANES), lambda i: (now(i), 0, 0)),
            ),
            (total_log, whole(logs_shape)),
            (incoming, once((state_size, inner))),
            (ynorm, once((tokens, inner))),
            (proj_output, once((inner, width))),
            (packed_back, once(packed_shape)),
            (normed, far),
            (cotangent, far),
            par,
            hot,
            (grad_rows, whole((HALO, inner))),
            (input_pre, prior(inner)),
            (input_pre, prior_edge(inner)),
            (input_halo, whole((HALO, inner))),
            (states_pre, prior(two)),
            (states_pre, prior_edge(two)),
            (states_halo, whole((HALO, two))),
        ],
        [
            (sds((tokens, inner + LANES), BF16), prior(inner + LANES)),
            (sds((tokens, two), BF16), whole((tokens, two))),
            (sds((16, inner)), whole((16, inner))),
            (sds((HALO, two)), whole((HALO, two))),
            (sds((tokens, width + LANES), BF16), far),
            (sds((width, inner + LANES)), far),
            (sds((width, inner)), far),
        ],
        scratch=[
            pltpu.VMEM((tokens, inner + LANES), BF16),
            pltpu.VMEM((tokens, two), BF16),
            pltpu.VMEM((2 * Q, LANES), BF16),
            pltpu.VMEM((Q, inner), F32),
            pltpu.VMEM((Q, inner), F32),
            pltpu.VMEM((Q, Q), F32),
            pltpu.VMEM((Q + HALO, inner), F32),
            pltpu.VMEM((2 * Q + HALO, two), F32),
            pltpu.VMEM((Q + HALO, inner), F32),
            pltpu.VMEM((Q + HALO, two), F32),
            pltpu.VMEM((HALO, inner), F32),
            pltpu.VMEM((HALO, inner), F32),
            pltpu.VMEM((HALO, two), F32),
            pltpu.VMEM((HALO, two), F32),
            pltpu.VMEM((tokens, two), F32),
            pltpu.VMEM((count * (Q + 16), two), BF16),
            pltpu.VMEM((n, groups * (Q + 16), two), BF16),
            dma((4,)),
            dma((count,)),
            dma((n, groups)),
            dma((n, groups)),
            dma((n, groups)),
            pltpu.VMEM((state_size, inner), F32),
            *swap_scratch(ns, (state_size, inner)),
            pltpu.VMEM((tokens, width), BF16),
            pltpu.VMEM((tokens, width), BF16),
            pltpu.VMEM((width, inner + LANES), F32),
            pltpu.VMEM((width, inner), F32),
            dma((5,)),
            pltpu.VMEM((tokens, width + LANES), BF16),
            *chain_scratch(tokens, width, n),
        ],
        flops=40 * tokens * inner * Q,
        collective=4,
    )
    row_start = head_index * row_width
    own_states = lax.dynamic_update_slice_in_dim(
        jnp.zeros((width, two), BF16), proj_states, row_start, 0
    )
    normed_rows = lax.dynamic_slice_in_dim(normed, row_start, row_width, 1)
    local_proj_states = transposed_times(grad_states_b, normed_rows)
    summed_out = lax.psum_scatter(
        local_proj_output, "seq", scatter_dimension=0, tiled=True
    )
    summed_in = lax.psum_scatter(local_proj_in, "seq", scatter_dimension=0, tiled=True)
    grad_code, sum_a, sum_b, sum_s = reduce_over_heads(
        [
            (grad_gate_pre, proj_gate),
            (grad_in_b, proj_input),
            (grad_in_b, proj_step_tall),
            (grad_states_b, own_states),
        ],
        [NT, NT, NN, NT],
        (None, (0, inner), (inner, inner + LANES), None),
        2,
        (hidden, inv_rms, small_a, small_b, local_proj_states),
    )

    def ones(value):
        return (value, fixed(value.shape))

    def outs(*shape):
        return (sds(shape), fixed(shape))

    (
        result, grad_hidden, grad_proj_output, grad_proj_states, grad_conv_input, grad_conv_states,
    ) = call(
        finish_kernel,
        (tokens // stripe,),
        [
            (branch_code, striped(width + LANES)),
            (grad_code, striped(width + LANES)),
            (hidden, striped(width)),
            (cotangent, striped(width)),
            (inv_rms, striped(1)),
            ones(vec),
            ones(sum_a),
            ones(sum_b),
            ones(sum_s),
            ones(summed_out),
        ],
        [
            (sds((tokens, width)), striped(width)),
            (sds((tokens, width)), striped(width)),
            outs(width // ns, inner),
            outs(two // ns, row_width),
            outs(TAPS, inner),
            outs(TAPS, two),
        ],
        flops=40 * tokens * width,
    )
    grad_proj_input, grad_proj_step = call(
        part_kernel, (1,), [ones(summed_in)], [outs(width // ns, inner), outs(heads, width // ns)]
    )
    return (
        result,
        grad_hidden,
        sum_b[0],
        grad_proj_gate,
        grad_proj_input,
        grad_proj_states.T,
        grad_proj_step.T,
        grad_conv_input,
        sum_a[4],
        grad_conv_states,
        sum_b[12, :two],
        sum_a[7, LANES : LANES + heads],
        sum_a[7, :heads],
        jnp.sum(sum_a[6].reshape(heads, head_dim), axis=1),
        sum_a[5],
        grad_proj_output.T,
    )


def solution(mesh):
    in_specs = (
        P("seq", None),
        P(),
        P(None, "head"),
        P(None, "head"),
        P("head", None),
        P(None, "head"),
        P(None, "head"),
        P("head"),
        P(),
        P(),
        P("head"),
        P("head"),
        P("head"),
        P("head"),
        P("head", None),
        P("seq", None),
    )
    out_specs = (
        P("seq", None),
        P("seq", None),
        P(),
        P("seq", "head"),
        P("seq", "head"),
        P("head", "seq"),
        P("seq", "head"),
        P(None, "head"),
        P("head"),
        P(),
        P(),
        P("head"),
        P("head"),
        P("head"),
        P("head"),
        P("head", "seq"),
    )

    return jax.shard_map(
        on_device, mesh=mesh, in_specs=in_specs, out_specs=out_specs, check_vma=False
    )
```

```python
import functools

import jax
import jax.numpy as jnp
import numpy as np
from jax import lax
from jax.experimental import pallas as pl
from jax.experimental.pallas import tpu as pltpu
from jax.sharding import PartitionSpec as P


DI = 3072
EPS = 1e-05
Q = 128
LANES = 128
HALO = 8
TAPS = 4
GROUP = 4

F32 = jnp.float32
BF16 = jnp.bfloat16
NN = (((1,), (0,)), ((), ()))
NT = (((1,), (1,)), ((), ()))
TN = (((0,), (0,)), ((), ()))
VMEM_LIMIT = 63 * 1024 * 1024
MESH_ID = pl.DeviceIdType.MESH


def dg(left, right, dims):
    return lax.dot_general(left, right, dims, preferred_element_type=F32)


def split(value):
    high = value.astype(BF16)
    return high, (value - high.astype(F32)).astype(BF16)


def dot3(left, right, dims):
    (lh, ll), (rh, rl) = split(left), split(right)
    return dg(lh, rh, dims) + (dg(lh, rl, dims) + dg(ll, rh, dims))


def spread(heads, onehot):
    high, low = split(heads)
    return dg(high, onehot, NN) + dg(low, onehot, NN)


def gather(wide, onehot):
    high, low = split(wide)
    return dg(high, onehot, NT) + dg(low, onehot, NT)


def sigmoid(value):
    return 0.5 * jnp.tanh(0.5 * value) + 0.5


def silu(value):
    return value * sigmoid(value)


def call(kernel, grid, ins, outs, scratch=(), flops=0, collective=None):
    in_specs = [spec for _, spec in ins]
    size = sum(a.size * a.dtype.itemsize for a, _ in ins) + sum(
        s.size * s.dtype.itemsize for s, _ in outs
    )
    return pl.pallas_call(
        kernel,
        grid=grid,
        in_specs=in_specs,
        out_specs=[spec for _, spec in outs],
        out_shape=[shape for shape, _ in outs],
        scratch_shapes=list(scratch),
        cost_estimate=pl.CostEstimate(flops=flops, bytes_accessed=size, transcendentals=0),
        compiler_params=pltpu.CompilerParams(vmem_limit_bytes=VMEM_LIMIT)
        if collective is None
        else pltpu.CompilerParams(
            vmem_limit_bytes=VMEM_LIMIT, collective_id=collective, has_side_effects=True
        ),
    )(*[a for a, _ in ins])


def sds(shape, dtype=F32):
    return jax.ShapeDtypeStruct(shape, dtype)


def rows(width, height=Q):
    return pl.BlockSpec((height, width), lambda c: (c, 0))


def whole(shape):
    return pl.BlockSpec(shape, lambda c: (0,) * len(shape))


def before(width, height):
    return pl.BlockSpec((HALO, width), lambda c: (jnp.maximum(c * (height // HALO) - 1, 0), 0))


def triangle(lower):
    a = lax.broadcasted_iota(jnp.int32, (Q, Q), 0)
    b = lax.broadcasted_iota(jnp.int32, (Q, Q), 1)
    return a >= b if lower else a <= b


def tri_sum(lower, value):
    mask = triangle(lower).astype(BF16)
    high = value.astype(BF16)
    rest = value - high.astype(F32)
    mid = rest.astype(BF16)
    low = (rest - mid.astype(F32)).astype(BF16)
    return dg(mask, high, NN) + (dg(mask, mid, NN) + dg(mask, low, NN))


def conv_act(pre, ext_ref, params, at):
    size = ext_ref.shape[1]
    height = pre.shape[0]
    ext_ref[HALO:, :] = pre
    total = params[at + TAPS : at + TAPS + 1, :size] + params[at + TAPS - 1 : at + TAPS, :size] * pre
    for k in range(TAPS - 1):
        start = HALO - TAPS + 1 + k
        total = total + params[at + k : at + k + 1, :size] * ext_ref[start : start + height, :]
    return total


def line(vec, first, size):
    return jnp.concatenate([vec[r : r + 1, :] for r in range(first, first + size // LANES)], axis=1)


def front_kernel(
    n, ns, hidden, cotangent, tail, vec, input_far, gate_far, output_far, piece,
    normed_o, inv_o, pre_o, gate_o, gyn_o, full_o, nhalo_o, halo_o,
    full, halo, proj_input, proj_gate, proj_output, s_sem, r_sem, w_sem, v_sem, h_sem, l_sem,
):
    loads = [
        pltpu.make_async_copy(src, dst, l_sem.at[k])
        for k, (src, dst) in enumerate(
            [(input_far, proj_input), (gate_far, proj_gate), (output_far, proj_output)]
        )
    ]
    c = pl.program_id(0)
    me, seq = lax.axis_index("head"), lax.axis_index("seq")
    height = piece.shape[0]
    short = height // 2
    odd = seq % 2
    last = pl.num_programs(0) - 1

    def slab(j):
        return pl.ds(pl.multiple_of(j * height, height), height)

    def part(j, which):
        return pl.ds(pl.multiple_of(j * height + which * short, short), short)

    def give(k, arriving):
        other = (me + k) % n
        owner = other if arriving else me
        return pltpu.make_async_remote_copy(
            src_ref=piece.at[pl.ds(pl.multiple_of(odd * short, short), short)],
            dst_ref=full.at[part(owner, odd)],
            send_sem=s_sem.at[k],
            recv_sem=r_sem.at[owner],
            device_id={"head": other},
            device_id_type=MESH_ID,
        )

    def swap(k, arriving):
        owner = (me + k) % n
        where = part(owner, 1 - odd if arriving else odd)
        return pltpu.make_async_remote_copy(
            src_ref=full.at[where],
            dst_ref=full.at[where],
            send_sem=w_sem.at[k],
            recv_sem=v_sem.at[k],
            device_id={"seq": seq + 1 - 2 * odd},
            device_id_type=MESH_ID,
        )

    def edge():
        return pltpu.make_async_remote_copy(
            src_ref=tail,
            dst_ref=halo,
            send_sem=h_sem.at[0],
            recv_sem=h_sem.at[1],
            device_id={"seq": (seq + 1) % ns},
            device_id_type=MESH_ID,
        )

    def norm(value):
        value = value.astype(F32)
        inv = lax.rsqrt(jnp.mean(value * value, axis=-1, keepdims=True) + EPS)
        return inv, (value * inv * gain).astype(BF16)

    first = 3 + (2 * pre_o.shape[1] + piece.shape[1]) // LANES
    gain = line(vec, first, hidden.shape[1])
    barrier = pltpu.get_barrier_semaphore()

    @pl.when(c == 0)
    def _():
        greet(n, ns)
        for load in loads:
            load.start()

    inv, normed = norm(hidden[...])
    inv_o[...] = inv
    normed_o[...] = normed

    @pl.when(c == 0)
    def _():
        loads[0].wait()

    pre_o[...] = dg(normed, proj_input[...], NN)

    @pl.when(c == 0)
    def _():
        pl.semaphore_wait(barrier, n + ns - 2)
        for k in range(1, n):
            give(k, False).start()

        @pl.when(seq < ns - 1)
        def _():
            edge().start()

        full[slab(me), :] = piece[...]
        loads[1].wait()
        loads[2].wait()

    gate_o[...] = dg(normed, proj_gate[...], NN)
    gyn_o[...] = dg(cotangent[...], proj_output[...], NT)

    @pl.when(c == jnp.maximum(last - 1, 0))
    def _():
        for k in range(1, n):
            give(k, True).wait_recv()
            swap(k, False).start()

    @pl.when(c == last)
    def _():
        @pl.when(seq > 0)
        def _():
            edge().wait_recv()

        @pl.when(seq == 0)
        def _():
            halo[...] = jnp.zeros_like(halo)

        before_first = norm(halo[...])[1]
        nhalo_o[...] = before_first
        halo_o[...] = dg(before_first, proj_input[...], NN)[16 - HALO :, :]

        @pl.when(seq < ns - 1)
        def _():
            edge().wait_send()

        for k in range(1, n):
            swap(k, True).wait_recv()
        full_o[...] = full[...]
        for k in range(1, n):
            swap(k, False).wait_send()
            give(k, False).wait_send()


def states_kernel(
    pre, pre_prev, pre_halo, normed, normed_halo, step_w, vec, taps_in, taps_st, full, onehot, *refs
):
    act_o, sact_o, spre_o, shalo_o, spre_step_o, step_o, cum_o, cumt_o, sin_o, dev_o, total_o = refs[:11]
    before_o, params = refs[11:13]
    ext, sext, state, total = refs[13:]
    c = pl.program_id(0)
    state_size = bmat_width(sact_o)
    inner = pre.shape[1]
    two = 2 * state_size
    hot = onehot[...]

    height = pre.shape[0]

    @pl.when(c == 0)
    def _():
        state[...] = jnp.zeros_like(state)
        total[...] = jnp.zeros_like(total)
        params[...] = jnp.zeros_like(params)
        per = inner // LANES
        params[0:TAPS, :] = taps_in[...].astype(F32)
        params[4:5, :] = line(vec, 3, inner)
        params[5:6, :] = line(vec, 3 + per, inner)
        params[6:7, :] = spread(jnp.broadcast_to(vec[2:3, :], (HALO, LANES)), hot)[:1]
        params[7:8, :LANES] = -jnp.exp(vec[0:1, :])
        params[7:8, LANES : 2 * LANES] = vec[1:2, :]
        params[8 : 8 + TAPS, :two] = taps_st[...].astype(F32)
        params[12:13, :two] = line(vec, 3 + 2 * per, two)
        shalo_o[...] = dg(normed_halo[...], full[...], NN)[16 - HALO :, :]
        sext[height:, :] = shalo_o[...]
        ext[:HALO, :] = pre_halo[...]

    @pl.when(c > 0)
    def _():
        ext[:HALO, :] = pre_prev[...]

    sext[:HALO, :] = sext[height:, :]
    spre = dg(normed[...], full[...], NN)
    spre_o[...] = spre
    step_pre = dg(normed[...], step_w[...], NT)
    spre_step_o[...] = step_pre
    act = conv_act(pre[...], ext, params, 0)
    sact = conv_act(spre, sext, params, 8)
    act_o[...] = act
    sact_o[...] = sact
    step = jax.nn.softplus(step_pre + params[7:8, LANES : 2 * LANES])
    step_o[...] = step
    x = silu(act)
    bmat_all = silu(sact[:, :state_size])
    for j in range(height // Q):
        part = slice(j * Q, (j + 1) * Q)
        cum = tri_sum(True, step[part] * params[7:8, :LANES])
        cum_o[part, :] = cum
        cumt_o[part, :] = cum.T
        last = cum[Q - 1 :, :]
        xw = x[part] * spread(step[part] * jnp.exp(last - cum), hot)
        sin_o[j * state_size : (j + 1) * state_size, :] = state[...]
        before_o[j] = total[...]
        decay = spread(jnp.broadcast_to(jnp.exp(last), (HALO, LANES)), hot)[:1]
        state[...] = state[...] * decay + dot3(bmat_all[part], xw, TN)
        total[...] = total[...] + last
    dev_o[...] = state[...]
    total_o[...] = jnp.broadcast_to(total[...], (HALO, LANES))


def bmat_width(ref):
    return ref.shape[1] // 2


def pair_stack(value):
    high, low = split(value)
    return jnp.concatenate(
        [
            jnp.concatenate([high, low], axis=1),
            jnp.concatenate([high, jnp.zeros_like(high)], axis=1),
        ],
        axis=0,
    )


def intra(base, act, sact, step, cum, cumt, params, onehot, out, xs_ref):
    state_size = bmat_width(sact)
    x = silu(act[...])
    xs_ref[...] = x * spread(step[...], onehot[...])
    height = act.shape[0]
    out[pl.ds(pl.multiple_of(base, height), height), :] = x * params[6:7, :]

    @pl.loop(0, height // Q)
    def _(chunk):
        here = pl.ds(pl.multiple_of(chunk * Q, Q), Q)
        there = pl.ds(pl.multiple_of(base + chunk * Q, Q), Q)
        sconv = silu(sact[here, :])
        bmat, cmat = sconv[:, :state_size], sconv[:, state_size:]
        scores = dot3(cmat, bmat, NT)
        causal = triangle(True)
        lane = lax.broadcasted_iota(jnp.int32, (Q, LANES), 1)
        sums, turned = cum.at[here], cumt.at[here]
        for p in range(act.shape[1] // LANES):
            cols = slice(p * LANES, (p + 1) * LANES)
            right = pair_stack(xs_ref[here, cols])
            got = []
            for j in range(2):
                h = p * 2 + j
                gap = sums[:, h : h + 1] - turned[h : h + 1, :]
                mixing = scores * jnp.exp(jnp.where(causal, gap, -1e30))
                wide = dg(jnp.concatenate(split(mixing), axis=1), right, NN)
                got.append(wide[:, :LANES] + wide[:, LANES:])
            out[there, cols] = out[there, cols] + jnp.where(lane < LANES // 2, got[0], got[1])


STREAMS = 8
OPENING = 4
CLOSING = 0
SPAN = 83.0


def encode(value):
    top = jnp.max(jnp.abs(value), axis=1, keepdims=True)
    scale = (top * 1.004 + 1e-30).astype(BF16)
    code = jnp.exp(value * (SPAN / scale.astype(F32))).astype(BF16)
    return code, jnp.broadcast_to(scale, (value.shape[0], LANES))


def decode(block, width):
    scale = block[:, width : width + 1].astype(F32) * (1.0 / SPAN)
    return jnp.log(block[:, :width].astype(F32)) * scale


def swap_states(ns, packed, logs, onehot, out, got_s, got_d, prefix, sems, reverse):
    seq = lax.axis_index("seq")
    own = out.shape[0] // ns

    def rows_of(j):
        return pl.ds(pl.multiple_of(j * own, own), own)

    def remote(src, dst, send, recv, to):
        return pltpu.make_async_remote_copy(
            src_ref=src,
            dst_ref=dst,
            send_sem=send,
            recv_sem=recv,
            device_id={"seq": to},
            device_id_type=MESH_ID,
        )

    def copies(k, arriving):
        other = (seq + k) % ns
        slot = other if arriving else seq
        part = packed.at[rows_of(other)]
        return (
            remote(part, got_s.at[slot], sems.at[0, k], sems.at[1, slot], other),
            remote(logs, got_d.at[slot], sems.at[2, k], sems.at[3, slot], other),
        )

    def answer(k, arriving):
        other = (seq + k) % ns
        slot = other if arriving else seq
        return remote(
            prefix.at[other], out.at[rows_of(slot)], sems.at[4, k], sems.at[5, slot], other
        )

    def begin():
        for k in range(1, ns):
            for copy in copies(k, False):
                copy.start()

    def turn():
        got_s[seq] = packed[rows_of(seq), :]
        got_d[seq] = logs[...]
        for k in range(1, ns):
            for copy in copies(k, True):
                copy.wait_recv()
        carry = jnp.zeros((own, out.shape[1]), F32)
        for i in reversed(range(ns)) if reverse else range(ns):
            prefix[i] = carry
            carry = carry * spread(jnp.exp(got_d[i]), onehot[...])[:1] + got_s[i]
        for k in range(1, ns):
            answer(k, False).start()
        out[rows_of(seq), :] = prefix[seq]

    def end():
        for k in range(1, ns):
            answer(k, True).wait_recv()
        for k in range(1, ns):
            answer(k, False).wait_send()
            for copy in copies(k, False):
                copy.wait_send()

    return begin, turn, end


def swap_scratch(ns, shape):
    own = shape[0] // ns
    return [
        pltpu.VMEM((ns, own, shape[1]), F32),
        pltpu.VMEM((ns, HALO, LANES), F32),
        pltpu.VMEM((ns, own, shape[1]), F32),
        pltpu.SemaphoreType.DMA((6, ns)),
    ]


def put(ref, where, value):
    code, scale = encode(value)
    width = value.shape[1]
    ref[where, :width] = code
    ref[where, width:] = scale


def chain_scratch(tokens, width, n):
    coded = pltpu.VMEM((tokens, width + LANES), BF16)
    return [pltpu.VMEM((tokens, width), F32), coded, coded, coded] + [
        pltpu.SemaphoreType.DMA((STREAMS, n))
    ] * 6


def chains(n, all_ref, part, code, got_r, got_l, s_sem, rr_sem, rl_sem, ar_sem, al_sem, ag_sem):
    me = lax.axis_index("head")
    tokens, width = part.shape
    span = tokens // STREAMS
    rows_own = span // n
    has_right, has_left = me < n - 1, me > 0

    def at(d, h):
        return pl.ds(pl.multiple_of(h * span + d * rows_own, rows_own), rows_own)

    def step(d, h, right):
        return pltpu.make_async_remote_copy(
            src_ref=code.at[at(d, h)],
            dst_ref=(got_r if right else got_l).at[at(d, h)],
            send_sem=s_sem.at[h, d],
            recv_sem=(rr_sem if right else rl_sem).at[h, d],
            device_id={"head": me + 1 if right else me - 1},
            device_id_type=MESH_ID,
        )

    def hand_on(b, h, right):
        return pltpu.make_async_remote_copy(
            src_ref=all_ref.at[at(b, h)],
            dst_ref=all_ref.at[at(b, h)],
            send_sem=(ar_sem if right else al_sem).at[h, b],
            recv_sem=ag_sem.at[h, b],
            device_id={"head": me + 1 if right else me - 1},
            device_id_type=MESH_ID,
        )

    def chain(h, u):
        for right in (True, False):
            d = me + (n - 1 - u) if right else me - (n - 1 - u)
            got = got_r if right else got_l
            inside = d <= n - 1 if right else d >= 0
            fed = has_left if right else has_right

            @pl.when(inside & fed)
            def _():
                step(d, h, right).wait_recv()
                put(code, at(d, h), part[at(d, h), :] + decode(got[at(d, h), :], width))
                step(d, h, right).start()

            @pl.when(inside & jnp.logical_not(fed))
            def _():
                put(code, at(d, h), part[at(d, h), :])
                step(d, h, right).start()

    def finish(h):
        own = at(me, h)

        @pl.when(has_left)
        def _():
            step(me, h, True).wait_recv()
            part[own, :] = part[own, :] + decode(got_r[own, :], width)

        @pl.when(has_right)
        def _():
            step(me, h, False).wait_recv()
            part[own, :] = part[own, :] + decode(got_l[own, :], width)

        put(all_ref, own, part[own, :])

        @pl.when(has_right)
        def _():
            hand_on(me, h, True).start()

        @pl.when(has_left)
        def _():
            hand_on(me, h, False).start()

    def relay(h, s):
        @pl.when(me - s >= 0)
        def _():
            hand_on(me - s, h, True).wait_recv()

            @pl.when(has_right)
            def _():
                hand_on(me - s, h, True).start()

        @pl.when(me + s < n)
        def _():
            hand_on(me + s, h, False).wait_recv()

            @pl.when(has_left)
            def _():
                hand_on(me + s, h, False).start()

    def slot(t):
        for u in range(2 * n - 2, -1, -1):
            h = t - u

            @pl.when((h >= 0) & (h < STREAMS))
            def _():
                if u < n - 1:
                    chain(h, u)
                elif u == n - 1:
                    finish(h)
                else:
                    relay(h, u - n + 1)

    def drain():
        @pl.loop(0, STREAMS)
        def _(h):
            for i in range(n):

                @pl.when(i > me)
                def _():
                    step(i, h, True).wait_send()

                @pl.when(i < me)
                def _():
                    step(i, h, False).wait_send()

                @pl.when(has_right & (i <= me))
                def _():
                    hand_on(i, h, True).wait_send()

                @pl.when(has_left & (i >= me))
                def _():
                    hand_on(i, h, False).wait_send()

    return slot, drain


def slots_of(n):
    return STREAMS - 1 + 2 * n - 1


def greet(n, ns):
    barrier = pltpu.get_barrier_semaphore()
    me, seq = lax.axis_index("head"), lax.axis_index("seq")
    for k in range(1, n):
        pl.semaphore_signal(
            barrier, inc=1, device_id={"head": (me + k) % n}, device_id_type=MESH_ID
        )
    for k in range(1, ns):
        pl.semaphore_signal(
            barrier, inc=1, device_id={"seq": (seq + k) % ns}, device_id_type=MESH_ID
        )
    return barrier


def reduce_kernel(n, ns, dims, cols, *refs):
    terms = len(dims)
    *far, hidden_far = refs[: 2 * terms + 1]
    refs = refs[2 * terms + 1 :]
    near, refs = refs[-2 * terms - 2 : -1], (*refs[: -2 * terms - 2], refs[-1])
    lefts, rights, hidden_ref = near[:terms], near[terms : 2 * terms], near[-1]
    loads = [
        pltpu.make_async_copy(src, dst, refs[-1].at[k])
        for k, (src, dst) in enumerate(zip((*far, hidden_far), near))
    ]
    inv_ref, small_a, small_b, states_ref, out_ref, sum_a, sum_b, sum_s = refs[:8]
    slot, drain = chains(n, out_ref, *refs[8:18])
    part = refs[8]
    got_a, got_b, got_s, got_c, mine_b = refs[18:23]
    sa_sem, ra_sem, sb_sem, rb_sem, ss_sem, rs_sem, sc_sem, rc_sem = refs[23:-1]
    me, seq = lax.axis_index("head"), lax.axis_index("seq")
    tokens, _ = part.shape
    span = tokens // STREAMS
    barrier = greet(n, ns)
    for load in loads:
        load.start()

    def to_seq(src, dst, ssem, rsem, k):
        return pltpu.make_async_remote_copy(
            src_ref=src,
            dst_ref=dst.at[seq],
            send_sem=ssem.at[k],
            recv_sem=rsem.at[seq],
            device_id={"seq": (seq + k) % ns},
            device_id_type=MESH_ID,
        )

    def from_seq(src, dst, ssem, rsem, k):
        other = (seq + k) % ns
        return pltpu.make_async_remote_copy(
            src_ref=src,
            dst_ref=dst.at[other],
            send_sem=ssem.at[k],
            recv_sem=rsem.at[other],
            device_id={"seq": other},
            device_id_type=MESH_ID,
        )

    def states_at(j):
        own = sum_s.shape[0]
        return states_ref.at[pl.ds(pl.multiple_of(j * own, own), own)]

    def compute(h):
        where = pl.ds(pl.multiple_of(h * span, span), span)
        total = None
        for left, right, dim, col in zip(lefts, rights, dims, cols):
            value = left[where, :] if col is None else left[where, col[0] : col[1]]
            term = dg(value, right[...], dim)
            total = term if total is None else total + term
        part[where, :] = total

    def see(h):
        where = pl.ds(pl.multiple_of(h * span, span), span)
        seen = part[where, :] * (hidden_ref[where, :].astype(F32) * inv_ref[where, :])
        mine_b[0:1, :] = mine_b[0:1, :] + jnp.sum(seen, axis=0, keepdims=True)

    mine_b[...] = jnp.zeros_like(mine_b)
    mine_b[8:16, : small_b.shape[1]] = small_b[...]
    for load in loads[:-1]:
        load.wait()
    compute(0)
    pl.semaphore_wait(barrier, n + ns - 2)
    for k in range(1, ns):
        to_seq(small_a, got_a, sa_sem, ra_sem, k).start()
        to_seq(states_at((seq + k) % ns), got_s, ss_sem, rs_sem, k).start()

    loads[-1].wait()

    @pl.loop(0, STREAMS - 1)
    def _(t):
        slot(t)
        see(t)
        compute(t + 1)

    see(STREAMS - 1)
    for k in range(1, ns):
        to_seq(mine_b, got_b, sb_sem, rb_sem, k).start()

    @pl.loop(STREAMS - 1, slots_of(n) - 2)
    def _(t):
        slot(t)

    total = small_a[...]
    for k in range(1, ns):
        from_seq(small_a, got_a, sa_sem, ra_sem, k).wait_recv()
        total = total + got_a[(seq + k) % ns]
    sum_a[...] = total
    total = states_at(seq)[...]
    for k in range(1, ns):
        from_seq(states_at(seq), got_s, ss_sem, rs_sem, k).wait_recv()
        total = total + got_s[(seq + k) % ns]
    sum_s[...] = total
    total = mine_b[...]
    for k in range(1, ns):
        from_seq(mine_b, got_b, sb_sem, rb_sem, k).wait_recv()
        total = total + got_b[(seq + k) % ns]
    sum_b[...] = total

    def to_head(k):
        return pltpu.make_async_remote_copy(
            src_ref=sum_b,
            dst_ref=got_c.at[me],
            send_sem=sc_sem.at[k],
            recv_sem=rc_sem.at[me],
            device_id={"head": (me + k) % n},
            device_id_type=MESH_ID,
        )

    def from_head(k):
        other = (me + k) % n
        return pltpu.make_async_remote_copy(
            src_ref=sum_b,
            dst_ref=got_c.at[other],
            send_sem=sc_sem.at[k],
            recv_sem=rc_sem.at[other],
            device_id={"head": other},
            device_id_type=MESH_ID,
        )

    for k in range(1, n):
        to_head(k).start()

    @pl.loop(slots_of(n) - 2, slots_of(n))
    def _(t):
        slot(t)

    total = sum_b[...]
    for k in range(1, n):
        from_head(k).wait_recv()
    for k in range(1, n):
        to_head(k).wait_send()
        total = total + got_c[(me + k) % n]
    sum_b[...] = total
    for k in range(1, ns):
        to_seq(small_a, got_a, sa_sem, ra_sem, k).wait_send()
        to_seq(states_at((seq + k) % ns), got_s, ss_sem, rs_sem, k).wait_send()
        to_seq(mine_b, got_b, sb_sem, rb_sem, k).wait_send()
    drain()


def reduce_over_heads(products, dims, cols, collective, sums):
    n, ns = lax.axis_size("head"), lax.axis_size("seq")
    tokens, width = sums[0].shape
    lefts, rights = [a for a, _ in products], [b for _, b in products]
    dma = pltpu.SemaphoreType.DMA
    small_a = sums[2].shape
    states = (sums[4].shape[0] // ns, sums[4].shape[1])
    out_shape = [sds((tokens, width + LANES), BF16), sds(small_a), sds((16, width)), sds(states)]
    scratch = chain_scratch(tokens, width, n) + [
        pltpu.VMEM((ns, *small_a), F32),
        pltpu.VMEM((ns, 16, width), F32),
        pltpu.VMEM((ns, *states), F32),
        pltpu.VMEM((n, 16, width), F32),
        pltpu.VMEM((16, width), F32),
    ]
    scratch += [dma((ns,))] * 6 + [dma((n,))] * 2
    moved = [*lefts, *rights, sums[0]]
    scratch += [pltpu.VMEM(value.shape, value.dtype) for value in moved] + [dma((len(moved),))]
    vmem = pl.BlockSpec(memory_space=pltpu.VMEM)
    return pl.pallas_call(
        functools.partial(reduce_kernel, n, ns, dims, cols),
        in_specs=[pl.BlockSpec(memory_space=pl.ANY)] * len(moved) + [vmem] * (len(sums) - 1),
        out_specs=[vmem] * len(out_shape),
        out_shape=out_shape,
        scratch_shapes=scratch,
        compiler_params=pltpu.CompilerParams(
            collective_id=collective, has_side_effects=True, vmem_limit_bytes=VMEM_LIMIT
        ),
        cost_estimate=pl.CostEstimate(
            flops=2 * tokens * width * sum(a.shape[1] for a in lefts),
            bytes_accessed=100 * tokens * width,
            transcendentals=0,
        ),
        name="reduce_heads",
    )(*lefts, *rights, *sums)


def transposed(value):
    high, wide = value.shape
    value = jnp.concatenate([value, jnp.zeros((-high % LANES, wide), F32)], axis=0)
    return value.T[:, :high]


def finish_kernel(
    branch, code, hidden, cotangent, inv, vec, sum_a, sum_b, sum_s, out_grad,
    result, out, grad_out, grad_states, taps_in, taps_st,
):
    width = out.shape[1]
    inner = taps_in.shape[1]
    gain = line(vec, 3 + (2 * inner + taps_st.shape[1]) // LANES, width)
    resid = hidden[...].astype(F32)
    result[...] = resid + decode(branch[...], width)
    grad = decode(code[...], width) * gain
    scale = inv[...]
    dots = jnp.sum(grad * resid, axis=1, keepdims=True) * (1.0 / width)
    out[...] = (
        cotangent[...].astype(F32) + scale * grad - resid * (scale * scale * scale * dots)
    )

    @pl.when(pl.program_id(0) == 0)
    def _():
        grad_out[...] = out_grad[...]
        grad_states[...] = sum_s[...]
        taps_in[...] = sum_a[:TAPS, :]
        taps_st[...] = sum_b[8 : 8 + TAPS, : taps_st.shape[1]]


def part_kernel(in_grad, grad_in, grad_step):
    inner = grad_in.shape[1]
    grad_in[...] = in_grad[:, :inner]
    grad_step[...] = transposed(in_grad[:, inner:])[: grad_step.shape[0]]


def rows_of_sums(square, cross):
    first = jnp.sum(square, axis=1, keepdims=True)
    second = jnp.sum(cross, axis=1, keepdims=True)
    lane = lax.broadcasted_iota(jnp.int32, (square.shape[0], LANES), 1)
    columns = jnp.where(lane == 0, first, jnp.where(lane == 1, second, 0.0))
    parts = [columns[r : r + Q].T[:HALO] for r in range(0, square.shape[0], Q)]
    return jnp.concatenate(parts, axis=1)


def middle_kernel(
    n, ns, act, sact, step, cum, cumt, sin, before_log, gate, gyn, params, onehot, packed, logs,
    y_o, ynorm_o, gpre_o, gssd_o, dout_o, dev_o, rows_o, incoming_o,
    keep, mine, got, adj, xs_ref, incoming, got_s, got_d, prefix, swap_sems, ssem, rsem,
):
    i = pl.program_id(0)
    half = pl.num_programs(0) // 3
    c = jnp.where(i < half, i, jnp.where(i < 2 * half, i - half, 3 * half - 1 - i))
    me = lax.axis_index("head")
    state_size = bmat_width(sact)
    gain = params[5:6, :]
    height = gate.shape[0]
    where = pl.ds(pl.multiple_of(c * height, height), height)
    begin, turn, end = swap_states(
        ns, packed, logs, onehot, incoming, got_s, got_d, prefix, swap_sems, False
    )

    def copy(k, arriving):
        other = (me + k) % n
        return pltpu.make_async_remote_copy(
            src_ref=mine,
            dst_ref=got.at[other if arriving else me],
            send_sem=ssem.at[k],
            recv_sem=rsem.at[other if arriving else me],
            device_id={"head": other},
            device_id_type=MESH_ID,
        )

    @pl.when(i == 0)
    def _():
        barrier = greet(n, ns)
        pl.semaphore_wait(barrier, n + ns - 2)
        begin()

    @pl.when(i < half)
    def _():
        intra(c * height, act, sact, step, cum, cumt, params, onehot, keep, xs_ref)

    @pl.when(i == half // 2)
    def _():
        turn()

    @pl.when(i == half - 1)
    def _():
        end()
        incoming_o[...] = incoming[...]

    @pl.when((i >= half) & (i < 2 * half))
    def _():
        hot = onehot[...]
        cmat = silu(sact[:, state_size:])
        growth = spread(jnp.exp(cum[...]), hot)
        ahead = []
        for j in range(height // Q):
            part = slice(j * Q, (j + 1) * Q)
            carry = spread(jnp.broadcast_to(jnp.exp(before_log[j]), (HALO, LANES)), hot)[:1]
            state = sin[j * state_size : (j + 1) * state_size, :] + carry * incoming[...]
            ahead.append(dot3(cmat[part], state, NN))
        y = keep[where, :] + growth * jnp.concatenate(ahead, axis=0)
        y_o[...] = y
        keep[where, :] = y
        gated = y * silu(gate[...])
        mine[:, where] = rows_of_sums(gated * gated, gyn[...] * gain * gated)

    @pl.when(i == 2 * half - 1)
    def _():
        for k in range(1, n):
            copy(k, False).start()

    @pl.when(i == 2 * half)
    def _():
        adj[...] = jnp.zeros_like(adj)
        rows_o[...] = jnp.zeros_like(rows_o)
        total = mine[...]
        for k in range(1, n):
            copy(k, True).wait_recv()
        for k in range(1, n):
            copy(k, False).wait_send()
            total = total + got[(me + k) % n]
        mine[...] = total

    @pl.when(i >= 2 * half)
    def _():
        hot = onehot[...]
        cmat = silu(sact[:, state_size:])
        gv = gate[...]
        sg = sigmoid(gv)
        gsilu = gv * sg
        growth = spread(jnp.exp(cum[...]), hot)
        total = mine[:, where]
        blank = jnp.zeros((Q - HALO, Q), F32)
        columns = jnp.concatenate(
            [
                jnp.concatenate([total[:, r : r + Q], blank], axis=0).T
                for r in range(0, height, Q)
            ],
            axis=0,
        )
        inv = lax.rsqrt(columns[:, 0:1] / DI + EPS)
        cross = columns[:, 1:2] / DI
        yv = keep[where, :]
        gated = yv * gsilu
        normed = gated * inv
        ynorm_o[...] = (normed * gain).astype(BF16)
        rows_o[0:1, :] = rows_o[0:1, :] + jnp.sum(gyn[...] * normed, axis=0, keepdims=True)
        ggated = inv * (gyn[...] * gain) - normed * (inv * inv * cross)
        gpre_o[...] = (ggated * yv * sg * (1.0 + gv * (1.0 - sg))).astype(BF16)
        gssd = ggated * gsilu
        gssd_o[...] = gssd
        rows_o[1:2, :] = rows_o[1:2, :] + jnp.sum(gssd * silu(act[...]), axis=0, keepdims=True)
        scaled = gssd * growth
        for j in reversed(range(height // Q)):
            part = slice(j * Q, (j + 1) * Q)
            dout_o[j * state_size : (j + 1) * state_size, :] = adj[...]
            last = cum[(j + 1) * Q - 1 : (j + 1) * Q, :]
            decay = spread(jnp.broadcast_to(jnp.exp(last), (HALO, LANES)), hot)[:1]
            adj[...] = adj[...] * decay + dot3(cmat[part], scaled[part], TN)

    @pl.when(i == 3 * half - 1)
    def _():
        dev_o[...] = adj[...]


def back_kernel(
    n, ns, act, sact, y, gssd, step, step_pre, cum, cumt, sin, dout, before_log, total_log, incoming,
    ynorm_far, output_far, packed, normed_far, cotangent_far,
    params, onehot, rows_in, pre, pre_prev, pre_halo, spre, spre_prev, spre_halo,
    gin_o, gsb_out, small_a, small_b, code_far, win_far, wout_far,
    gin_all, gsb_o, gstep, xs_ref, u_ref, st_ref, gext, sext, pext, spext, halo_send, halo_got, shalo_send, shalo_got,
    psum, psend, pgot, h_sem, p_send, p_recv, g_send, g_recv,
    later, got_states, got_decays, prefix, swap_sems, ynorm, proj_output, normed, cotangent, win_o, wout_o, c_sem,
    all_ref, part, *chain_refs,
):
    load_ynorm = pltpu.make_async_copy(ynorm_far, ynorm, c_sem.at[5])
    load_output = pltpu.make_async_copy(output_far, proj_output, c_sem.at[6])
    load_cotangent = pltpu.make_async_copy(cotangent_far, cotangent, c_sem.at[0])
    load_normed = pltpu.make_async_copy(normed_far, normed, c_sem.at[1])
    save_out = pltpu.make_async_copy(wout_o, wout_far, c_sem.at[2])
    save_in = pltpu.make_async_copy(win_o, win_far, c_sem.at[3])
    save_code = pltpu.make_async_copy(all_ref, code_far, c_sem.at[4])
    i = pl.program_id(0)
    c = i - 1
    count = pl.num_programs(0) - 2
    total_chunks = psum.shape[0] // Q
    begin, turn, end = swap_states(
        ns, packed, total_log, onehot, later, got_states, got_decays, prefix, swap_sems, True
    )
    slot, drain = chains(n, all_ref, part, *chain_refs)
    span = part.shape[0] // STREAMS
    groups = total_chunks // n
    taps = TAPS
    me, seq = lax.axis_index("head"), lax.axis_index("seq")
    state_size = bmat_width(sact)
    two = 2 * state_size

    def halo(src, dst, k):
        return pltpu.make_async_remote_copy(
            src_ref=src,
            dst_ref=dst,
            send_sem=h_sem.at[k],
            recv_sem=h_sem.at[k + 1],
            device_id={"seq": (seq + ns - 1) % ns},
            device_id_type=MESH_ID,
        )

    def chunk_rows(k):
        return pl.ds(pl.multiple_of(k * Q, Q), Q)

    def code_rows(k):
        return pl.ds(pl.multiple_of(k * (Q + 16), 16), Q + 16)

    def to_owner(k):
        return pltpu.make_async_remote_copy(
            src_ref=psend.at[code_rows(k)],
            dst_ref=pgot.at[me, code_rows(k // n)],
            send_sem=p_send.at[k],
            recv_sem=p_recv.at[me, k // n],
            device_id={"head": k % n},
            device_id_type=MESH_ID,
        )

    def from_other(j, g):
        return pltpu.make_async_remote_copy(
            src_ref=psend.at[code_rows(g)],
            dst_ref=pgot.at[j, code_rows(g)],
            send_sem=p_send.at[g],
            recv_sem=p_recv.at[j, g],
            device_id={"head": j},
            device_id_type=MESH_ID,
        )

    def give(k, g, arriving):
        other = (me + k) % n
        owner = other if arriving else me
        where = chunk_rows(g * n + owner)
        return pltpu.make_async_remote_copy(
            src_ref=gsb_o.at[where],
            dst_ref=gsb_o.at[where],
            send_sem=g_send.at[k, g],
            recv_sem=g_recv.at[owner, g],
            device_id={"head": other},
            device_id_type=MESH_ID,
        )

    @pl.when(i == 0)
    def _():
        barrier = greet(n, ns)
        load_ynorm.start()
        load_output.start()
        load_cotangent.start()
        load_normed.start()
        small_a[...] = jnp.zeros_like(small_a)
        small_b[...] = jnp.zeros_like(small_b)
        small_a[5:7, :] = rows_in[0:2, :]

        def compute(h):
            where = pl.ds(pl.multiple_of(h * span, span), span)
            part[where, :] = dg(ynorm[where, :], proj_output[...], NN)

        load_ynorm.wait()
        load_output.wait()
        compute(0)
        pl.semaphore_wait(barrier, n + ns - 2)
        begin()

        @pl.loop(0, 2)
        def _(t):
            slot(t)
            compute(t + 1)

        def product(m):
            cols = pl.ds(pl.multiple_of(m * 256, 256), 256)
            wout_o[cols, :] = dg(cotangent[:, cols], ynorm[...], TN)

        tiles = wout_o.shape[0] // 256

        @pl.loop(3, STREAMS)
        def _(h):
            compute(h)

        load_cotangent.wait()

        @pl.loop(0, tiles // 2)
        def _(m):
            product(m)

        turn()

        @pl.loop(2, OPENING - 1)
        def _(t):
            slot(t)

        @pl.loop(tiles // 2, tiles)
        def _(m):
            product(m)

        save_out.start()
        slot(OPENING - 1)
        end()

    @pl.when((c >= 0) & (c < count))
    def _():
        hot = onehot[...]
        skip = params[6:7, :]
        rate = params[7:8, :LANES]
        sactv = sact[...]
        ssg = sigmoid(sactv)
        sconv = sactv * ssg
        bmat, cmat = sconv[:, :state_size], sconv[:, state_size:]
        actv = act[...]
        sg = sigmoid(actv)
        x = actv * sg
        cumv, stepv = cum[...], step[...]
        last = cumv[Q - 1 :, :]
        step_wide = spread(stepv, hot)
        xs = x * step_wide
        xs_ref[...] = xs
        g = gssd[...]

        def row(value):
            return spread(jnp.broadcast_to(jnp.exp(value), (HALO, LANES)), hot)[:1]

        state = sin[...] + row(before_log[...]) * incoming[...]
        adj = dout[...] + row(total_log[0:1, :] - before_log[...] - last) * later[...]
        to_end = spread(jnp.exp(last - cumv), hot)
        u_state = to_end * dot3(bmat, adj, NN)
        ends = row(last) * jnp.sum(adj * state, axis=0, keepdims=True) + jnp.sum(
            xs * u_state, axis=0, keepdims=True
        )
        scores_t = dot3(bmat, cmat, NT)
        later_mask = triangle(False)
        lane = lax.broadcasted_iota(jnp.int32, (Q, LANES), 1)
        st_ref[...] = jnp.zeros_like(st_ref)
        for p in range(act.shape[1] // LANES):
            cols = slice(p * LANES, (p + 1) * LANES)
            right = pair_stack(gssd[:, cols])
            g_high, g_low = right[:Q, :LANES], right[:Q, LANES:]
            twice = jnp.concatenate([g_high, g_high], axis=1)
            pair = xs_ref[:, cols]
            got = []
            for j in range(2):
                h = p * 2 + j
                gap = cumt[h : h + 1, :] - cum[:, h : h + 1]
                decay = jnp.exp(jnp.where(later_mask, gap, -1e30))
                wide = dg(jnp.concatenate(split(scores_t * decay), axis=1), right, NN)
                got.append(wide[:, :LANES] + wide[:, LANES:])
                mine = (lane < LANES // 2) if j == 0 else (lane >= LANES // 2)
                xh, xl = split(jnp.where(mine, pair, 0.0))
                inner = dg(jnp.concatenate([xh, xl], axis=1), twice, NT) + dg(xh, g_low, NT)
                st_ref[...] = st_ref[...] + decay * inner
            u_ref[:, cols] = jnp.where(lane < LANES // 2, got[0], got[1])
        u = u_ref[...] + u_state
        sc = st_ref[...]
        g_scaled = g * spread(jnp.exp(cumv), hot)
        gstates = jnp.concatenate(
            [
                dot3(sc, cmat, NN) + dot3(xs * to_end, adj, NT),
                dot3(sc.T, bmat, NN) + dot3(g_scaled, state, NT),
            ],
            axis=1,
        )
        gsact = gstates * (ssg * (1.0 + sactv * (1.0 - ssg)))
        gact = (step_wide * u + skip * g) * (sg * (1.0 + actv * (1.0 - sg)))
        u_ref[...] = gact
        sext[Q + HALO :, :] = gsact
        small_a[4:5, :] = small_a[4:5, :] + jnp.sum(gact, axis=0, keepdims=True)
        small_b[4:5, :] = small_b[4:5, :] + jnp.sum(gsact, axis=0, keepdims=True)
        direct = gather(x * u, hot)
        flow = gather(g * (y[...] - skip * x), hot) - stepv * direct
        ends_heads = gather(jnp.broadcast_to(ends, (HALO, ends.shape[1])), hot)[:1]
        da = tri_sum(False, flow) + ends_heads
        slope = (direct + rate * da) * sigmoid(step_pre[...] + params[7:8, LANES : 2 * LANES])
        gstep[Q:, :] = slope.astype(BF16)
        small_a[7:8, :LANES] = small_a[7:8, :LANES] + jnp.sum(
            stepv * rate * da, axis=0, keepdims=True
        )
        small_a[7:8, LANES : 2 * LANES] = small_a[7:8, LANES : 2 * LANES] + jnp.sum(
            slope, axis=0, keepdims=True
        )

    @pl.when(c == 0)
    def _():
        halo_send[...] = u_ref[:HALO, :]
        shalo_send[...] = sext[Q + HALO : Q + 2 * HALO, :]

        @pl.when(seq > 0)
        def _():
            halo(halo_send, halo_got, 0).start()
            halo(shalo_send, shalo_got, 2).start()

    @pl.when(c == count)
    def _():
        @pl.when(seq < ns - 1)
        def _():
            halo(halo_send, halo_got, 0).wait_recv()
            halo(shalo_send, shalo_got, 2).wait_recv()
            u_ref[:HALO, :] = halo_got[...]
            sext[Q + HALO : Q + 2 * HALO, :] = shalo_got[...]

        @pl.when(seq == ns - 1)
        def _():
            u_ref[:HALO, :] = jnp.zeros((HALO, u_ref.shape[1]), F32)
            sext[Q + HALO : Q + 2 * HALO, :] = jnp.zeros((HALO, two), F32)

        @pl.when(seq > 0)
        def _():
            halo(halo_send, halo_got, 0).wait_send()
            halo(shalo_send, shalo_got, 2).wait_send()

    @pl.when(c >= 1)
    def _():
        gext[Q:, :] = u_ref[:HALO, :]
        sext[Q : Q + HALO, :] = sext[Q + HALO : Q + 2 * HALO, :]
        pext[:HALO, :] = jnp.where(c == 1, pre_halo[...], pre_prev[...])
        pext[HALO:, :] = pre[...]
        spext[:HALO, :] = jnp.where(c == 1, spre_halo[...], spre_prev[...])
        spext[HALO:, :] = spre[...]

        def conv_back(ext, ext_pre, taps_at, size, sums):
            g = ext[:Q, :]
            total = params[taps_at + taps - 1 : taps_at + taps, :size] * g
            for k in range(taps - 1):
                start = taps - 1 - k
                total = total + params[taps_at + k : taps_at + k + 1, :size] * ext[start : start + Q, :]
            for k in range(taps):
                start = HALO - taps + 1 + k
                sums[k : k + 1, :] = sums[k : k + 1, :] + jnp.sum(
                    g * ext_pre[start : start + Q, :], axis=0, keepdims=True
                )
            return total

        inner = gext.shape[1]
        gin_o[:, :inner] = conv_back(gext, pext, 0, inner, small_a).astype(BF16)
        gin_o[:, inner:] = gstep[:Q, :]
        gin_all[chunk_rows(c - 1), :] = gin_o[...]
        mine = conv_back(sext, spext, 8, two, small_b)
        psum[chunk_rows(c - 1), :] = mine

        @pl.when((c - 1) % n != me)
        def _():
            top = jnp.max(jnp.abs(mine), axis=0, keepdims=True)
            scale = (top * 1.004 + 1e-30).astype(BF16)
            first = pl.multiple_of((c - 1) * (Q + 16), 16)
            psend[pl.ds(first, Q), :] = jnp.exp(mine * (SPAN / scale.astype(F32))).astype(BF16)
            psend[pl.ds(first + Q, 16), :] = jnp.broadcast_to(scale, (16, two))

    @pl.when((c >= 0) & (c < count))
    def _():
        gext[:Q, :] = u_ref[...]
        gstep[:Q, :] = gstep[Q:, :]
        sext[:Q, :] = sext[Q + HALO :, :]

    last_step = count + 1
    tail_slot = slots_of(n) - CLOSING
    more = tail_slot - OPENING

    @pl.when((i >= 1) & (i < last_step))
    def _():
        @pl.loop(OPENING + (i - 1) * more // count, OPENING + i * more // count)
        def _(t):
            slot(t)

    @pl.when((c >= 1) & ((c - 1) % n != me))
    def _():
        to_owner(c - 1).start()

    @pl.when(i == last_step)
    def _():
        @pl.loop(tail_slot, tail_slot + CLOSING // 2)
        def _(t):
            slot(t)

        load_normed.wait()

        @pl.loop(0, win_o.shape[0] // 256)
        def _(m):
            cols = pl.ds(pl.multiple_of(m * 256, 256), 256)
            win_o[cols, :] = dg(normed[:, cols], gin_all[...], TN)

        save_in.start()

    for g in range(groups):

        @pl.when(c == min((g + 1) * n + 2, total_chunks))
        def _():
            own = chunk_rows(g * n + me)
            total = psum[own, :]
            for k in range(1, n):
                j = (me + k) % n
                from_other(j, g).wait_recv()
                first = g * (Q + 16)
                scale = pgot[j, first + Q : first + Q + 16, :].astype(F32)[:1] * (1.0 / SPAN)
                total = total + jnp.log(pgot[j, first : first + Q, :].astype(F32)) * scale
            gsb_o[own, :] = total.astype(BF16)
            for k in range(1, n):
                give(k, g, False).start()

    @pl.when(i == last_step)
    def _():
        @pl.loop(tail_slot + CLOSING // 2, tail_slot + CLOSING)
        def _(t):
            slot(t)

        save_code.start()
        for g in range(groups):
            for k in range(1, n):
                give(k, g, True).wait_recv()
        gsb_out[...] = gsb_o[...]
        for g in range(groups):
            for k in range(1, n):
                give(k, g, False).wait_send()
        for k in range(total_chunks):

            @pl.when(k % n != me)
            def _():
                to_owner(k).wait_send()

    @pl.when(i == last_step)
    def _():
        drain()
        save_code.wait()
        save_out.wait()
        save_in.wait()


def transposed_times(left, right):
    return dg(left, right, TN)


def on_device(
    hidden,
    in_gain,
    proj_gate,
    proj_input,
    proj_states,
    proj_step,
    conv_input,
    conv_input_bias,
    conv_states,
    conv_states_bias,
    step_bias,
    decay_log,
    skip_gain,
    gate_gain,
    proj_output,
    cotangent,
):
    seg_count = lax.axis_size("seq")
    head_index = lax.axis_index("head")
    tokens, width = hidden.shape
    heads = proj_step.shape[1]
    inner = proj_gate.shape[1]
    state_size = conv_states.shape[1] // 2
    head_dim = inner // heads
    row_width = proj_states.shape[0]
    count = tokens // Q

    def pad_heads(value):
        return jnp.pad(value, [(0, 0)] * (value.ndim - 1) + [(0, LANES - heads)])

    n, ns = lax.axis_size("head"), seg_count

    two = 2 * state_size
    fields = [
        (decay_log, LANES),
        (step_bias, LANES),
        (skip_gain, LANES),
        (conv_input_bias, inner),
        (gate_gain, inner),
        (conv_states_bias, two),
        (in_gain, width),
    ]
    used = sum(size for _, size in fields)
    used += -used % 1024
    flat, place = jnp.zeros((used,), F32), 0
    for value, size in fields:
        flat = flat + jnp.pad(value.astype(F32), (place, used - place - value.shape[0]))
        place += size
    vec = flat.reshape(-1, LANES)
    stripe = 256
    far = pl.BlockSpec(memory_space=pl.ANY)

    def striped(size):
        return pl.BlockSpec((stripe, size), lambda c: (c, 0))

    def fixed(shape, at=0):
        return pl.BlockSpec(shape, lambda c: (at, 0), pipeline_mode=pl.Buffered(1))

    (
        normed, inv_rms, input_pre, gate_pre, grad_ynorm, proj_states_full, normed_halo, input_halo,
    ) = call(
        functools.partial(front_kernel, n, ns),
        (tokens // stripe,),
        [
            (hidden, striped(width)),
            (cotangent, striped(width)),
            (hidden, fixed((16, width), tokens // 16 - 1)),
            (vec, fixed(vec.shape)),
            (proj_input, far),
            (proj_gate, far),
            (proj_output, far),
            (proj_states, fixed((row_width, 2 * state_size))),
        ],
        [
            (sds((tokens, width), BF16), striped(width)),
            (sds((tokens, 1)), striped(1)),
            (sds((tokens, inner)), striped(inner)),
            (sds((tokens, inner)), striped(inner)),
            (sds((tokens, inner)), striped(inner)),
            (sds((width, 2 * state_size), BF16), whole((width, 2 * state_size))),
            (sds((16, width), BF16), whole((16, width))),
            (sds((HALO, inner)), whole((HALO, inner))),
        ],
        scratch=[
            pltpu.VMEM((width, 2 * state_size), BF16),
            pltpu.VMEM((16, width), BF16),
            pltpu.VMEM((width, inner), BF16),
            pltpu.VMEM((width, inner), BF16),
            pltpu.VMEM((inner, width), BF16),
            pltpu.SemaphoreType.DMA((n,)),
            pltpu.SemaphoreType.DMA((n,)),
            pltpu.SemaphoreType.DMA((n,)),
            pltpu.SemaphoreType.DMA((n,)),
            pltpu.SemaphoreType.DMA((2,)),
            pltpu.SemaphoreType.DMA((3,)),
        ],
        flops=6 * tokens * inner * width,
        collective=6,
    )
    proj_step_tall = pad_heads(proj_step).T
    onehot = jnp.asarray(
        np.arange(LANES)[:, None] == np.arange(inner)[None, :] // head_dim, dtype=BF16
    )
    hot = (onehot, whole((LANES, inner)))
    state_rows = pl.BlockSpec((state_size, inner), lambda c: (c, 0))
    packed_shape = (state_size, inner)
    logs_shape = (HALO, LANES)
    big = GROUP * Q
    (
        act, sact, states_pre, states_halo, step_pre, step, cum, cumt, sin, packed, total_log,
        before_log, params,
    ) = call(
        states_kernel,
        (count // GROUP,),
        [
            (input_pre, rows(inner, big)),
            (input_pre, before(inner, big)),
            (input_halo, whole((HALO, inner))),
            (normed, rows(width, big)),
            (normed_halo, whole((16, width))),
            (proj_step_tall, whole((LANES, width))),
            (vec, whole(vec.shape)),
            (conv_input, whole(conv_input.shape)),
            (conv_states, whole(conv_states.shape)),
            (proj_states_full, whole((width, two))),
            hot,
        ],
        [
            (sds((tokens, inner)), rows(inner, big)),
            (sds((tokens, two)), rows(two, big)),
            (sds((tokens, two)), rows(two, big)),
            (sds((HALO, two)), whole((HALO, two))),
            (sds((tokens, LANES)), rows(LANES, big)),
            (sds((tokens, LANES)), rows(LANES, big)),
            (sds((tokens, LANES)), rows(LANES, big)),
            (sds((tokens, LANES)), rows(LANES, big)),
            (sds((count * state_size, inner)), pl.BlockSpec((GROUP * state_size, inner), lambda c: (c, 0))),
            (sds(packed_shape), whole(packed_shape)),
            (sds((HALO, LANES)), whole((HALO, LANES))),
            (sds((count, 1, LANES)), pl.BlockSpec((GROUP, 1, LANES), lambda c: (c, 0, 0))),
            (sds((16, inner)), whole((16, inner))),
        ],
        scratch=[
            pltpu.VMEM((big + HALO, inner), F32),
            pltpu.VMEM((big + HALO, two), F32),
            pltpu.VMEM((state_size, inner), F32),
            pltpu.VMEM((1, LANES), F32),
        ],
        flops=10 * tokens * inner * state_size,
    )
    par = (params, whole((16, inner)))
    half = count // GROUP

    def zero(i):
        return jnp.minimum(i, half - 1)

    def one(i):
        return jnp.clip(i - half, 0, half - 1)

    def two_(i):
        return jnp.minimum(3 * half - 1 - i, half - 1)

    def both(i):
        return jnp.where(i < 2 * half, one(i), two_(i))

    def ends(i):
        return jnp.where(i < half, i, two_(i))

    def every(i):
        return jnp.where(i < half, i, both(i))

    def at(size, which, height=big):
        return pl.BlockSpec((height, size), lambda i: (which(i), 0))

    y, ynorm, grad_gate_pre, grad_ssd, dout, packed_back, grad_rows, incoming = call(
        functools.partial(middle_kernel, n, ns),
        (3 * half,),
        [
            (act, at(inner, ends)),
            (sact, at(two, every)),
            (step, at(LANES, zero)),
            (cum, at(LANES, every)),
            (cumt, at(LANES, zero)),
            (sin, at(inner, one, GROUP * state_size)),
            (before_log, pl.BlockSpec((GROUP, 1, LANES), lambda i: (one(i), 0, 0))),
            (gate_pre, at(inner, both)),
            (grad_ynorm, at(inner, both)),
            par,
            hot,
            (packed, whole(packed_shape)),
            (total_log, whole(logs_shape)),
        ],
        [
            (sds((tokens, inner)), at(inner, one)),
            (sds((tokens, inner), BF16), at(inner, two_)),
            (sds((tokens, inner), BF16), at(inner, two_)),
            (sds((tokens, inner)), at(inner, two_)),
            (sds((count * state_size, inner)), at(inner, two_, GROUP * state_size)),
            (sds(packed_shape), whole(packed_shape)),
            (sds((HALO, inner)), whole((HALO, inner))),
            (sds((state_size, inner)), whole((state_size, inner))),
        ],
        scratch=[
            pltpu.VMEM((tokens, inner), F32),
            pltpu.VMEM((HALO, tokens), F32),
            pltpu.VMEM((n, HALO, tokens), F32),
            pltpu.VMEM((state_size, inner), F32),
            pltpu.VMEM((big, inner), F32),
            pltpu.VMEM((state_size, inner), F32),
            *swap_scratch(ns, (state_size, inner)),
            pltpu.SemaphoreType.DMA((n,)),
            pltpu.SemaphoreType.DMA((n,)),
        ],
        flops=24 * tokens * inner * state_size,
        collective=3,
    )
    local_proj_gate = transposed_times(normed, grad_gate_pre)
    grad_proj_gate = lax.psum_scatter(
        local_proj_gate, "seq", scatter_dimension=0, tiled=True
    )

    def now(i):
        return jnp.clip(i - 1, 0, count - 1)

    def past(i):
        return jnp.maximum(i - 2, 0)

    def held(size, height=Q):
        return pl.BlockSpec((height, size), lambda i: (now(i), 0))

    def prior(size):
        return pl.BlockSpec((Q, size), lambda i: (past(i), 0))

    def prior_edge(size):
        return pl.BlockSpec(
            (HALO, size), lambda i: (jnp.maximum(past(i) * (Q // HALO) - 1, 0), 0)
        )

    def once(shape):
        return pl.BlockSpec(shape, lambda i: (0, 0), pipeline_mode=pl.Buffered(1))

    dma = pltpu.SemaphoreType.DMA
    groups = count // n
    grad_in_b, grad_states_b, small_a, small_b, branch_code, local_proj_in, local_proj_output = call(
        functools.partial(back_kernel, n, ns),
        (count + 2,),
        [
            (act, held(inner)),
            (sact, held(two)),
            (y, held(inner)),
            (grad_ssd, held(inner)),
            (step, held(LANES)),
            (step_pre, held(LANES)),
            (cum, held(LANES)),
            (cumt, held(LANES)),
            (sin, held(inner, state_size)),
            (dout, held(inner, state_size)),
            (
                before_log,
                pl.BlockSpec((None, 1, LANES), lambda i: (now(i), 0, 0)),
            ),
            (total_log, whole(logs_shape)),
            (incoming, once((state_size, inner))),
            (ynorm, far),
            (proj_output, far),
            (packed_back, once(packed_shape)),
            (normed, far),
            (cotangent, far),
            par,
            hot,
            (grad_rows, whole((HALO, inner))),
            (input_pre, prior(inner)),
            (input_pre, prior_edge(inner)),
            (input_halo, whole((HALO, inner))),
            (states_pre, prior(two)),
            (states_pre, prior_edge(two)),
            (states_halo, whole((HALO, two))),
        ],
        [
            (sds((tokens, inner + LANES), BF16), prior(inner + LANES)),
            (sds((tokens, two), BF16), whole((tokens, two))),
            (sds((16, inner)), whole((16, inner))),
            (sds((HALO, two)), whole((HALO, two))),
            (sds((tokens, width + LANES), BF16), far),
            (sds((width, inner + LANES)), far),
            (sds((width, inner)), far),
        ],
        scratch=[
            pltpu.VMEM((tokens, inner + LANES), BF16),
            pltpu.VMEM((tokens, two), BF16),
            pltpu.VMEM((2 * Q, LANES), BF16),
            pltpu.VMEM((Q, inner), F32),
            pltpu.VMEM((Q, inner), F32),
            pltpu.VMEM((Q, Q), F32),
            pltpu.VMEM((Q + HALO, inner), F32),
            pltpu.VMEM((2 * Q + HALO, two), F32),
            pltpu.VMEM((Q + HALO, inner), F32),
            pltpu.VMEM((Q + HALO, two), F32),
            pltpu.VMEM((HALO, inner), F32),
            pltpu.VMEM((HALO, inner), F32),
            pltpu.VMEM((HALO, two), F32),
            pltpu.VMEM((HALO, two), F32),
            pltpu.VMEM((tokens, two), F32),
            pltpu.VMEM((count * (Q + 16), two), BF16),
            pltpu.VMEM((n, groups * (Q + 16), two), BF16),
            dma((4,)),
            dma((count,)),
            dma((n, groups)),
            dma((n, groups)),
            dma((n, groups)),
            pltpu.VMEM((state_size, inner), F32),
            *swap_scratch(ns, (state_size, inner)),
            pltpu.VMEM((tokens, inner), BF16),
            pltpu.VMEM((inner, width), BF16),
            pltpu.VMEM((tokens, width), BF16),
            pltpu.VMEM((tokens, width), BF16),
            pltpu.VMEM((width, inner + LANES), F32),
            pltpu.VMEM((width, inner), F32),
            dma((7,)),
            pltpu.VMEM((tokens, width + LANES), BF16),
            *chain_scratch(tokens, width, n),
        ],
        flops=40 * tokens * inner * Q,
        collective=4,
    )
    row_start = head_index * row_width
    own_states = lax.dynamic_update_slice_in_dim(
        jnp.zeros((width, two), BF16), proj_states, row_start, 0
    )
    normed_rows = lax.dynamic_slice_in_dim(normed, row_start, row_width, 1)
    local_proj_states = transposed_times(grad_states_b, normed_rows)
    summed_out = lax.psum_scatter(
        local_proj_output, "seq", scatter_dimension=0, tiled=True
    )
    summed_in = lax.psum_scatter(local_proj_in, "seq", scatter_dimension=0, tiled=True)
    grad_code, sum_a, sum_b, sum_s = reduce_over_heads(
        [
            (grad_gate_pre, proj_gate),
            (grad_in_b, proj_input),
            (grad_in_b, proj_step_tall),
            (grad_states_b, own_states),
        ],
        [NT, NT, NN, NT],
        (None, (0, inner), (inner, inner + LANES), None),
        2,
        (hidden, inv_rms, small_a, small_b, local_proj_states),
    )

    def ones(value):
        return (value, fixed(value.shape))

    def outs(*shape):
        return (sds(shape), fixed(shape))

    (
        result, grad_hidden, grad_proj_output, grad_proj_states, grad_conv_input, grad_conv_states,
    ) = call(
        finish_kernel,
        (tokens // stripe,),
        [
            (branch_code, striped(width + LANES)),
            (grad_code, striped(width + LANES)),
            (hidden, striped(width)),
            (cotangent, striped(width)),
            (inv_rms, striped(1)),
            ones(vec),
            ones(sum_a),
            ones(sum_b),
            ones(sum_s),
            ones(summed_out),
        ],
        [
            (sds((tokens, width)), striped(width)),
            (sds((tokens, width)), striped(width)),
            outs(width // ns, inner),
            outs(two // ns, row_width),
            outs(TAPS, inner),
            outs(TAPS, two),
        ],
        flops=40 * tokens * width,
    )
    grad_proj_input, grad_proj_step = call(
        part_kernel, (1,), [ones(summed_in)], [outs(width // ns, inner), outs(heads, width // ns)]
    )
    return (
        result,
        grad_hidden,
        sum_b[0],
        grad_proj_gate,
        grad_proj_input,
        grad_proj_states.T,
        grad_proj_step.T,
        grad_conv_input,
        sum_a[4],
        grad_conv_states,
        sum_b[12, :two],
        sum_a[7, LANES : LANES + heads],
        sum_a[7, :heads],
        jnp.sum(sum_a[6].reshape(heads, head_dim), axis=1),
        sum_a[5],
        grad_proj_output.T,
    )


def solution(mesh):
    in_specs = (
        P("seq", None),
        P(),
        P(None, "head"),
        P(None, "head"),
        P("head", None),
        P(None, "head"),
        P(None, "head"),
        P("head"),
        P(),
        P(),
        P("head"),
        P("head"),
        P("head"),
        P("head"),
        P("head", None),
        P("seq", None),
    )
    out_specs = (
        P("seq", None),
        P("seq", None),
        P(),
        P("seq", "head"),
        P("seq", "head"),
        P("head", "seq"),
        P("seq", "head"),
        P(None, "head"),
        P("head"),
        P(),
        P(),
        P("head"),
        P("head"),
        P("head"),
        P("head"),
        P("head", "seq"),
    )

    return jax.shard_map(
        on_device, mesh=mesh, in_specs=in_specs, out_specs=out_specs, check_vma=False
    )
```
